128 devices in a mesh: req: 4 (over z_hi, core), tile: 32 (over y, z_lo, x).
Axes of the slice: x: 4, y: 4, z: 4 (z_hi: 2, z_lo: 2; z = z_hi * 2 + z_lo), core: 2. Of those that a mesh axis runs over, the one named last changes fastest.
Arguments:
- latents: bfloat16 [4, 3840, 1536], P('req', 'tile'), may hold values from -6 to 6
- modulation: bfloat16 [4, 6, 1536], P('req'), may hold values from -2.5 to 2.5
- kv_cache: bfloat16 [4, 3840, 3072], P('req', 'tile'), may hold values from -6 to 6
- text_kv: bfloat16 [4, 154, 3072], P('req'), as said below
- lengths: int32 [4], P('req'), may hold values from 960 to 3840, as said below
- refresh: int32 [4, 4], P('req'), may hold values from 0 to 31, as said below
- w_qkv: bfloat16 [1536, 4608], replicated, may hold values from -0.15625 to 0.15625
- w_out: bfloat16 [1536, 1536], P('req'), may hold values from -6 to 6
- w_up: bfloat16 [1536, 6144], P(None, 'req'), may hold values from -0.15625 to 0.15625
- w_down: bfloat16 [6144, 1536], P('req'), may hold values from -0.078125 to 0.078125
Outputs:
- block_out: bfloat16 [4, 3840, 1536], P('req', 'tile')
The draws below stay inside these ranges and needn't reach their ends.
Inputs may be any that keep to these rules, and one draw needn't show every extreme that they name: `lengths`: some request has exactly 3840 live tokens and another exactly 960. `refresh`: each row holds 4 different tile indices; the first and the last tile each appear in some row. `text_kv`: keys in the first 1536 columns, values in the last 1536.
All inputs are finite; a program needn't handle non-finite values.
Results may differ from the reference program's by a relative error of at most 0.017.
Values may be sent and summed in bfloat16 or wider, within the bound.
No kernel may reach another device: no remote copies, remote signals or barrier semaphores. Data moves between devices by JAX's collectives and lax.ppermute only.
A program may use at most 192 MiB of HBM per device.

```python
import math
import jax
import jax.numpy as jnp
from jax import lax

D = 1536
FF = 6144
HEAD = 64
TXT = 154
TOK_DEV = 120
IMG = 3840
REQS = 4
NREF = 4
N_TILE = 32


def draw_lengths(key, part):
    key_length, key_place = jax.random.split(key)
    values = jax.random.randint(key_length, (REQS,), IMG // 4, IMG + 1)
    place = jax.random.randint(key_place, (), 0, REQS)
    values = values.at[place].set(IMG)
    values = values.at[(place + 1) % REQS].set(IMG // 4)
    return values.astype(jnp.int32)


def pick_tiles(subkey):
    return jax.random.permutation(subkey, N_TILE)[:NREF].astype(jnp.int32)


def draw_refresh(key, part):
    key_rows, key_place, key_top, key_low, key_roll = jax.random.split(key, 5)
    subkeys = jax.random.split(key_rows, REQS)
    rows = jax.vmap(pick_tiles)(subkeys).astype(jnp.int32)
    place = jax.random.randint(key_place, (), 0, REQS)
    rest_top = jax.random.permutation(key_top, N_TILE - 1)[:NREF - 1].astype(jnp.int32)
    top_row = jnp.concatenate([jnp.full((1,), N_TILE - 1, jnp.int32), rest_top])
    rest_low = (jax.random.permutation(key_low, N_TILE - 1)[:NREF - 1] + 1).astype(jnp.int32)
    low_row = jnp.concatenate([jnp.zeros((1,), jnp.int32), rest_low])
    roll_keys = jax.random.split(key_roll, 2)
    top_row = jnp.roll(top_row, jax.random.randint(roll_keys[0], (), 0, NREF))
    low_row = jnp.roll(low_row, jax.random.randint(roll_keys[1], (), 0, NREF))
    rows = rows.at[place].set(top_row)
    rows = rows.at[(place + 1) % REQS].set(low_row)
    return rows.astype(jnp.int32)


def draw_text_kv(key, part):
    values = jax.random.normal(key, (REQS, TXT, 2 * D), jnp.float32)
    return values.astype(jnp.bfloat16)


def block_scale(key, shape, cuts, low, high):
    gain = 1.0
    for axis_at, shards_of in cuts:
        heights = jax.random.uniform(jax.random.fold_in(jax.random.fold_in(key, 6), axis_at), (shards_of,), jnp.float32, low / len(cuts), high / len(cuts))
        gain = gain * jnp.repeat(jnp.exp(heights), shape[axis_at] // shards_of).reshape((-1,) + (1,) * (len(shape) - 1 - axis_at))
    return gain


def bell_draw(rng, dims, scale, bound, cuts=(), kind=jnp.bfloat16):
    entries = scale * jax.random.normal(rng, dims, jnp.float32)
    if cuts:
        entries = entries * block_scale(rng, dims, cuts, -0.22, 0.18)
    return jnp.clip(entries, -bound, bound).astype(kind)


def setup_inputs(seed: int = 0) -> dict:
    arg_keys = jax.random.split(jax.random.key(seed), 11)
    latents = bell_draw(arg_keys[0], (REQS, IMG, D), 1.0, 6.0, ((0, 4), (1, 32)))
    modulation = bell_draw(arg_keys[1], (REQS, 6, D), 0.5, 2.5, ((0, 4),))
    kv_cache = bell_draw(arg_keys[2], (REQS, IMG, 2 * D), 1.0, 6.0, ((0, 4), (1, 32)))
    text_kv = draw_text_kv(jax.random.fold_in(arg_keys[10], 71), 0)
    lengths = draw_lengths(jax.random.fold_in(arg_keys[10], 71), 0)
    refresh = draw_refresh(jax.random.fold_in(arg_keys[10], 71), 0)
    w_qkv = bell_draw(arg_keys[6], (D, 3 * D), D ** -0.5, 0.15625)
    w_out = bell_draw(arg_keys[7], (D, D), (max(1, 4 * D // IMG)) ** -0.5, 6.0, ((0, 4),))
    w_up = bell_draw(arg_keys[8], (D, FF), D ** -0.5, 0.15625, ((1, 4),))
    w_down = bell_draw(arg_keys[9], (FF, D), FF ** -0.5, 0.078125, ((0, 4),))
    return {"latents": latents, "modulation": modulation, "kv_cache": kv_cache, "text_kv": text_kv, "lengths": lengths, "refresh": refresh, "w_qkv": w_qkv, "w_out": w_out, "w_up": w_up, "w_down": w_down}


def layer_norm(values):
    average = lax.optimization_barrier(jnp.mean(values, -1, keepdims=True))
    centred = values - average
    spread = lax.optimization_barrier(jnp.mean(centred * centred, -1, keepdims=True))
    return centred * lax.rsqrt(spread + 1e-06)

def attend(queries, key_rows, text_rows, live_keys):
    model_width = queries.shape[1]
    row_count = queries.shape[0]
    head_count = model_width // HEAD
    head_group = math.gcd(head_count, 4)
    outputs = []
    for head_start in range(0, head_count, head_group):
        col_low = head_start * HEAD
        col_high = (head_start + head_group) * HEAD
        q_part = queries[:, col_low:col_high].reshape(row_count, head_group, HEAD).astype(jnp.float32)
        img_keys = key_rows[:, col_low:col_high].reshape(-1, head_group, HEAD).astype(jnp.float32)
        img_vals = key_rows[:, model_width + col_low:model_width + col_high].reshape(-1, head_group, HEAD).astype(jnp.float32)
        txt_keys = text_rows[:, col_low:col_high].reshape(-1, head_group, HEAD).astype(jnp.float32)
        txt_vals = text_rows[:, model_width + col_low:model_width + col_high].reshape(-1, head_group, HEAD).astype(jnp.float32)
        img_scores = jnp.einsum('qhe,khe->hqk', q_part, img_keys) * 0.125
        img_scores = jnp.where(live_keys[None, None, :], img_scores, -1e+30)
        txt_scores = jnp.einsum('qhe,khe->hqk', q_part, txt_keys) * 0.125
        row_max = jnp.maximum(lax.optimization_barrier(jnp.max(img_scores, -1, keepdims=True)), lax.optimization_barrier(jnp.max(txt_scores, -1, keepdims=True)))
        img_probs = jnp.exp(img_scores - row_max)
        txt_probs = jnp.exp(txt_scores - row_max)
        total_weight = lax.optimization_barrier(jnp.sum(img_probs, -1, keepdims=True)) + lax.optimization_barrier(jnp.sum(txt_probs, -1, keepdims=True))
        img_weights = (img_probs / total_weight).astype(jnp.bfloat16).astype(jnp.float32)
        txt_weights = (txt_probs / total_weight).astype(jnp.bfloat16).astype(jnp.float32)
        mixed_part = jnp.einsum('hqk,khe->qhe', img_weights, img_vals) + jnp.einsum('hqk,khe->qhe', txt_weights, txt_vals)
        outputs.append(mixed_part.reshape(row_count, head_group * HEAD))
    return jnp.concatenate(outputs, axis=1).astype(jnp.bfloat16)

def reference(latents, modulation, kv_cache, text_kv, lengths, refresh, w_qkv, w_out, w_up, w_down):
    model_width = latents.shape[2]
    results = []
    for request in range(REQS):
        tokens = latents[request]
        modulate = modulation[request].astype(jnp.float32)
        normed = (layer_norm(tokens.astype(jnp.float32)) * (1.0 + modulate[1]) + modulate[0]).astype(jnp.bfloat16)
        projections = jnp.dot(normed, w_qkv, preferred_element_type=jnp.float32).astype(jnp.bfloat16)
        queries = projections[:, :model_width]
        fresh_rows = projections[:, model_width:]
        block_ids = jnp.arange(IMG, dtype=jnp.int32) // TOK_DEV
        flagged = jnp.any(block_ids[:, None] == refresh[request][None, :], axis=1)
        live_keys = jnp.arange(IMG, dtype=jnp.int32) < lengths[request]
        cached = kv_cache[request]
        text_rows = text_kv[request]

        def one_tile(tile_pos):
            chosen = jnp.logical_or(flagged, block_ids == tile_pos)
            key_rows = jnp.where(chosen[:, None], fresh_rows, cached)
            tile_queries = lax.dynamic_slice_in_dim(queries, (tile_pos * TOK_DEV).astype(jnp.int32), TOK_DEV, 0)
            return attend(tile_queries, key_rows, text_rows, live_keys)
        attended = lax.map(one_tile, jnp.arange(N_TILE, dtype=jnp.int32)).reshape(IMG, model_width)
        projected = jnp.dot(attended, w_out, preferred_element_type=jnp.float32)
        mixed = tokens.astype(jnp.float32) + modulate[2] * projected
        mlp_input = (layer_norm(mixed) * (1.0 + modulate[4]) + modulate[3]).astype(jnp.bfloat16)
        hidden = jax.nn.gelu(jnp.dot(mlp_input, w_up, preferred_element_type=jnp.float32), approximate=True).astype(jnp.bfloat16)
        mlp_out = jnp.dot(hidden, w_down, preferred_element_type=jnp.float32)
        finished = jnp.where(live_keys[:, None], mixed + modulate[5] * mlp_out, 0.0)
        results.append(finished.astype(jnp.bfloat16))
    return jnp.stack(results)
```

```python
import functools

import jax
import jax.numpy as jnp
from jax import lax
from jax.experimental import pallas as pl
from jax.experimental.pallas import tpu as pltpu
from jax.sharding import Mesh
from jax.sharding import PartitionSpec as P

REQ = ("zh", "co")
TILE = ("y", "zl", "x")
HEAD = 64
BIG = 1e30
F32 = jnp.float32
BF16 = jnp.bfloat16


def layer_norm(values):
    average = jnp.mean(values, -1, keepdims=True)
    centred = values - average
    spread = jnp.mean(centred * centred, -1, keepdims=True)
    return centred * lax.rsqrt(spread + 1e-06)


def lane_iota(shape):
    return lax.broadcasted_iota(jnp.int32, shape, len(shape) - 1)


def row_iota(shape):
    return lax.broadcasted_iota(jnp.int32, shape, len(shape) - 2)


def swap_halves(values):
    return pltpu.roll(values, HEAD, axis=1)


def project_kernel(
    flag_ref, tokens_ref, mod_ref, wq_ref, wk_ref, wv_ref, ck_ref, cv_ref, send_ref, own_ref, normed_ref
):
    step = pl.program_id(0)
    rows = tokens_ref.shape[0]
    half = send_ref.shape[1] - rows

    @pl.when(step == 0)
    def _():
        shift = mod_ref[0:1, :].astype(F32)
        scale = mod_ref[1:2, :].astype(F32)
        normed = layer_norm(tokens_ref[...].astype(F32)) * (1.0 + scale) + shift
        normed_ref[...] = normed.astype(BF16)

    normed = normed_ref[...]
    wide = wq_ref.shape[1]
    heads = wide // HEAD
    queries = jnp.dot(normed, wq_ref[...], preferred_element_type=F32) * 0.125
    keys = jnp.dot(normed, wk_ref[...], preferred_element_type=F32)
    values = jnp.dot(normed, wv_ref[...], preferred_element_type=F32)
    flagged = flag_ref[0] != 0
    low = lane_iota((rows, 2 * HEAD)) < HEAD
    low_q = lane_iota((half, 2 * HEAD)) < HEAD
    pad = jnp.zeros((2 * half - rows, 2 * HEAD), F32)
    for pair in range(heads // 2):
        cols = slice(pair * 2 * HEAD, (pair + 1) * 2 * HEAD)
        q_top = queries[:half, cols]
        q_end = jnp.concatenate([queries[half:, cols], pad], axis=0)
        k_new, v_new = keys[:, cols], values[:, cols]
        k_out = jnp.where(flagged, k_new, ck_ref[:, cols].astype(F32))
        v_out = jnp.where(flagged, v_new, cv_ref[:, cols].astype(F32))
        for odd in range(2):
            if odd:
                q_pack = jnp.where(low_q, swap_halves(q_top), q_end)
                join = lambda k, v: jnp.where(low, swap_halves(k), v)
            else:
                q_pack = jnp.where(low_q, q_top, swap_halves(q_end))
                join = lambda k, v: jnp.where(low, k, swap_halves(v))
            q_pack = q_pack.astype(BF16)
            sent = join(k_out, v_out).astype(BF16)
            head = step * heads + pair * 2 + odd
            dest = head + head // 3
            own_ref[head, :rows, :] = join(k_new, v_new).astype(BF16)
            own_ref[head, rows:, :] = q_pack
            send_ref[dest, :rows, :] = sent
            send_ref[dest, rows:, :] = q_pack

            @pl.when(head % 3 == 2)
            def _():
                send_ref[dest + 1, :rows, :] = sent
                send_ref[dest + 1, rows:, :] = q_pack


def project(flag, tokens, modulate, w_qkv, cached):
    rows, width = tokens.shape
    half = 64
    block = 256
    steps = width // block
    heads = width // HEAD
    dests = heads + heads // 3
    whole = lambda *shape: pl.BlockSpec(shape, lambda s: (0,) * len(shape))
    return pl.pallas_call(
        project_kernel,
        grid=(steps,),
        out_shape=(
            jax.ShapeDtypeStruct((dests, rows + half, 2 * HEAD), BF16),
            jax.ShapeDtypeStruct((heads, rows + half, 2 * HEAD), BF16),
        ),
        in_specs=[
            pl.BlockSpec(memory_space=pltpu.SMEM),
            whole(rows, width),
            whole(6, width),
            pl.BlockSpec((width, block), lambda s: (0, s)),
            pl.BlockSpec((width, block), lambda s: (0, s + steps)),
            pl.BlockSpec((width, block), lambda s: (0, s + 2 * steps)),
            pl.BlockSpec((rows, block), lambda s: (0, s)),
            pl.BlockSpec((rows, block), lambda s: (0, s + steps)),
        ],
        out_specs=(
            whole(dests, rows + half, 2 * HEAD),
            whole(heads, rows + half, 2 * HEAD),
        ),
        scratch_shapes=[pltpu.VMEM((rows, width), BF16)],
        compiler_params=pltpu.CompilerParams(vmem_limit_bytes=40 << 20),
        name="project",
    )(flag, tokens, modulate, w_qkv, w_qkv, w_qkv, cached, cached)


def own_kernel(live_ref, own_ref, tk_ref, tv_ref, out_ref):
    rows = out_ref.shape[1]
    texts = tk_ref.shape[0]
    half = own_ref.shape[1] - rows
    low = lane_iota((rows, 2 * HEAD)) < HEAD
    live = lane_iota((rows, rows)) < live_ref[0]
    nt = (((1,), (1,)), ((), ()))
    text_keys = tk_ref[...]
    text_values = tv_ref[...]
    for odd in range(2):
        kv = own_ref[odd, :rows, :]
        folded = own_ref[odd, rows:, :].astype(F32)
        query = jnp.concatenate([folded, swap_halves(folded)[: rows - half]], axis=0)
        query = jnp.where(low, query, 0.0)
        text_query = swap_halves(query) if odd else query
        query = query.astype(BF16)
        text_query = text_query.astype(BF16)
        s_own = lax.dot_general(query, kv, nt, preferred_element_type=F32)
        s_own = jnp.where(live, s_own, -BIG)
        s_text = lax.dot_general(text_query, text_keys, nt, preferred_element_type=F32)
        top = jnp.maximum(
            jnp.max(s_own, -1, keepdims=True), jnp.max(s_text, -1, keepdims=True)
        )
        p_own = jnp.exp(s_own - top)
        p_text = jnp.exp(s_text - top)
        total = jnp.sum(p_own, -1, keepdims=True) + jnp.sum(p_text, -1, keepdims=True)
        mixed = jnp.dot(p_own.astype(BF16), kv, preferred_element_type=F32)
        from_text = jnp.dot(p_text.astype(BF16), text_values, preferred_element_type=F32)
        if not odd:
            from_text = swap_halves(from_text)
        mixed = (mixed + from_text) / total
        out_ref[odd] = jnp.where(low, top + jnp.log(total), mixed)


def own_attend(live, own, text_rows):
    heads, packed, _ = own.shape
    rows = packed - 64
    texts, width2 = text_rows.shape
    pairs = heads // 2
    return pl.pallas_call(
        own_kernel,
        grid=(pairs,),
        out_shape=jax.ShapeDtypeStruct((heads, rows, 2 * HEAD), F32),
        in_specs=[
            pl.BlockSpec(memory_space=pltpu.SMEM),
            pl.BlockSpec((2, packed, 2 * HEAD), lambda p: (p, 0, 0)),
            pl.BlockSpec((texts, 2 * HEAD), lambda p: (0, p)),
            pl.BlockSpec((texts, 2 * HEAD), lambda p: (0, p + pairs)),
        ],
        out_specs=pl.BlockSpec((2, rows, 2 * HEAD), lambda p: (p, 0, 0)),
        compiler_params=pltpu.CompilerParams(vmem_limit_bytes=16 << 20),
        cost_estimate=pl.CostEstimate(
            flops=2 * 4 * rows * (rows + texts) * 64 * heads,
            bytes_accessed=6 << 20,
            transcendentals=rows * (rows + texts) * heads,
        ),
        name="own_attend",
    )(live, own, text_rows, text_rows)


def head_kernel(len_ref, pack_ref, out_ref, q_ref, k_ref, v_ref, kt_ref, s_ref):
    step = pl.program_id(0)
    tiles, packed, _ = pack_ref.shape
    rows = packed - 64
    total_rows = tiles * rows
    block = out_ref.shape[0]
    chunk = 256

    @pl.when(step == 0)
    def _():
        low = lane_iota((2 * rows, 2 * HEAD)) < HEAD
        feature = lane_iota((2 * rows, 2 * HEAD)) - HEAD
        second = (row_iota((2 * rows, 2 * HEAD)) >= rows).astype(jnp.int32)

        def fill(pair, carry):
            first = 2 * pair
            kv = jnp.concatenate(
                [pack_ref[first, :rows, :].astype(F32), pack_ref[first + 1, :rows, :].astype(F32)],
                axis=0,
            )
            parts = []
            for t in range(2):
                folded = pack_ref[first + t, rows:, :].astype(F32)
                parts += [folded, swap_halves(folded)[: rows - 64]]
            query = jnp.concatenate(parts, axis=0)
            tile = first + second
            masked = jnp.logical_or(feature == tile, feature == 32)
            query = jnp.where(low, query, jnp.where(masked, -BIG, 0.0))
            index = pair * 2 * rows + row_iota((2 * rows, 2 * HEAD))
            dead = jnp.logical_and(feature == 32, index >= len_ref[0])
            held = jnp.logical_or(feature == tile, dead)
            key = jnp.where(low, kv, jnp.where(held, 1.0, 0.0))
            at = pl.ds(pl.multiple_of(pair * 2 * rows, 16), 2 * rows)
            q_ref[at, :] = query.astype(BF16)
            k_ref[at, :] = key.astype(BF16)
            v_ref[at, :] = jnp.where(low, 1.0, kv).astype(BF16)
            return carry

        lax.fori_loop(0, tiles // 2, fill, 0)
        for c in range(total_rows // chunk):
            part = slice(c * chunk, (c + 1) * chunk)
            kt_ref[:, part] = jnp.transpose(k_ref[part, :].astype(F32)).astype(BF16)

    query = q_ref[pl.ds(pl.multiple_of(step * block, block), block), :]
    top = jnp.full((block, 128), -jnp.inf, F32)
    for c in range(total_rows // chunk):
        part = slice(c * chunk, (c + 1) * chunk)
        scores = jnp.dot(query, kt_ref[:, part], preferred_element_type=F32)
        s_ref[:, part] = scores
        for i in range(chunk // 128):
            top = jnp.maximum(top, scores[:, i * 128 : (i + 1) * 128])
    top = jnp.max(top, -1, keepdims=True)
    total = jnp.zeros((block, 2 * HEAD), F32)
    for c in range(total_rows // chunk):
        part = slice(c * chunk, (c + 1) * chunk)
        probs = jnp.exp(s_ref[:, part] - top).astype(BF16)
        total = total + jnp.dot(probs, v_ref[part, :], preferred_element_type=F32)
    weight = total[:, 0:1]
    lse = top + jnp.log(weight)
    high = lse.astype(BF16).astype(F32)
    lane = lane_iota((block, 2 * HEAD))
    result = jnp.where(lane < 32, high, jnp.where(lane < HEAD, lse - high, total / weight))
    out_ref[...] = result.astype(BF16)


def head_attend(length, pack):
    tiles, packed, lanes = pack.shape
    rows = packed - 64
    total_rows = tiles * rows
    block = 384
    return pl.pallas_call(
        head_kernel,
        grid=(total_rows // block,),
        out_shape=jax.ShapeDtypeStruct((total_rows, lanes), BF16),
        in_specs=[
            pl.BlockSpec(memory_space=pltpu.SMEM),
            pl.BlockSpec((tiles, packed, lanes), lambda s: (0, 0, 0)),
        ],
        out_specs=pl.BlockSpec((block, lanes), lambda s: (s, 0)),
        scratch_shapes=[
            pltpu.VMEM((total_rows, lanes), BF16),
            pltpu.VMEM((total_rows, lanes), BF16),
            pltpu.VMEM((total_rows, lanes), BF16),
            pltpu.VMEM((lanes, total_rows), BF16),
            pltpu.VMEM((block, total_rows), F32),
        ],
        compiler_params=pltpu.CompilerParams(vmem_limit_bytes=40 << 20),
        name="head_attend",
    )(length, pack)


def merge_kernel(far_ref, own_ref, out_ref):
    heads = own_ref.shape[0]
    rows = own_ref.shape[1]
    low = lane_iota((rows, 2 * HEAD)) < HEAD
    for pair in range(heads // 2):
        both = []
        for odd in range(2):
            head = 2 * pair + odd
            far = far_ref[head + head // 3].astype(F32)
            own = own_ref[head]
            far_lse = far[:, 0:1] + far[:, 32:33]
            own_lse = own[:, 0:1]
            share = 1.0 / (1.0 + jnp.exp(own_lse - far_lse))
            other = 1.0 / (1.0 + jnp.exp(far_lse - own_lse))
            both.append(share * far + other * own)
        joined = jnp.where(low, swap_halves(both[0]), both[1])
        out_ref[:, pair * 2 * HEAD : (pair + 1) * 2 * HEAD] = joined.astype(BF16)


def merge(far, own):
    heads, rows, lanes = own.shape
    return pl.pallas_call(
        merge_kernel,
        out_shape=jax.ShapeDtypeStruct((rows, heads * HEAD), BF16),
        in_specs=[pl.BlockSpec(memory_space=pltpu.VMEM)] * 2,
        out_specs=pl.BlockSpec(memory_space=pltpu.VMEM),
        compiler_params=pltpu.CompilerParams(vmem_limit_bytes=16 << 20),
        name="merge",
    )(far, own)


def swap(values, axis):
    return lax.ppermute(values, axis, [(0, 1), (1, 0)])


def per_device(
    latents, modulation, kv_cache, text_kv, lengths, refresh, w_qkv, w_out, w_up, w_down
):
    tokens = latents[0]
    rows = tokens.shape[0]
    modulate = modulation[0].astype(F32)
    tile_index = lax.axis_index(TILE)
    length = lengths[0]
    flag = jnp.any(refresh[0] == tile_index).astype(jnp.int32).reshape(1)
    all_w_out = lax.all_gather(w_out, REQ, axis=0, tiled=True)
    send, own = project(flag, tokens, modulation[0], w_qkv, kv_cache[0])
    pack = lax.all_to_all(send, TILE, split_axis=0, concat_axis=0, tiled=True)
    live = (length - tile_index * rows).reshape(1)
    own_part = own_attend(live, own, text_kv[0])
    far = head_attend(length.reshape(1), pack)
    far = lax.all_to_all(
        far.reshape(-1, rows, 2 * HEAD), TILE, split_axis=0, concat_axis=0, tiled=True
    )
    attended = merge(far, own_part)
    projected = jnp.dot(attended, all_w_out, preferred_element_type=F32)
    mixed = tokens.astype(F32) + modulate[2] * projected
    mlp_input = (layer_norm(mixed) * (1.0 + modulate[4]) + modulate[3]).astype(BF16)

    def feed(values):
        hidden = jax.nn.gelu(jnp.dot(values, w_up, preferred_element_type=F32), approximate=True)
        return jnp.dot(hidden.astype(BF16), w_down, preferred_element_type=F32)

    far_z = swap(mlp_input, "zh")
    near = swap(mlp_input, "co")
    far_both = swap(far_z, "co")
    parts_near = feed(jnp.concatenate([mlp_input, near], axis=0))
    parts_far = feed(jnp.concatenate([far_z, far_both], axis=0))
    sum_far = parts_far[:rows] + swap(parts_far[rows:].astype(BF16), "co").astype(F32)
    sum_near = parts_near[:rows] + swap(parts_near[rows:].astype(BF16), "co").astype(F32)
    mlp_out = sum_near + swap(sum_far.astype(BF16), "zh").astype(F32)
    positions = tile_index * rows + jnp.arange(rows, dtype=jnp.int32)
    live_rows = positions < length
    finished = jnp.where(live_rows[:, None], mixed + modulate[5] * mlp_out, 0.0)
    return finished.astype(BF16)[None]


def solution(mesh):
    fine = Mesh(mesh.devices.reshape(2, 2, 4, 2, 4), REQ + TILE)
    return jax.shard_map(
        per_device,
        mesh=fine,
        in_specs=(
            P(REQ, TILE, None),
            P(REQ, None, None),
            P(REQ, TILE, None),
            P(REQ, None, None),
            P(REQ),
            P(REQ, None),
            P(),
            P(REQ, None),
            P(None, REQ),
            P(REQ, None),
        ),
        out_specs=P(REQ, TILE, None),
        check_vma=False,
    )
```

```python
import jax
import jax.numpy as jnp
from jax import lax
from jax.experimental import pallas as pl
from jax.experimental.pallas import tpu as pltpu
from jax.sharding import Mesh
from jax.sharding import PartitionSpec as P

REQ = ("zh", "co")
TILE = ("y", "zl", "x")
HEAD = 64
BIG = 1e30
F32 = jnp.float32
BF16 = jnp.bfloat16


def layer_norm(values):
    average = jnp.mean(values, -1, keepdims=True)
    centred = values - average
    spread = jnp.mean(centred * centred, -1, keepdims=True)
    return centred * lax.rsqrt(spread + 1e-06)


def lane_iota(shape):
    return lax.broadcasted_iota(jnp.int32, shape, len(shape) - 1)


def row_iota(shape):
    return lax.broadcasted_iota(jnp.int32, shape, len(shape) - 2)


def swap_halves(values):
    return pltpu.roll(values, HEAD, axis=1)


def project_kernel(
    tile_ref,
    refresh_ref,
    tokens_ref,
    mod_ref,
    wq_ref,
    wk_ref,
    wv_ref,
    ck_ref,
    cv_ref,
    send_ref,
    own_ref,
    normed_ref,
):
    step = pl.program_id(0)
    rows = tokens_ref.shape[0]
    half = send_ref.shape[1] - rows

    @pl.when(step == 0)
    def _():
        shift = mod_ref[0:1, :].astype(F32)
        scale = mod_ref[1:2, :].astype(F32)
        normed = layer_norm(tokens_ref[...].astype(F32)) * (1.0 + scale) + shift
        normed_ref[...] = normed.astype(BF16)

    normed = normed_ref[...]
    wide = wq_ref.shape[1]
    heads = wide // HEAD
    queries = jnp.dot(normed, wq_ref[...], preferred_element_type=F32) * 0.125
    keys = jnp.dot(normed, wk_ref[...], preferred_element_type=F32)
    values = jnp.dot(normed, wv_ref[...], preferred_element_type=F32)
    flagged = refresh_ref[0, 0] == tile_ref[0]
    for slot in range(1, refresh_ref.shape[1]):
        flagged = jnp.logical_or(flagged, refresh_ref[0, slot] == tile_ref[0])
    low = lane_iota((rows, 2 * HEAD)) < HEAD
    low_q = lane_iota((half, 2 * HEAD)) < HEAD
    pad = jnp.zeros((2 * half - rows, 2 * HEAD), F32)
    for pair in range(heads // 2):
        cols = slice(pair * 2 * HEAD, (pair + 1) * 2 * HEAD)
        q_top = queries[:half, cols]
        q_end = jnp.concatenate([queries[half:, cols], pad], axis=0)
        k_new, v_new = keys[:, cols], values[:, cols]
        k_out = jnp.where(flagged, k_new, ck_ref[:, cols].astype(F32))
        v_out = jnp.where(flagged, v_new, cv_ref[:, cols].astype(F32))
        for odd in range(2):
            if odd:
                q_pack = jnp.where(low_q, swap_halves(q_top), q_end)
                join = lambda k, v: jnp.where(low, swap_halves(k), v)
            else:
                q_pack = jnp.where(low_q, q_top, swap_halves(q_end))
                join = lambda k, v: jnp.where(low, k, swap_halves(v))
            q_pack = q_pack.astype(BF16)
            sent = join(k_out, v_out).astype(BF16)
            head = step * heads + pair * 2 + odd
            dest = head + head // 3
            own_ref[head, :rows, :] = join(k_new, v_new).astype(BF16)
            own_ref[head, rows:, :] = q_pack
            send_ref[dest, :rows, :] = sent
            send_ref[dest, rows:, :] = q_pack

            @pl.when(head % 3 == 2)
            def _():
                send_ref[dest + 1, :rows, :] = sent
                send_ref[dest + 1, rows:, :] = q_pack


def project(tile_index, refresh, tokens, modulate, w_qkv, cached):
    rows, width = tokens.shape
    half = 64
    block = 256
    steps = width // block
    heads = width // HEAD
    dests = heads + heads // 3
    whole = lambda *shape: pl.BlockSpec(shape, lambda s: (0,) * len(shape))
    return pl.pallas_call(
        project_kernel,
        grid=(steps,),
        out_shape=(
            jax.ShapeDtypeStruct((dests, rows + half, 2 * HEAD), BF16),
            jax.ShapeDtypeStruct((heads, rows + half, 2 * HEAD), BF16),
        ),
        in_specs=[
            pl.BlockSpec(memory_space=pltpu.SMEM),
            pl.BlockSpec(memory_space=pltpu.SMEM),
            whole(rows, width),
            whole(6, width),
            pl.BlockSpec((width, block), lambda s: (0, s)),
            pl.BlockSpec((width, block), lambda s: (0, s + steps)),
            pl.BlockSpec((width, block), lambda s: (0, s + 2 * steps)),
            pl.BlockSpec((rows, block), lambda s: (0, s)),
            pl.BlockSpec((rows, block), lambda s: (0, s + steps)),
        ],
        out_specs=(
            whole(dests, rows + half, 2 * HEAD),
            whole(heads, rows + half, 2 * HEAD),
        ),
        scratch_shapes=[pltpu.VMEM((rows, width), BF16)],
        compiler_params=pltpu.CompilerParams(vmem_limit_bytes=40 << 20),
        name="project",
    )(tile_index, refresh, tokens, modulate, w_qkv, w_qkv, w_qkv, cached, cached)


def own_kernel(live_ref, own_ref, tk_ref, tv_ref, out_ref):
    rows = out_ref.shape[1]
    texts = tk_ref.shape[0]
    half = own_ref.shape[1] - rows
    low = lane_iota((rows, 2 * HEAD)) < HEAD
    live = lane_iota((rows, rows)) < live_ref[0]
    nt = (((1,), (1,)), ((), ()))
    text_keys = tk_ref[...]
    text_values = tv_ref[...]
    for odd in range(2):
        kv = own_ref[odd, :rows, :]
        folded = own_ref[odd, rows:, :].astype(F32)
        query = jnp.concatenate([folded, swap_halves(folded)[: rows - half]], axis=0)
        query = jnp.where(low, query, 0.0)
        text_query = swap_halves(query) if odd else query
        query = query.astype(BF16)
        text_query = text_query.astype(BF16)
        s_own = lax.dot_general(query, kv, nt, preferred_element_type=F32)
        s_own = jnp.where(live, s_own, -BIG)
        s_text = lax.dot_general(text_query, text_keys, nt, preferred_element_type=F32)
        top = jnp.maximum(
            jnp.max(s_own, -1, keepdims=True), jnp.max(s_text, -1, keepdims=True)
        )
        p_own = jnp.exp(s_own - top)
        p_text = jnp.exp(s_text - top)
        total = jnp.sum(p_own, -1, keepdims=True) + jnp.sum(p_text, -1, keepdims=True)
        mixed = jnp.dot(p_own.astype(BF16), kv, preferred_element_type=F32)
        from_text = jnp.dot(p_text.astype(BF16), text_values, preferred_element_type=F32)
        if not odd:
            from_text = swap_halves(from_text)
        mixed = (mixed + from_text) / total
        out_ref[odd] = jnp.where(low, top + jnp.log(total), mixed)


def own_attend(live, own, text_rows):
    heads, packed, _ = own.shape
    rows = packed - 64
    texts, width2 = text_rows.shape
    pairs = heads // 2
    return pl.pallas_call(
        own_kernel,
        grid=(pairs,),
        out_shape=jax.ShapeDtypeStruct((heads, rows, 2 * HEAD), F32),
        in_specs=[
            pl.BlockSpec(memory_space=pltpu.SMEM),
            pl.BlockSpec((2, packed, 2 * HEAD), lambda p: (p, 0, 0)),
            pl.BlockSpec((texts, 2 * HEAD), lambda p: (0, p)),
            pl.BlockSpec((texts, 2 * HEAD), lambda p: (0, p + pairs)),
        ],
        out_specs=pl.BlockSpec((2, rows, 2 * HEAD), lambda p: (p, 0, 0)),
        compiler_params=pltpu.CompilerParams(vmem_limit_bytes=16 << 20),
        cost_estimate=pl.CostEstimate(
            flops=2 * 4 * rows * (rows + texts) * 64 * heads,
            bytes_accessed=6 << 20,
            transcendentals=rows * (rows + texts) * heads,
        ),
        name="own_attend",
    )(live, own, text_rows, text_rows)


def head_kernel(len_ref, pack_ref, out_ref, v_ref, kt_ref, s_ref):
    step = pl.program_id(0)
    tiles, packed, lanes = pack_ref.shape
    rows = packed - HEAD
    total_rows = tiles * rows
    group = out_ref.shape[0]
    block = group * rows
    piece = 256
    chunk = 1920
    low = lane_iota((1, lanes)) < HEAD

    @pl.when(step == 0)
    def _():
        for pair in range(tiles // 2):
            both = jnp.concatenate(
                [pack_ref[2 * pair + t, :rows, :].astype(F32) for t in range(2)], axis=0
            )
            v_ref[pair * 2 * rows : (pair + 1) * 2 * rows, :] = both.astype(BF16)
        feature = row_iota((HEAD, piece))
        for c in range(total_rows // piece):
            part = slice(c * piece, (c + 1) * piece)
            kv = v_ref[part, :]
            index = lane_iota((HEAD, piece)) + c * piece
            own = jnp.logical_and(index >= feature * rows, index < feature * rows + rows)
            held = jnp.logical_or(own, jnp.logical_and(feature == tiles, index >= len_ref[0]))
            kt_ref[:HEAD, part] = jnp.transpose(kv.astype(F32))[:HEAD].astype(BF16)
            kt_ref[HEAD:, part] = jnp.where(held, 1.0, 0.0).astype(BF16)
            v_ref[part, :] = jnp.where(low, jnp.ones((), BF16), kv)

    feature = lane_iota((1, lanes)) - HEAD
    parts = []
    for t in range(group):
        tile = step * group + t
        mask = jnp.where(jnp.logical_or(feature == tile, feature == tiles), -BIG, 0.0)
        folded = pack_ref[tile, rows:, :].astype(F32)
        parts.append(jnp.where(low, folded, mask))
        parts.append(jnp.where(low, swap_halves(folded)[: rows - HEAD], mask))
    query = jnp.concatenate(parts, axis=0).astype(BF16)
    top = jnp.full((block, 128), -jnp.inf, F32)
    for c in range(total_rows // chunk):
        part = slice(c * chunk, (c + 1) * chunk)
        scores = jnp.dot(query, kt_ref[:, part], preferred_element_type=F32)
        s_ref[:, part] = scores
        for i in range(chunk // 128):
            top = jnp.maximum(top, scores[:, i * 128 : (i + 1) * 128])
    top = jnp.max(top, -1, keepdims=True)
    total = jnp.zeros((block, lanes), F32)
    for c in range(total_rows // chunk):
        part = slice(c * chunk, (c + 1) * chunk)
        probs = jnp.exp(s_ref[:, part] - top).astype(BF16)
        total = total + jnp.dot(probs, v_ref[part, :], preferred_element_type=F32)
    weight = total[:, 0:1]
    lse = jnp.broadcast_to(top + jnp.log(weight), (block, lanes))
    result = total / weight
    diagonal = row_iota((HEAD, lanes)) == lane_iota((HEAD, lanes))
    line = row_iota((8, lanes))
    pad = jnp.zeros((2 * HEAD - rows, lanes), F32)
    for t in range(group):
        first = slice(t * rows, t * rows + HEAD)
        rest = slice(t * rows + HEAD, (t + 1) * rows)
        lse_a = jnp.sum(jnp.where(diagonal, lse[first], 0.0), 0, keepdims=True)
        lse_b = jnp.concatenate([lse[rest], pad], axis=0)
        lse_b = jnp.sum(jnp.where(diagonal, lse_b, 0.0), 0, keepdims=True)
        high_a = lse_a.astype(BF16).astype(F32)
        high_b = lse_b.astype(BF16).astype(F32)
        stats = jnp.where(line == 2, lse_a - high_a, lse_b - high_b)
        stats = jnp.where(line == 0, high_a, jnp.where(line == 1, high_b, stats))
        folded = jnp.concatenate([swap_halves(result[rest]), stats], axis=0)
        out_ref[t] = jnp.where(low, folded, result[first]).astype(BF16)


def head_attend(length, pack):
    tiles, packed, lanes = pack.shape
    rows = packed - HEAD
    total_rows = tiles * rows
    group = 8
    block = group * rows
    return pl.pallas_call(
        head_kernel,
        grid=(tiles // group,),
        out_shape=jax.ShapeDtypeStruct((tiles, HEAD, lanes), BF16),
        in_specs=[
            pl.BlockSpec(memory_space=pltpu.SMEM),
            pl.BlockSpec((tiles, packed, lanes), lambda s: (0, 0, 0)),
        ],
        out_specs=pl.BlockSpec((group, HEAD, lanes), lambda s: (s, 0, 0)),
        scratch_shapes=[
            pltpu.VMEM((total_rows, lanes), BF16),
            pltpu.VMEM((lanes, total_rows), BF16),
            pltpu.VMEM((block, total_rows), F32),
        ],
        compiler_params=pltpu.CompilerParams(vmem_limit_bytes=44 << 20),
        cost_estimate=pl.CostEstimate(
            flops=4 * total_rows * total_rows * 128,
            bytes_accessed=4 << 20,
            transcendentals=total_rows * total_rows,
        ),
        name="head_attend",
    )(length, pack)


def merge_kernel(far_ref, own_ref, w_ref, tokens_ref, mod_ref, mixed_ref, input_ref, att_ref):
    heads, rows, lanes = own_ref.shape
    low = lane_iota((1, lanes)) < HEAD
    diagonal = row_iota((HEAD, lanes)) == lane_iota((HEAD, lanes))

    def column(line):
        spread = jnp.where(diagonal, jnp.broadcast_to(line, (HEAD, lanes)), 0.0)
        return jnp.sum(spread, -1, keepdims=True)

    for pair in range(heads // 2):
        both = []
        for odd in range(2):
            head = 2 * pair + odd
            folded = far_ref[head + head // 3].astype(F32)
            stats = folded[rows - HEAD :]
            first = column(stats[0:1] + stats[2:3])
            rest = column(stats[1:2] + stats[3:4])
            far_lse = jnp.concatenate([first, rest[: rows - HEAD]], axis=0)
            far = jnp.concatenate([folded, swap_halves(folded)[: rows - HEAD]], axis=0)
            own = own_ref[head]
            gap = jnp.broadcast_to(far_lse, (rows, lanes)) - own[:, 0:1]
            share = 1.0 / (1.0 + jnp.exp(-gap))
            other = 1.0 / (1.0 + jnp.exp(gap))
            both.append(share * far + other * own)
        joined = jnp.where(low, swap_halves(both[0]), both[1])
        att_ref[:, pair * lanes : (pair + 1) * lanes] = joined.astype(BF16)
    projected = jnp.dot(att_ref[...], w_ref[...], preferred_element_type=F32)
    mod = mod_ref[...].astype(F32)
    mixed = tokens_ref[...].astype(F32) + mod[2:3] * projected
    mixed_ref[...] = mixed
    input_ref[...] = (layer_norm(mixed) * (1.0 + mod[4:5]) + mod[3:4]).astype(BF16)


def merge(far, own, w_out, tokens, modulate):
    rows, width = tokens.shape
    return pl.pallas_call(
        merge_kernel,
        out_shape=(
            jax.ShapeDtypeStruct((rows, width), F32),
            jax.ShapeDtypeStruct((rows, width), BF16),
        ),
        in_specs=[pl.BlockSpec(memory_space=pltpu.VMEM)] * 5,
        out_specs=(pl.BlockSpec(memory_space=pltpu.VMEM),) * 2,
        scratch_shapes=[pltpu.VMEM((rows, width), BF16)],
        compiler_params=pltpu.CompilerParams(vmem_limit_bytes=24 << 20),
        name="merge",
    )(far, own, w_out, tokens, modulate)


def feed_kernel(first_ref, second_ref, up_ref, down_ref, keep_ref, pass_ref, x_ref, sum_ref):
    step = pl.program_id(0)
    rows = first_ref.shape[0]

    @pl.when(step == 0)
    def _():
        both = [first_ref[...].astype(F32), second_ref[...].astype(F32)]
        x_ref[...] = jnp.concatenate(both, axis=0).astype(BF16)

    hidden = jnp.dot(x_ref[...], up_ref[...], preferred_element_type=F32)
    hidden = jax.nn.gelu(hidden, approximate=True).astype(BF16)
    part = jnp.dot(hidden, down_ref[...], preferred_element_type=F32)
    last = pl.num_programs(0) - 1

    @pl.when(step == 0)
    def _():
        sum_ref[...] = part

    @pl.when(jnp.logical_and(step > 0, step < last))
    def _():
        sum_ref[...] += part

    @pl.when(step == last)
    def _():
        keep_ref[...] = sum_ref[:rows] + part[:rows]
        pass_ref[...] = (sum_ref[rows:] + part[rows:]).astype(BF16)


def feed(first, second, w_up, w_down):
    rows, width = first.shape
    hidden = w_up.shape[1]
    block = 512
    whole = lambda *shape: pl.BlockSpec(shape, lambda s: (0,) * len(shape))
    return pl.pallas_call(
        feed_kernel,
        grid=(hidden // block,),
        out_shape=(
            jax.ShapeDtypeStruct((rows, width), F32),
            jax.ShapeDtypeStruct((rows, width), BF16),
        ),
        in_specs=[
            whole(rows, width),
            whole(rows, width),
            pl.BlockSpec((width, block), lambda s: (0, s)),
            pl.BlockSpec((block, width), lambda s: (s, 0)),
        ],
        out_specs=(whole(rows, width), whole(rows, width)),
        scratch_shapes=[
            pltpu.VMEM((2 * rows, width), BF16),
            pltpu.VMEM((2 * rows, width), F32),
        ],
        compiler_params=pltpu.CompilerParams(vmem_limit_bytes=32 << 20),
        cost_estimate=pl.CostEstimate(
            flops=8 * rows * width * hidden,
            bytes_accessed=4 * width * hidden,
            transcendentals=2 * rows * hidden,
        ),
        name="feed",
    )(first, second, w_up, w_down)


def swap(values, axis):
    return lax.ppermute(values, axis, [(0, 1), (1, 0)])


def per_device(
    latents, modulation, kv_cache, text_kv, lengths, refresh, w_qkv, w_out, w_up, w_down
):
    tokens = latents[0]
    rows = tokens.shape[0]
    tile_index = lax.axis_index(TILE).astype(jnp.int32)
    length = lengths[0]
    all_w_out = lax.all_gather(w_out, REQ, axis=0, tiled=True)
    send, own = project(
        tile_index.reshape(1), refresh, tokens, modulation[0], w_qkv, kv_cache[0]
    )
    pack = lax.all_to_all(send, TILE, split_axis=0, concat_axis=0, tiled=True)
    live = (length - tile_index * rows).reshape(1)
    own_part = own_attend(live, own, text_kv[0])
    pack, own_part = lax.optimization_barrier((pack, own_part))
    far = head_attend(lengths, pack)
    far = lax.all_to_all(far, TILE, split_axis=0, concat_axis=0, tiled=True)
    mixed, mlp_input = merge(far, own_part, all_w_out, tokens, modulation[0])

    far_z = swap(mlp_input, "zh")
    near = swap(mlp_input, "co")
    near_keep, near_pass = feed(mlp_input, near, w_up, w_down)
    far_z, near_keep, near_pass = lax.optimization_barrier((far_z, near_keep, near_pass))
    far_both = swap(far_z, "co")
    far_keep, far_pass = feed(far_z, far_both, w_up, w_down)
    sum_far = (far_keep + swap(far_pass, "co").astype(F32)).astype(BF16)
    near_sum = near_keep + swap(near_pass, "co").astype(F32)
    mlp_out = near_sum + swap(sum_far, "zh").astype(F32)
    positions = tile_index * rows + jnp.arange(rows, dtype=jnp.int32)
    live_rows = positions < length
    gate = modulation[0, 5].astype(F32)
    finished = jnp.where(live_rows[:, None], mixed + gate * mlp_out, 0.0)
    return finished.astype(BF16)[None]


def solution(mesh):
    fine = Mesh(mesh.devices.reshape(2, 2, 4, 2, 4), REQ + TILE)
    return jax.shard_map(
        per_device,
        mesh=fine,
        in_specs=(
            P(REQ, TILE, None),
            P(REQ, None, None),
            P(REQ, TILE, None),
            P(REQ, None, None),
            P(REQ),
            P(REQ, None),
            P(),
            P(REQ, None),
            P(None, REQ),
            P(REQ, None),
        ),
        out_specs=P(REQ, TILE, None),
        check_vma=False,
    )
```

```python
import jax
import jax.numpy as jnp
from jax import lax
from jax.experimental import pallas as pl
from jax.experimental.pallas import tpu as pltpu
from jax.sharding import Mesh
from jax.sharding import PartitionSpec as P

REQ = ("zh", "co")
TILE = ("y", "zl", "x")
HEAD = 64
BIG = 1e30
F32 = jnp.float32
BF16 = jnp.bfloat16


def layer_norm(values):
    average = jnp.mean(values, -1, keepdims=True)
    centred = values - average
    spread = jnp.mean(centred * centred, -1, keepdims=True)
    return centred * lax.rsqrt(spread + 1e-06)


def lane_iota(shape):
    return lax.broadcasted_iota(jnp.int32, shape, len(shape) - 1)


def row_iota(shape):
    return lax.broadcasted_iota(jnp.int32, shape, len(shape) - 2)


def swap_halves(values):
    return pltpu.roll(values, HEAD, axis=1)


def project_kernel(
    tile_ref,
    refresh_ref,
    tokens_ref,
    mod_ref,
    w_ref,
    cache_ref,
    send_ref,
    own_ref,
    picks,
    tokens,
    mod,
    weights,
    cache,
    sent,
    kept,
    in_sems,
    w_sems,
    send_sem,
    own_sem,
):
    rows, width = tokens.shape
    half = HEAD
    blocks = w_sems.shape[0]
    wide = width // blocks
    inputs = (
        (tokens_ref, tokens),
        (mod_ref, mod),
        (refresh_ref, picks),
        (cache_ref, cache),
    )
    input_copies = [
        pltpu.make_async_copy(src, dst, in_sems.at[i]) for i, (src, dst) in enumerate(inputs)
    ]
    w_copies = [
        [
            pltpu.make_async_copy(
                w_ref.at[:, kind * width + b * wide : kind * width + (b + 1) * wide],
                weights.at[:, kind * width + b * wide : kind * width + (b + 1) * wide],
                w_sems.at[b, kind],
            )
            for kind in range(3)
        ]
        for b in range(blocks)
    ]
    for copy in input_copies[:3]:
        copy.start()
    for kind in range(3):
        w_copies[0][kind].start()
    input_copies[3].start()
    for b in range(1, blocks):
        for copy in w_copies[b]:
            copy.start()
    for copy in input_copies[:3]:
        copy.wait()
    normed = layer_norm(tokens[...].astype(F32)) * (1.0 + mod[1:2, :].astype(F32))
    normed = (normed + mod[0:1, :].astype(F32)).astype(BF16)
    flagged = picks[0, 0] == tile_ref[0]
    for slot in range(1, picks.shape[1]):
        flagged = jnp.logical_or(flagged, picks[0, slot] == tile_ref[0])
    low = lane_iota((1, 2 * HEAD)) < HEAD
    pad = jnp.zeros((2 * half - rows, 2 * HEAD), F32)
    input_copies[3].wait()
    out_copies = []
    for b in range(blocks):
        made = []
        for kind in range(3):
            w_copies[b][kind].wait()
            first = kind * width + b * wide
            made.append(
                jnp.dot(normed, weights[:, first : first + wide], preferred_element_type=F32)
            )
        queries, keys, values = made
        queries = queries * 0.125
        k_old = cache[:, b * wide : (b + 1) * wide].astype(F32)
        v_old = cache[:, width + b * wide : width + (b + 1) * wide].astype(F32)
        k_sent = jnp.where(flagged, keys, k_old)
        v_sent = jnp.where(flagged, values, v_old)
        for pair in range(wide // (2 * HEAD)):
            cols = slice(pair * 2 * HEAD, (pair + 1) * 2 * HEAD)
            q_top = queries[:half, cols]
            q_end = jnp.concatenate([queries[half:, cols], pad], axis=0)
            for odd in range(2):
                if odd:
                    q_pack = jnp.where(low, swap_halves(q_top), q_end)
                    join = lambda k, v: jnp.where(low, swap_halves(k), v)
                else:
                    q_pack = jnp.where(low, q_top, swap_halves(q_end))
                    join = lambda k, v: jnp.where(low, k, swap_halves(v))
                q_pack = q_pack.astype(BF16)
                out = join(k_sent[:, cols], v_sent[:, cols]).astype(BF16)
                head = (b * wide) // HEAD + pair * 2 + odd
                kept[head, :rows, :] = join(keys[:, cols], values[:, cols]).astype(BF16)
                kept[head, rows:, :] = q_pack
                dest = head + head // 3
                for copy in range(2 if head % 3 == 2 else 1):
                    sent[dest + copy, :rows, :] = out
                    sent[dest + copy, rows:, :] = q_pack
        head = (b * wide) // HEAD
        last = (b + 1) * wide // HEAD
        dest, dest_last = head + head // 3, last + last // 3
        out_copies.append(
            pltpu.make_async_copy(
                sent.at[dest:dest_last], send_ref.at[dest:dest_last], send_sem.at[b]
            )
        )
        out_copies.append(
            pltpu.make_async_copy(kept.at[head:last], own_ref.at[head:last], own_sem.at[b])
        )
        out_copies[-2].start()
        out_copies[-1].start()
    for copy in out_copies:
        copy.wait()


def project(tile_index, refresh, tokens, modulate, w_qkv, cached):
    rows, width = tokens.shape
    blocks = 4
    heads = width // HEAD
    dests = heads + heads // 3
    packed = rows + HEAD
    anywhere = pl.BlockSpec(memory_space=pltpu.HBM)
    return pl.pallas_call(
        project_kernel,
        out_shape=(
            pltpu.HBM((dests, packed, 2 * HEAD), BF16),
            pltpu.HBM((heads, packed, 2 * HEAD), BF16),
        ),
        in_specs=[pl.BlockSpec(memory_space=pltpu.SMEM)] + [anywhere] * 5,
        out_specs=(anywhere, anywhere),
        scratch_shapes=[
            pltpu.SMEM(refresh.shape, jnp.int32),
            pltpu.VMEM(tokens.shape, BF16),
            pltpu.VMEM(modulate.shape, BF16),
            pltpu.VMEM(w_qkv.shape, BF16),
            pltpu.VMEM(cached.shape, BF16),
            pltpu.VMEM((dests, packed, 2 * HEAD), BF16),
            pltpu.VMEM((heads, packed, 2 * HEAD), BF16),
            pltpu.SemaphoreType.DMA((4,)),
            pltpu.SemaphoreType.DMA((blocks, 3)),
            pltpu.SemaphoreType.DMA((blocks,)),
            pltpu.SemaphoreType.DMA((blocks,)),
        ],
        compiler_params=pltpu.CompilerParams(vmem_limit_bytes=60 << 20),
        cost_estimate=pl.CostEstimate(
            flops=6 * rows * width * width,
            bytes_accessed=6 * width * width + (4 << 20),
            transcendentals=0,
        ),
        name="project",
    )(tile_index, refresh, tokens, modulate, w_qkv, cached)


def own_kernel(live_ref, own_ref, tk_ref, tv_ref, out_ref):
    rows = out_ref.shape[1]
    texts = tk_ref.shape[0]
    half = own_ref.shape[1] - rows
    low = lane_iota((rows, 2 * HEAD)) < HEAD
    live = lane_iota((rows, rows)) < live_ref[0]
    nt = (((1,), (1,)), ((), ()))
    text_keys = tk_ref[...]
    text_values = tv_ref[...]
    for odd in range(2):
        kv = own_ref[odd, :rows, :]
        folded = own_ref[odd, rows:, :].astype(F32)
        query = jnp.concatenate([folded, swap_halves(folded)[: rows - half]], axis=0)
        query = jnp.where(low, query, 0.0)
        text_query = swap_halves(query) if odd else query
        query = query.astype(BF16)
        text_query = text_query.astype(BF16)
        s_own = lax.dot_general(query, kv, nt, preferred_element_type=F32)
        s_own = jnp.where(live, s_own, -BIG)
        s_text = lax.dot_general(text_query, text_keys, nt, preferred_element_type=F32)
        top = jnp.maximum(
            jnp.max(s_own, -1, keepdims=True), jnp.max(s_text, -1, keepdims=True)
        )
        p_own = jnp.exp(s_own - top)
        p_text = jnp.exp(s_text - top)
        total = jnp.sum(p_own, -1, keepdims=True) + jnp.sum(p_text, -1, keepdims=True)
        mixed = jnp.dot(p_own.astype(BF16), kv, preferred_element_type=F32)
        from_text = jnp.dot(p_text.astype(BF16), text_values, preferred_element_type=F32)
        if not odd:
            from_text = swap_halves(from_text)
        mixed = (mixed + from_text) / total
        out_ref[odd] = jnp.where(low, top + jnp.log(total), mixed)


def own_attend(live, own, text_rows):
    heads, packed, _ = own.shape
    rows = packed - 64
    texts, width2 = text_rows.shape
    pairs = heads // 2
    return pl.pallas_call(
        own_kernel,
        grid=(pairs,),
        out_shape=jax.ShapeDtypeStruct((heads, rows, 2 * HEAD), F32),
        in_specs=[
            pl.BlockSpec(memory_space=pltpu.SMEM),
            pl.BlockSpec((2, packed, 2 * HEAD), lambda p: (p, 0, 0)),
            pl.BlockSpec((texts, 2 * HEAD), lambda p: (0, p)),
            pl.BlockSpec((texts, 2 * HEAD), lambda p: (0, p + pairs)),
        ],
        out_specs=pl.BlockSpec((2, rows, 2 * HEAD), lambda p: (p, 0, 0)),
        compiler_params=pltpu.CompilerParams(vmem_limit_bytes=16 << 20),
        cost_estimate=pl.CostEstimate(
            flops=2 * 4 * rows * (rows + texts) * 64 * heads,
            bytes_accessed=6 << 20,
            transcendentals=rows * (rows + texts) * heads,
        ),
        name="own_attend",
    )(live, own, text_rows, text_rows)


def head_kernel(len_ref, pack_ref, out_ref, v_ref, kt_ref, s_ref):
    step = pl.program_id(0)
    tiles, packed, lanes = pack_ref.shape
    rows = packed - HEAD
    total_rows = tiles * rows
    group = out_ref.shape[0]
    block = group * rows
    piece = 256
    chunk = 1920
    low = lane_iota((1, lanes)) < HEAD

    @pl.when(step == 0)
    def _():
        for pair in range(tiles // 2):
            both = jnp.concatenate(
                [pack_ref[2 * pair + t, :rows, :].astype(F32) for t in range(2)], axis=0
            )
            v_ref[pair * 2 * rows : (pair + 1) * 2 * rows, :] = both.astype(BF16)
        feature = row_iota((HEAD, piece))
        for c in range(total_rows // piece):
            part = slice(c * piece, (c + 1) * piece)
            kv = v_ref[part, :]
            index = lane_iota((HEAD, piece)) + c * piece
            own = jnp.logical_and(index >= feature * rows, index < feature * rows + rows)
            held = jnp.logical_or(own, jnp.logical_and(feature == tiles, index >= len_ref[0]))
            kt_ref[:HEAD, part] = jnp.transpose(kv.astype(F32))[:HEAD].astype(BF16)
            kt_ref[HEAD:, part] = jnp.where(held, 1.0, 0.0).astype(BF16)
            v_ref[part, :] = jnp.where(low, jnp.ones((), BF16), kv)

    feature = lane_iota((1, lanes)) - HEAD
    parts = []
    for t in range(group):
        tile = step * group + t
        mask = jnp.where(jnp.logical_or(feature == tile, feature == tiles), -BIG, 0.0)
        folded = pack_ref[tile, rows:, :].astype(F32)
        parts.append(jnp.where(low, folded, mask))
        parts.append(jnp.where(low, swap_halves(folded)[: rows - HEAD], mask))
    query = jnp.concatenate(parts, axis=0).astype(BF16)
    top = jnp.full((block, 128), -jnp.inf, F32)
    for c in range(total_rows // chunk):
        part = slice(c * chunk, (c + 1) * chunk)
        scores = jnp.dot(query, kt_ref[:, part], preferred_element_type=F32)
        s_ref[:, part] = scores
        for i in range(chunk // 128):
            top = jnp.maximum(top, scores[:, i * 128 : (i + 1) * 128])
    top = jnp.max(top, -1, keepdims=True)
    total = jnp.zeros((block, lanes), F32)
    for c in range(total_rows // chunk):
        part = slice(c * chunk, (c + 1) * chunk)
        probs = jnp.exp(s_ref[:, part] - top).astype(BF16)
        total = total + jnp.dot(probs, v_ref[part, :], preferred_element_type=F32)
    weight = total[:, 0:1]
    lse = jnp.broadcast_to(top + jnp.log(weight), (block, lanes))
    result = total / weight
    diagonal = row_iota((HEAD, lanes)) == lane_iota((HEAD, lanes))
    line = row_iota((8, lanes))
    pad = jnp.zeros((2 * HEAD - rows, lanes), F32)
    for t in range(group):
        first = slice(t * rows, t * rows + HEAD)
        rest = slice(t * rows + HEAD, (t + 1) * rows)
        lse_a = jnp.sum(jnp.where(diagonal, lse[first], 0.0), 0, keepdims=True)
        lse_b = jnp.concatenate([lse[rest], pad], axis=0)
        lse_b = jnp.sum(jnp.where(diagonal, lse_b, 0.0), 0, keepdims=True)
        high_a = lse_a.astype(BF16).astype(F32)
        high_b = lse_b.astype(BF16).astype(F32)
        stats = jnp.where(line == 2, lse_a - high_a, lse_b - high_b)
        stats = jnp.where(line == 0, high_a, jnp.where(line == 1, high_b, stats))
        folded = jnp.concatenate([swap_halves(result[rest]), stats], axis=0)
        out_ref[t] = jnp.where(low, folded, result[first]).astype(BF16)


def head_attend(length, pack):
    tiles, packed, lanes = pack.shape
    rows = packed - HEAD
    total_rows = tiles * rows
    group = 8
    block = group * rows
    return pl.pallas_call(
        head_kernel,
        grid=(tiles // group,),
        out_shape=pltpu.HBM((tiles, HEAD, lanes), BF16),
        in_specs=[
            pl.BlockSpec(memory_space=pltpu.SMEM),
            pl.BlockSpec((tiles, packed, lanes), lambda s: (0, 0, 0)),
        ],
        out_specs=pl.BlockSpec((group, HEAD, lanes), lambda s: (s, 0, 0)),
        scratch_shapes=[
            pltpu.VMEM((total_rows, lanes), BF16),
            pltpu.VMEM((lanes, total_rows), BF16),
            pltpu.VMEM((block, total_rows), F32),
        ],
        compiler_params=pltpu.CompilerParams(vmem_limit_bytes=44 << 20),
        cost_estimate=pl.CostEstimate(
            flops=4 * total_rows * total_rows * 128,
            bytes_accessed=4 << 20,
            transcendentals=total_rows * total_rows,
        ),
        name="head_attend",
    )(length, pack)


def join_kernel(far_ref, own_ref, w0, w1, w2, w3, att_ref, w_ref, sems):
    heads, rows, lanes = own_ref.shape
    depth = att_ref.shape[2]
    copies = []
    first = 0
    for i, part in enumerate((w0, w1, w2, w3)):
        last = first + part.shape[0]
        copies.append(pltpu.make_async_copy(part, w_ref.at[first:last], sems.at[i]))
        first = last
    for copy in copies:
        copy.start()
    per = depth // lanes
    low = lane_iota((1, lanes)) < HEAD
    diagonal = row_iota((HEAD, lanes)) == lane_iota((HEAD, lanes))

    def column(line):
        spread = jnp.where(diagonal, jnp.broadcast_to(line, (HEAD, lanes)), 0.0)
        return jnp.sum(spread, -1, keepdims=True)

    for pair in range(heads // 2):
        both = []
        for odd in range(2):
            head = 2 * pair + odd
            folded = far_ref[head + head // 3].astype(F32)
            stats = folded[rows - HEAD :]
            begin = column(stats[0:1] + stats[2:3])
            rest = column(stats[1:2] + stats[3:4])
            far_lse = jnp.concatenate([begin, rest[: rows - HEAD]], axis=0)
            far = jnp.concatenate([folded, swap_halves(folded)[: rows - HEAD]], axis=0)
            own = own_ref[head]
            gap = jnp.broadcast_to(far_lse, (rows, lanes)) - own[:, 0:1]
            share = 1.0 / (1.0 + jnp.exp(-gap))
            other = 1.0 / (1.0 + jnp.exp(gap))
            both.append(share * far + other * own)
        joined = jnp.where(low, swap_halves(both[0]), both[1])
        at = (pair % per) * lanes
        att_ref[pair // per, :, at : at + lanes] = joined.astype(BF16)
    for copy in copies:
        copy.wait()


def join(far, own, w_parts):
    heads, rows, _ = own.shape
    depth, width = w_parts[0].shape
    fetched = sum(part.shape[0] for part in w_parts)
    local = pl.BlockSpec(memory_space=pltpu.VMEM)
    anywhere = pl.BlockSpec(memory_space=pltpu.HBM)
    return pl.pallas_call(
        join_kernel,
        out_shape=(
            jax.ShapeDtypeStruct((width // depth, rows, depth), BF16),
            pltpu.VMEM((fetched, width), BF16),
        ),
        in_specs=[local, local] + [anywhere] * 4,
        out_specs=(local, local),
        scratch_shapes=[pltpu.SemaphoreType.DMA((4,))],
        compiler_params=pltpu.CompilerParams(vmem_limit_bytes=24 << 20),
        cost_estimate=pl.CostEstimate(
            flops=64 * heads * rows * 128, bytes_accessed=8 << 20, transcendentals=heads * rows * 256
        ),
        name="join",
    )(far, own, *w_parts)


def mix_kernel(
    place_ref, att_ref, w_ref, w2_ref, w3_ref, tokens_ref, mod_ref, mixed_ref, input_ref
):
    place = place_ref[0]
    depth = att_ref.shape[2]
    late = w2_ref.shape[0]
    early = depth - late
    near = att_ref[place + 1 - 2 * (place % 2)]
    far = att_ref[(place + 2) % 4]
    far_near = att_ref[3 - place]
    dot = lambda a, b: jnp.dot(a, b, preferred_element_type=F32)
    projected = dot(att_ref[place], w_ref[:depth])
    projected += dot(near, w_ref[depth : 2 * depth])
    projected += dot(far[:, :early], w_ref[2 * depth : 2 * depth + early])
    projected += dot(far_near[:, :early], w_ref[2 * depth + early :])
    projected += dot(far[:, early:], w2_ref[...])
    projected += dot(far_near[:, early:], w3_ref[...])
    mod = mod_ref[...].astype(F32)
    mixed = tokens_ref[...].astype(F32) + mod[2:3] * projected
    mixed_ref[...] = mixed
    input_ref[...] = (layer_norm(mixed) * (1.0 + mod[4:5]) + mod[3:4]).astype(BF16)


def mix(place, attended, w_main, w2_late, w3_late, tokens, modulate):
    local = pl.BlockSpec(memory_space=pltpu.VMEM)
    return pl.pallas_call(
        mix_kernel,
        out_shape=(
            jax.ShapeDtypeStruct(tokens.shape, F32),
            jax.ShapeDtypeStruct(tokens.shape, BF16),
        ),
        in_specs=[pl.BlockSpec(memory_space=pltpu.SMEM)] + [local] * 6,
        out_specs=(local, local),
        compiler_params=pltpu.CompilerParams(vmem_limit_bytes=24 << 20),
        name="mix",
    )(place, attended, w_main, w2_late, w3_late, tokens, modulate)


def feed_blocks(first_ref, second_ref, keep_ref, pass_ref, up_ref, down_ref, ready):
    rows = first_ref.shape[0]
    hidden_width = up_ref.shape[1]
    wide = 512
    both = [first_ref[...].astype(F32), second_ref[...].astype(F32)]
    both = jnp.concatenate(both, axis=0).astype(BF16)
    total = None
    for c in range(hidden_width // wide):
        part = slice(c * wide, (c + 1) * wide)
        ready(2 * c)
        hidden = jnp.dot(both, up_ref[:, part], preferred_element_type=F32)
        hidden = jax.nn.gelu(hidden, approximate=True).astype(BF16)
        ready(2 * c + 1)
        product = jnp.dot(hidden, down_ref[part, :], preferred_element_type=F32)
        total = product if total is None else total + product
    keep_ref[...] = total[:rows]
    pass_ref[...] = total[rows:].astype(BF16)


def feed_near_kernel(first, second, up_hbm, down_hbm, keep, passed, up, down, sems):
    wide = 512
    copies = []
    for c in range(up.shape[1] // wide):
        part = slice(c * wide, (c + 1) * wide)
        copies.append(
            pltpu.make_async_copy(up_hbm.at[:, part], up.at[:, part], sems.at[2 * c])
        )
        copies.append(
            pltpu.make_async_copy(down_hbm.at[part], down.at[part], sems.at[2 * c + 1])
        )
    for copy in copies:
        copy.start()
    feed_blocks(first, second, keep, passed, up, down, lambda i: copies[i].wait())


def feed_far_kernel(first, second, up, down, keep, passed):
    feed_blocks(first, second, keep, passed, up, down, lambda i: None)


def feed_near(first, second, w_up, w_down):
    rows, width = first.shape
    local = pl.BlockSpec(memory_space=pltpu.VMEM)
    anywhere = pl.BlockSpec(memory_space=pltpu.HBM)
    return pl.pallas_call(
        feed_near_kernel,
        out_shape=(
            jax.ShapeDtypeStruct((rows, width), F32),
            jax.ShapeDtypeStruct((rows, width), BF16),
            pltpu.VMEM(w_up.shape, BF16),
            pltpu.VMEM(w_down.shape, BF16),
        ),
        in_specs=[local, local, anywhere, anywhere],
        out_specs=(local,) * 4,
        scratch_shapes=[pltpu.SemaphoreType.DMA((2 * (w_up.shape[1] // 512),))],
        compiler_params=pltpu.CompilerParams(vmem_limit_bytes=32 << 20),
        cost_estimate=pl.CostEstimate(
            flops=8 * rows * w_up.size, bytes_accessed=4 * w_up.size, transcendentals=0
        ),
        name="feed_near",
    )(first, second, w_up, w_down)


def feed_far(first, second, w_up, w_down):
    rows, width = first.shape
    local = pl.BlockSpec(memory_space=pltpu.VMEM)
    return pl.pallas_call(
        feed_far_kernel,
        out_shape=(
            jax.ShapeDtypeStruct((rows, width), F32),
            jax.ShapeDtypeStruct((rows, width), BF16),
        ),
        in_specs=[local] * 4,
        out_specs=(local,) * 2,
        compiler_params=pltpu.CompilerParams(vmem_limit_bytes=24 << 20),
        cost_estimate=pl.CostEstimate(
            flops=8 * rows * w_up.size, bytes_accessed=1 << 20, transcendentals=0
        ),
        name="feed_far",
    )(first, second, w_up, w_down)


def swap(values, axis):
    return lax.ppermute(values, axis, [(0, 1), (1, 0)])


def per_device(
    latents, modulation, kv_cache, text_kv, lengths, refresh, w_qkv, w_out, w_up, w_down
):
    tokens = latents[0]
    rows = tokens.shape[0]
    tile_index = lax.axis_index(TILE).astype(jnp.int32)
    length = lengths[0]
    place = lax.axis_index(REQ).astype(jnp.int32).reshape(1)
    part = w_out.shape[0] * 2 // 3
    send, own = project(
        tile_index.reshape(1), refresh, tokens, modulation[0], w_qkv, kv_cache[0]
    )
    pack = lax.all_to_all(send, TILE, split_axis=0, concat_axis=0, tiled=True)
    live = (length - tile_index * rows).reshape(1)
    own_part = own_attend(live, own, text_kv[0])
    own_part, w_here = lax.optimization_barrier((own_part, w_out))
    w2 = swap(w_here[:part], "zh")
    w2_late = swap(w_here[part:], "zh")
    pack, own_part = lax.optimization_barrier((pack, own_part))
    far = head_attend(lengths, pack)
    far, w2, w_here = lax.optimization_barrier((far, w2, w_here))
    w1 = swap(w_here, "co")
    w3 = swap(w2, "co")
    far = lax.all_to_all(far, TILE, split_axis=0, concat_axis=0, tiled=True)
    far, w1, w3, w2_late = lax.optimization_barrier((far, w1, w3, w2_late))
    w3_late = swap(w2_late, "co")
    attended, w_main = join(far, own_part, (w_out, w1, w2, w3))
    attended, w3_late = lax.optimization_barrier((attended, w3_late))
    mixed, mlp_input = mix(place, attended, w_main, w2_late, w3_late, tokens, modulation[0])

    far_z = swap(mlp_input, "zh")
    near = swap(mlp_input, "co")
    near_keep, near_pass, up, down = feed_near(mlp_input, near, w_up, w_down)
    far_z, near_keep, near_pass = lax.optimization_barrier((far_z, near_keep, near_pass))
    far_both = swap(far_z, "co")
    far_keep, far_pass = feed_far(far_z, far_both, up, down)
    sum_far = (far_keep + swap(far_pass, "co").astype(F32)).astype(BF16)
    near_sum = near_keep + swap(near_pass, "co").astype(F32)
    mlp_out = near_sum + swap(sum_far, "zh").astype(F32)
    positions = tile_index * rows + jnp.arange(rows, dtype=jnp.int32)
    live_rows = positions < length
    gate = modulation[0, 5].astype(F32)
    finished = jnp.where(live_rows[:, None], mixed + gate * mlp_out, 0.0)
    return finished.astype(BF16)[None]


def solution(mesh):
    fine = Mesh(mesh.devices.reshape(2, 2, 4, 2, 4), REQ + TILE)
    return jax.shard_map(
        per_device,
        mesh=fine,
        in_specs=(
            P(REQ, TILE, None),
            P(REQ, None, None),
            P(REQ, TILE, None),
            P(REQ, None, None),
            P(REQ),
            P(REQ, None),
            P(),
            P(REQ, None),
            P(None, REQ),
            P(REQ, None),
        ),
        out_specs=P(REQ, TILE, None),
        check_vma=False,
    )
```

```python
import jax
import jax.numpy as jnp
from jax import lax
from jax.experimental import pallas as pl
from jax.experimental.pallas import tpu as pltpu
from jax.sharding import Mesh
from jax.sharding import PartitionSpec as P

REQ = ("zh", "co")
TILE = ("y", "zl", "x")
HEAD = 64
BIG = 1e30
BLOCKS = ((0, 768), (768, 1152), (1152, 1536))
F32 = jnp.float32
BF16 = jnp.bfloat16


def layer_norm(values):
    average = jnp.mean(values, -1, keepdims=True)
    centred = values - average
    spread = jnp.mean(centred * centred, -1, keepdims=True)
    return centred * lax.rsqrt(spread + 1e-06)


def lane_iota(shape):
    return lax.broadcasted_iota(jnp.int32, shape, len(shape) - 1)


def row_iota(shape):
    return lax.broadcasted_iota(jnp.int32, shape, len(shape) - 2)


def swap_halves(values):
    return pltpu.roll(values, HEAD, axis=1)


def project_kernel(
    tile_ref,
    refresh_ref,
    tokens_ref,
    mod_ref,
    w_ref,
    cache_ref,
    send_ref,
    own_ref,
    picks,
    tokens,
    mod,
    weights,
    cache,
    in_sems,
    w_sems,
):
    rows, width = tokens.shape
    half = HEAD
    inputs = (
        (tokens_ref, tokens),
        (mod_ref, mod),
        (refresh_ref, picks),
        (cache_ref, cache),
    )
    input_copies = [
        pltpu.make_async_copy(src, dst, in_sems.at[i]) for i, (src, dst) in enumerate(inputs)
    ]
    w_copies = [
        [
            pltpu.make_async_copy(
                w_ref.at[:, kind * width + low : kind * width + high],
                weights.at[:, kind * width + low : kind * width + high],
                w_sems.at[b, kind],
            )
            for kind in range(3)
        ]
        for b, (low, high) in enumerate(BLOCKS)
    ]
    for copy in input_copies:
        copy.start()
    for copies in w_copies:
        for copy in copies:
            copy.start()
    low = lane_iota((1, 2 * HEAD)) < HEAD
    pad = jnp.zeros((2 * half - rows, 2 * HEAD), F32)

    def joined(keys, values, odd):
        if odd:
            return jnp.where(low, swap_halves(keys), values).astype(BF16)
        return jnp.where(low, keys, swap_halves(values)).astype(BF16)

    def store(head, at, block):
        dest = head + head // 3
        for copy in range(2 if head % 3 == 2 else 1):
            send_ref[dest + copy, at] = block

    for copy in input_copies:
        copy.wait()
    normed = layer_norm(tokens[...].astype(F32)) * (1.0 + mod[1:2, :].astype(F32))
    normed = (normed + mod[0:1, :].astype(F32)).astype(BF16)
    flagged = picks[0, 0] == tile_ref[0]
    for slot in range(1, picks.shape[1]):
        flagged = jnp.logical_or(flagged, picks[0, slot] == tile_ref[0])
    above, below = slice(0, half), slice(half, half + rows)

    @pl.when(jnp.logical_not(flagged))
    def _():
        for head in range(width // HEAD):
            first = head // 2 * 2 * HEAD
            k_old = cache[:, first : first + 2 * HEAD].astype(F32)
            v_old = cache[:, width + first : width + first + 2 * HEAD].astype(F32)
            store(head, below, joined(k_old, v_old, head % 2))

    for b, (start, end) in enumerate(BLOCKS):
        made = []
        for kind in range(3):
            w_copies[b][kind].wait()
            made.append(
                jnp.dot(
                    normed,
                    weights[:, kind * width + start : kind * width + end],
                    preferred_element_type=F32,
                )
            )
        queries, keys, values = made
        queries = queries * 0.125
        for pair in range((end - start) // (2 * HEAD)):
            cols = slice(pair * 2 * HEAD, (pair + 1) * 2 * HEAD)
            q_top = queries[:half, cols]
            q_end = jnp.concatenate([queries[half:, cols], pad], axis=0)
            for odd in range(2):
                head = start // HEAD + pair * 2 + odd
                q_pack = joined(q_top, q_end, odd)
                own_ref[head, above] = q_pack
                own_ref[head, below] = joined(keys[:, cols], values[:, cols], odd)
                store(head, above, q_pack)
        head, last = start // HEAD, end // HEAD

        @pl.when(flagged)
        def _():
            for h in range(head, last):
                store(h, below, own_ref[h, below])


def project(tile_index, refresh, tokens, modulate, w_qkv, cached):
    rows, width = tokens.shape
    blocks = len(BLOCKS)
    heads = width // HEAD
    dests = heads + heads // 3
    packed = rows + HEAD
    anywhere = pl.BlockSpec(memory_space=pltpu.HBM)
    return pl.pallas_call(
        project_kernel,
        out_shape=(
            jax.ShapeDtypeStruct((dests, packed, 2 * HEAD), BF16),
            jax.ShapeDtypeStruct((heads, packed, 2 * HEAD), BF16),
        ),
        in_specs=[pl.BlockSpec(memory_space=pltpu.SMEM)] + [anywhere] * 5,
        out_specs=(pl.BlockSpec(memory_space=pltpu.VMEM),) * 2,
        scratch_shapes=[
            pltpu.SMEM(refresh.shape, jnp.int32),
            pltpu.VMEM(tokens.shape, BF16),
            pltpu.VMEM(modulate.shape, BF16),
            pltpu.VMEM(w_qkv.shape, BF16),
            pltpu.VMEM(cached.shape, BF16),
            pltpu.SemaphoreType.DMA((4,)),
            pltpu.SemaphoreType.DMA((blocks, 3)),
        ],
        compiler_params=pltpu.CompilerParams(vmem_limit_bytes=36 << 20),
        cost_estimate=pl.CostEstimate(
            flops=6 * rows * width * width,
            bytes_accessed=6 * width * width + (4 << 20),
            transcendentals=0,
        ),
        name="project",
    )(tile_index, refresh, tokens, modulate, w_qkv, cached)


def own_kernel(live_ref, own_ref, tk_ref, tv_ref, out_ref):
    heads, rows, lanes = out_ref.shape
    low = lane_iota((1, lanes)) < HEAD
    live = lane_iota((rows, rows)) < live_ref[0]
    nt = (((1,), (1,)), ((), ()))
    scores = []
    for head in range(heads):
        cols = slice(head // 2 * lanes, (head // 2 + 1) * lanes)
        folded = own_ref[head, :HEAD, :].astype(F32)
        query = jnp.concatenate([folded, swap_halves(folded)[: rows - HEAD]], axis=0)
        query = jnp.where(low, query, 0.0)
        text_query = swap_halves(query) if head % 2 else query
        s_own = lax.dot_general(
            query.astype(BF16), own_ref[head, HEAD:, :], nt, preferred_element_type=F32
        )
        s_text = lax.dot_general(
            text_query.astype(BF16), tk_ref[:, cols], nt, preferred_element_type=F32
        )
        scores.append((jnp.where(live, s_own, -BIG), s_text))
    probs = []
    for s_own, s_text in scores:
        top = jnp.maximum(
            jnp.max(s_own, -1, keepdims=True), jnp.max(s_text, -1, keepdims=True)
        )
        p_own = jnp.exp(s_own - top)
        p_text = jnp.exp(s_text - top)
        total = jnp.sum(p_own, -1, keepdims=True) + jnp.sum(p_text, -1, keepdims=True)
        probs.append((p_own.astype(BF16), p_text.astype(BF16), top, total))
    for head, (p_own, p_text, top, total) in enumerate(probs):
        cols = slice(head // 2 * lanes, (head // 2 + 1) * lanes)
        mixed = jnp.dot(p_own, own_ref[head, HEAD:, :], preferred_element_type=F32)
        from_text = jnp.dot(p_text, tv_ref[:, cols], preferred_element_type=F32)
        if head % 2 == 0:
            from_text = swap_halves(from_text)
        out_ref[head] = jnp.where(low, top + jnp.log(total), (mixed + from_text) / total)


def own_attend(live, own, text_rows):
    heads, packed, lanes = own.shape
    rows = packed - HEAD
    texts = text_rows.shape[0]
    group = 8
    steps = heads // group
    return pl.pallas_call(
        own_kernel,
        grid=(steps,),
        out_shape=jax.ShapeDtypeStruct((heads, rows, lanes), F32),
        in_specs=[
            pl.BlockSpec(memory_space=pltpu.SMEM),
            pl.BlockSpec((group, packed, lanes), lambda p: (p, 0, 0)),
            pl.BlockSpec((texts, group * HEAD), lambda p: (0, p)),
            pl.BlockSpec((texts, group * HEAD), lambda p: (0, p + steps)),
        ],
        out_specs=pl.BlockSpec((group, rows, lanes), lambda p: (p, 0, 0)),
        compiler_params=pltpu.CompilerParams(vmem_limit_bytes=24 << 20),
        cost_estimate=pl.CostEstimate(
            flops=2 * 4 * rows * (rows + texts) * 64 * heads,
            bytes_accessed=6 << 20,
            transcendentals=rows * (rows + texts) * heads,
        ),
        name="own_attend",
    )(live, own, text_rows, text_rows)


def head_kernel(len_ref, pack_ref, out_ref, v_ref, kt_ref, s_ref):
    step = pl.program_id(0)
    tiles, packed, lanes = pack_ref.shape
    rows = packed - HEAD
    total_rows = tiles * rows
    group = out_ref.shape[0]
    block = group * rows
    piece = 256
    chunk = 1920
    low = lane_iota((1, lanes)) < HEAD

    @pl.when(step == 0)
    def _():
        for pair in range(tiles // 2):
            both = jnp.concatenate(
                [pack_ref[2 * pair + t, HEAD:, :].astype(F32) for t in range(2)], axis=0
            )
            v_ref[pair * 2 * rows : (pair + 1) * 2 * rows, :] = both.astype(BF16)
        feature = row_iota((HEAD, piece))
        for c in range(total_rows // piece):
            part = slice(c * piece, (c + 1) * piece)
            kv = v_ref[part, :]
            index = lane_iota((HEAD, piece)) + c * piece
            own = jnp.logical_and(index >= feature * rows, index < feature * rows + rows)
            held = jnp.logical_or(own, jnp.logical_and(feature == tiles, index >= len_ref[0]))
            kt_ref[:HEAD, part] = jnp.transpose(kv.astype(F32))[:HEAD].astype(BF16)
            kt_ref[HEAD:, part] = jnp.where(held, 1.0, 0.0).astype(BF16)
            v_ref[part, :] = jnp.where(low, jnp.ones((), BF16), kv)

    feature = lane_iota((1, lanes)) - HEAD
    parts = []
    for t in range(group):
        tile = step * group + t
        mask = jnp.where(jnp.logical_or(feature == tile, feature == tiles), -BIG, 0.0)
        folded = pack_ref[tile, :HEAD, :].astype(F32)
        parts.append(jnp.where(low, folded, mask))
        parts.append(jnp.where(low, swap_halves(folded)[: rows - HEAD], mask))
    query = jnp.concatenate(parts, axis=0).astype(BF16)
    top = jnp.full((block, 128), -jnp.inf, F32)
    for c in range(total_rows // chunk):
        part = slice(c * chunk, (c + 1) * chunk)
        scores = jnp.dot(query, kt_ref[:, part], preferred_element_type=F32)
        s_ref[:, part] = scores
        for i in range(chunk // 128):
            top = jnp.maximum(top, scores[:, i * 128 : (i + 1) * 128])
    top = jnp.max(top, -1, keepdims=True)
    total = jnp.zeros((block, lanes), F32)
    for c in range(total_rows // chunk):
        part = slice(c * chunk, (c + 1) * chunk)
        probs = jnp.exp(s_ref[:, part] - top).astype(BF16)
        total = total + jnp.dot(probs, v_ref[part, :], preferred_element_type=F32)
    weight = total[:, 0:1]
    lse = jnp.broadcast_to(top + jnp.log(weight), (block, lanes))
    result = total / weight
    diagonal = row_iota((HEAD, lanes)) == lane_iota((HEAD, lanes))
    line = row_iota((8, lanes))
    pad = jnp.zeros((2 * HEAD - rows, lanes), F32)
    for t in range(group):
        first = slice(t * rows, t * rows + HEAD)
        rest = slice(t * rows + HEAD, (t + 1) * rows)
        lse_a = jnp.sum(jnp.where(diagonal, lse[first], 0.0), 0, keepdims=True)
        lse_b = jnp.concatenate([lse[rest], pad], axis=0)
        lse_b = jnp.sum(jnp.where(diagonal, lse_b, 0.0), 0, keepdims=True)
        high_a = lse_a.astype(BF16).astype(F32)
        high_b = lse_b.astype(BF16).astype(F32)
        stats = jnp.where(line == 2, lse_a - high_a, lse_b - high_b)
        stats = jnp.where(line == 0, high_a, jnp.where(line == 1, high_b, stats))
        folded = jnp.concatenate([swap_halves(result[rest]), stats], axis=0)
        out_ref[t] = jnp.where(low, folded, result[first]).astype(BF16)


def head_attend(length, pack):
    tiles, packed, lanes = pack.shape
    rows = packed - HEAD
    total_rows = tiles * rows
    group = 8
    block = group * rows
    return pl.pallas_call(
        head_kernel,
        grid=(tiles // group,),
        out_shape=pltpu.HBM((tiles, HEAD, lanes), BF16),
        in_specs=[
            pl.BlockSpec(memory_space=pltpu.SMEM),
            pl.BlockSpec((tiles, packed, lanes), lambda s: (0, 0, 0)),
        ],
        out_specs=pl.BlockSpec((group, HEAD, lanes), lambda s: (s, 0, 0)),
        scratch_shapes=[
            pltpu.VMEM((total_rows, lanes), BF16),
            pltpu.VMEM((lanes, total_rows), BF16),
            pltpu.VMEM((block, total_rows), F32),
        ],
        compiler_params=pltpu.CompilerParams(vmem_limit_bytes=44 << 20),
        cost_estimate=pl.CostEstimate(
            flops=4 * total_rows * total_rows * 128,
            bytes_accessed=4 << 20,
            transcendentals=total_rows * total_rows,
        ),
        name="head_attend",
    )(length, pack)


def join_kernel(far_ref, own_ref, w0, w1, w2a, w2b, w3a, w3b, att_ref, w_ref, sems):
    heads, rows, lanes = own_ref.shape
    depth = att_ref.shape[2]
    copies = []
    first = 0
    for i, part in enumerate((w0, w1, w2a, w2b, w3a, w3b)):
        last = first + part.shape[0]
        copies.append(pltpu.make_async_copy(part, w_ref.at[first:last], sems.at[i]))
        first = last
    for copy in copies:
        copy.start()
    per = depth // lanes
    low = lane_iota((1, lanes)) < HEAD
    diagonal = row_iota((HEAD, lanes)) == lane_iota((HEAD, lanes))

    def column(line):
        spread = jnp.where(diagonal, jnp.broadcast_to(line, (HEAD, lanes)), 0.0)
        return jnp.sum(spread, -1, keepdims=True)

    for pair in range(heads // 2):
        both = []
        for odd in range(2):
            head = 2 * pair + odd
            folded = far_ref[head + head // 3].astype(F32)
            stats = folded[rows - HEAD :]
            begin = column(stats[0:1] + stats[2:3])
            rest = column(stats[1:2] + stats[3:4])
            far_lse = jnp.concatenate([begin, rest[: rows - HEAD]], axis=0)
            far = jnp.concatenate([folded, swap_halves(folded)[: rows - HEAD]], axis=0)
            own = own_ref[head]
            gap = jnp.broadcast_to(far_lse, (rows, lanes)) - own[:, 0:1]
            share = 1.0 / (1.0 + jnp.exp(-gap))
            other = 1.0 / (1.0 + jnp.exp(gap))
            both.append(share * far + other * own)
        joined = jnp.where(low, swap_halves(both[0]), both[1])
        at = (pair % per) * lanes
        att_ref[pair // per, :, at : at + lanes] = joined.astype(BF16)
    for copy in copies:
        copy.wait()


def join(far, own, w_parts):
    heads, rows, _ = own.shape
    depth, width = w_parts[0].shape
    fetched = sum(part.shape[0] for part in w_parts)
    local = pl.BlockSpec(memory_space=pltpu.VMEM)
    anywhere = pl.BlockSpec(memory_space=pl.ANY)
    return pl.pallas_call(
        join_kernel,
        out_shape=(
            jax.ShapeDtypeStruct((width // depth, rows, depth), BF16),
            pltpu.VMEM((fetched, width), BF16),
        ),
        in_specs=[local, local] + [anywhere] * 6,
        out_specs=(local, local),
        scratch_shapes=[pltpu.SemaphoreType.DMA((6,))],
        compiler_params=pltpu.CompilerParams(vmem_limit_bytes=24 << 20),
        cost_estimate=pl.CostEstimate(
            flops=64 * heads * rows * 128, bytes_accessed=8 << 20, transcendentals=heads * rows * 256
        ),
        name="join",
    )(far, own, *w_parts)


def mix_kernel(
    place_ref, att_ref, w_ref, w2_ref, w3_ref, tokens_ref, mod_ref, mixed_ref, top_ref, end_ref
):
    place = place_ref[0]
    depth = att_ref.shape[2]
    late = w2_ref.shape[0]
    early = depth - late
    far = att_ref[(place + 2) % 4]
    far_near = att_ref[3 - place]
    dot = lambda a, b: jnp.dot(a, b, preferred_element_type=F32)
    projected = dot(att_ref[place], w_ref[:depth])
    projected += dot(att_ref[place + 1 - 2 * (place % 2)], w_ref[depth : 2 * depth])
    projected += dot(far[:, :early], w_ref[2 * depth : 2 * depth + early])
    projected += dot(far_near[:, :early], w_ref[2 * depth + early :])
    projected += dot(far[:, early:], w2_ref[...])
    projected += dot(far_near[:, early:], w3_ref[...])
    mod = mod_ref[...].astype(F32)
    mixed = tokens_ref[...].astype(F32) + mod[2:3] * projected
    mixed_ref[...] = mixed
    normed = layer_norm(mixed) * (1.0 + mod[4:5]) + mod[3:4]
    top_ref[...] = normed[: top_ref.shape[0]].astype(BF16)
    end_ref[...] = normed[top_ref.shape[0] :].astype(BF16)


def mix(place, attended, w_main, w2_late, w3_late, tokens, modulate):
    rows, width = tokens.shape
    local = pl.BlockSpec(memory_space=pltpu.VMEM)
    return pl.pallas_call(
        mix_kernel,
        out_shape=(
            jax.ShapeDtypeStruct((rows, width), F32),
            jax.ShapeDtypeStruct((HEAD, width), BF16),
            jax.ShapeDtypeStruct((rows - HEAD, width), BF16),
        ),
        in_specs=[pl.BlockSpec(memory_space=pltpu.SMEM)] + [local] * 6,
        out_specs=(local,) * 3,
        compiler_params=pltpu.CompilerParams(vmem_limit_bytes=24 << 20),
        name="mix",
    )(place, attended, w_main, w2_late, w3_late, tokens, modulate)


def feed_blocks(pieces, outs, up_ref, down_ref, ready):
    hidden_width = up_ref.shape[1]
    wide = 512
    both = jnp.concatenate([piece[...].astype(F32) for piece in pieces], axis=0).astype(BF16)
    total = None
    for c in range(hidden_width // wide):
        part = slice(c * wide, (c + 1) * wide)
        ready(2 * c)
        hidden = jnp.dot(both, up_ref[:, part], preferred_element_type=F32)
        hidden = jax.nn.gelu(hidden, approximate=True).astype(BF16)
        ready(2 * c + 1)
        product = jnp.dot(hidden, down_ref[part, :], preferred_element_type=F32)
        total = product if total is None else total + product
    first = 0
    for out in outs:
        last = first + out.shape[0]
        out[...] = total[first:last].astype(out.dtype)
        first = last


def feed_near_kernel(a, b, c, d, up_hbm, down_hbm, keep_a, keep_b, pass_a, pass_b, up, down, sems):
    wide = 512
    copies = []
    for i in range(up.shape[1] // wide):
        part = slice(i * wide, (i + 1) * wide)
        copies.append(
            pltpu.make_async_copy(up_hbm.at[:, part], up.at[:, part], sems.at[2 * i])
        )
        copies.append(
            pltpu.make_async_copy(down_hbm.at[part], down.at[part], sems.at[2 * i + 1])
        )
    for copy in copies:
        copy.start()
    outs = (keep_a, keep_b, pass_a, pass_b)
    feed_blocks((a, b, c, d), outs, up, down, lambda i: copies[i].wait())


def feed_far_kernel(a, b, c, d, up, down, keep_a, keep_b, pass_a, pass_b):
    feed_blocks((a, b, c, d), (keep_a, keep_b, pass_a, pass_b), up, down, lambda i: None)


def feed_outs(pieces):
    kinds = (F32, F32, BF16, BF16)
    return tuple(jax.ShapeDtypeStruct(p.shape, k) for p, k in zip(pieces, kinds))


def feed_near(pieces, w_up, w_down):
    rows = sum(piece.shape[0] for piece in pieces)
    local = pl.BlockSpec(memory_space=pltpu.VMEM)
    anywhere = pl.BlockSpec(memory_space=pltpu.HBM)
    return pl.pallas_call(
        feed_near_kernel,
        out_shape=feed_outs(pieces) + (pltpu.VMEM(w_up.shape, BF16), pltpu.VMEM(w_down.shape, BF16)),
        in_specs=[local] * 4 + [anywhere] * 2,
        out_specs=(local,) * 6,
        scratch_shapes=[pltpu.SemaphoreType.DMA((2 * (w_up.shape[1] // 512),))],
        compiler_params=pltpu.CompilerParams(vmem_limit_bytes=32 << 20),
        cost_estimate=pl.CostEstimate(
            flops=4 * rows * w_up.size, bytes_accessed=4 * w_up.size, transcendentals=0
        ),
        name="feed_near",
    )(*pieces, w_up, w_down)


def feed_far(pieces, w_up, w_down):
    rows = sum(piece.shape[0] for piece in pieces)
    local = pl.BlockSpec(memory_space=pltpu.VMEM)
    return pl.pallas_call(
        feed_far_kernel,
        out_shape=feed_outs(pieces),
        in_specs=[local] * 6,
        out_specs=(local,) * 4,
        compiler_params=pltpu.CompilerParams(vmem_limit_bytes=24 << 20),
        cost_estimate=pl.CostEstimate(
            flops=4 * rows * w_up.size, bytes_accessed=1 << 20, transcendentals=0
        ),
        name="feed_far",
    )(*pieces, w_up, w_down)


def final_kernel(
    live_ref, mixed_ref, mod_ref, near_a, near_b, core_a, core_b, far_a, far_b, out_ref
):
    gate = mod_ref[...].astype(F32)[5:6]
    cut = near_a.shape[0]
    for rows, near, core, far in (
        (slice(0, cut), near_a, core_a, far_a),
        (slice(cut, mixed_ref.shape[0]), near_b, core_b, far_b),
    ):
        total = near[...] + core[...].astype(F32) + far[...].astype(F32)
        result = mixed_ref[rows] + gate * total
        position = row_iota(result.shape) + rows.start
        out_ref[rows] = jnp.where(position < live_ref[0], result, 0.0).astype(BF16)


def final(live, mixed, modulate, *pieces):
    local = pl.BlockSpec(memory_space=pltpu.VMEM)
    return pl.pallas_call(
        final_kernel,
        out_shape=jax.ShapeDtypeStruct(mixed.shape, BF16),
        in_specs=[pl.BlockSpec(memory_space=pltpu.SMEM)] + [local] * 8,
        out_specs=local,
        compiler_params=pltpu.CompilerParams(vmem_limit_bytes=16 << 20),
        name="final",
    )(live, mixed, modulate, *pieces)


def swap(values, axis):
    return lax.ppermute(values, axis, [(0, 1), (1, 0)])


def per_device(
    latents, modulation, kv_cache, text_kv, lengths, refresh, w_qkv, w_out, w_up, w_down
):
    tokens = latents[0]
    rows = tokens.shape[0]
    tile_index = lax.axis_index(TILE).astype(jnp.int32)
    length = lengths[0]
    place = lax.axis_index(REQ).astype(jnp.int32).reshape(1)
    send, own = project(
        tile_index.reshape(1), refresh, tokens, modulation[0], w_qkv, kv_cache[0]
    )
    live = (length - tile_index * rows).reshape(1)
    own_part = own_attend(live, own, text_kv[0])
    send, own_part = lax.optimization_barrier((send, own_part))
    pack = lax.all_to_all(send, TILE, split_axis=0, concat_axis=0, tiled=True)
    pack, w_here = lax.optimization_barrier((pack, w_out))
    third = w_out.shape[0] // 3
    w2 = [swap(w_here[i * third : (i + 1) * third], "zh") for i in range(3)]
    w1 = swap(w_here, "co")
    far = head_attend(lengths, pack)
    far, w1, w2a, w2b = lax.optimization_barrier((far, w1, w2[0], w2[1]))
    w3a, w3b = swap(w2a, "co"), swap(w2b, "co")
    far = lax.all_to_all(far, TILE, split_axis=0, concat_axis=0, tiled=True)
    far, w3a, w3b, w2c = lax.optimization_barrier((far, w3a, w3b, w2[2]))
    w3c = swap(w2c, "co")
    attended, w_main = join(far, own_part, (w_out, w1, w2a, w2b, w3a, w3b))
    attended, w3c = lax.optimization_barrier((attended, w3c))
    mixed, *mlp_input = mix(place, attended, w_main, w2c, w3c, tokens, modulation[0])

    far_z = [swap(piece, "zh") for piece in mlp_input]
    near = [swap(piece, "co") for piece in mlp_input]
    *near_parts, up, down = feed_near((*mlp_input, *near), w_up, w_down)
    far_z, near_parts = lax.optimization_barrier((far_z, near_parts))
    far_both = [swap(piece, "co") for piece in far_z]
    far_parts = feed_far((*far_z, *far_both), up, down)
    far_core = [swap(piece, "co") for piece in far_parts[2:]]
    far_sums = [
        (keep + core.astype(F32)).astype(BF16) for keep, core in zip(far_parts[:2], far_core)
    ]
    far_back = [swap(piece, "zh") for piece in far_sums]
    near_core = [swap(piece, "co") for piece in near_parts[2:]]
    out = final(live, mixed, modulation[0], *near_parts[:2], *near_core, *far_back)
    return out[None]


def solution(mesh):
    fine = Mesh(mesh.devices.reshape(2, 2, 4, 2, 4), REQ + TILE)
    return jax.shard_map(
        per_device,
        mesh=fine,
        in_specs=(
            P(REQ, TILE, None),
            P(REQ, None, None),
            P(REQ, TILE, None),
            P(REQ, None, None),
            P(REQ),
            P(REQ, None),
            P(),
            P(REQ, None),
            P(None, REQ),
            P(REQ, None),
        ),
        out_specs=P(REQ, TILE, None),
        check_vma=False,
    )
```

```python
import jax
import jax.numpy as jnp
from jax import lax
from jax.experimental import pallas as pl
from jax.experimental.pallas import tpu as pltpu
from jax.sharding import Mesh
from jax.sharding import PartitionSpec as P

REQ = ("zh", "co")
TILE = ("y", "zl", "x")
HEAD = 64
BIG = 1e30
BLOCKS = ((0, 768), (768, 1152), (1152, 1536))
F32 = jnp.float32
BF16 = jnp.bfloat16


def layer_norm(values):
    average = jnp.mean(values, -1, keepdims=True)
    centred = values - average
    spread = jnp.mean(centred * centred, -1, keepdims=True)
    return centred * lax.rsqrt(spread + 1e-06)


def lane_iota(shape):
    return lax.broadcasted_iota(jnp.int32, shape, len(shape) - 1)


def row_iota(shape):
    return lax.broadcasted_iota(jnp.int32, shape, len(shape) - 2)


def swap_halves(values):
    return pltpu.roll(values, HEAD, axis=1)


def project_kernel(
    tile_ref,
    refresh_ref,
    tokens_ref,
    mod_ref,
    w_ref,
    cache_ref,
    send_ref,
    own_ref,
    picks,
    tokens,
    mod,
    weights,
    cache,
    in_sems,
    w_sems,
):
    rows, width = tokens.shape
    half = HEAD
    inputs = (
        (tokens_ref, tokens),
        (mod_ref, mod),
        (refresh_ref, picks),
        (cache_ref, cache),
    )
    input_copies = [
        pltpu.make_async_copy(src, dst, in_sems.at[i]) for i, (src, dst) in enumerate(inputs)
    ]
    w_copies = [
        [
            pltpu.make_async_copy(
                w_ref.at[:, kind * width + low : kind * width + high],
                weights.at[:, kind * width + low : kind * width + high],
                w_sems.at[b, kind],
            )
            for kind in range(3)
        ]
        for b, (low, high) in enumerate(BLOCKS)
    ]
    for copy in input_copies:
        copy.start()
    for copies in w_copies:
        for copy in copies:
            copy.start()
    low = lane_iota((1, 2 * HEAD)) < HEAD
    pad = jnp.zeros((2 * half - rows, 2 * HEAD), F32)

    def joined(keys, values, odd):
        if odd:
            return jnp.where(low, swap_halves(keys), values).astype(BF16)
        return jnp.where(low, keys, swap_halves(values)).astype(BF16)

    def store(head, at, block):
        dest = head + head // 3
        for copy in range(2 if head % 3 == 2 else 1):
            send_ref[dest + copy, at] = block

    for copy in input_copies:
        copy.wait()
    normed = layer_norm(tokens[...].astype(F32)) * (1.0 + mod[1:2, :].astype(F32))
    normed = (normed + mod[0:1, :].astype(F32)).astype(BF16)
    flagged = picks[0, 0] == tile_ref[0]
    for slot in range(1, picks.shape[1]):
        flagged = jnp.logical_or(flagged, picks[0, slot] == tile_ref[0])
    above, below = slice(0, half), slice(half, half + rows)

    @pl.when(jnp.logical_not(flagged))
    def _():
        for head in range(width // HEAD):
            first = head // 2 * 2 * HEAD
            k_old = cache[:, first : first + 2 * HEAD].astype(F32)
            v_old = cache[:, width + first : width + first + 2 * HEAD].astype(F32)
            store(head, below, joined(k_old, v_old, head % 2))

    for b, (start, end) in enumerate(BLOCKS):
        made = []
        for kind in range(3):
            w_copies[b][kind].wait()
            made.append(
                jnp.dot(
                    normed,
                    weights[:, kind * width + start : kind * width + end],
                    preferred_element_type=F32,
                )
            )
        queries, keys, values = made
        queries = queries * 0.125
        for pair in range((end - start) // (2 * HEAD)):
            cols = slice(pair * 2 * HEAD, (pair + 1) * 2 * HEAD)
            q_top = queries[:half, cols]
            q_end = jnp.concatenate([queries[half:, cols], pad], axis=0)
            for odd in range(2):
                head = start // HEAD + pair * 2 + odd
                q_pack = joined(q_top, q_end, odd)
                own_ref[head, above] = q_pack
                own_ref[head, below] = joined(keys[:, cols], values[:, cols], odd)
                store(head, above, q_pack)
        head, last = start // HEAD, end // HEAD

        @pl.when(flagged)
        def _():
            for h in range(head, last):
                store(h, below, own_ref[h, below])


def project(tile_index, refresh, tokens, modulate, w_qkv, cached):
    rows, width = tokens.shape
    blocks = len(BLOCKS)
    heads = width // HEAD
    dests = heads + heads // 3
    packed = rows + HEAD
    anywhere = pl.BlockSpec(memory_space=pltpu.HBM)
    return pl.pallas_call(
        project_kernel,
        out_shape=(
            jax.ShapeDtypeStruct((dests, packed, 2 * HEAD), BF16),
            jax.ShapeDtypeStruct((heads, packed, 2 * HEAD), BF16),
        ),
        in_specs=[pl.BlockSpec(memory_space=pltpu.SMEM)] + [anywhere] * 5,
        out_specs=(pl.BlockSpec(memory_space=pltpu.VMEM),) * 2,
        scratch_shapes=[
            pltpu.SMEM(refresh.shape, jnp.int32),
            pltpu.VMEM(tokens.shape, BF16),
            pltpu.VMEM(modulate.shape, BF16),
            pltpu.VMEM(w_qkv.shape, BF16),
            pltpu.VMEM(cached.shape, BF16),
            pltpu.SemaphoreType.DMA((4,)),
            pltpu.SemaphoreType.DMA((blocks, 3)),
        ],
        compiler_params=pltpu.CompilerParams(vmem_limit_bytes=60 << 20),
        cost_estimate=pl.CostEstimate(
            flops=6 * rows * width * width,
            bytes_accessed=6 * width * width + (4 << 20),
            transcendentals=0,
        ),
        name="project",
    )(tile_index, refresh, tokens, modulate, w_qkv, cached)


def own_kernel(live_ref, own_ref, tk_ref, tv_ref, out_ref):
    heads, rows, lanes = out_ref.shape
    low = lane_iota((1, lanes)) < HEAD
    live = lane_iota((rows, rows)) < live_ref[0]
    nt = (((1,), (1,)), ((), ()))
    scores = []
    for head in range(heads):
        cols = slice(head // 2 * lanes, (head // 2 + 1) * lanes)
        folded = own_ref[head, :HEAD, :].astype(F32)
        query = jnp.concatenate([folded, swap_halves(folded)[: rows - HEAD]], axis=0)
        query = jnp.where(low, query, 0.0)
        text_query = swap_halves(query) if head % 2 else query
        s_own = lax.dot_general(
            query.astype(BF16), own_ref[head, HEAD:, :], nt, preferred_element_type=F32
        )
        s_text = lax.dot_general(
            text_query.astype(BF16), tk_ref[:, cols], nt, preferred_element_type=F32
        )
        scores.append((jnp.where(live, s_own, -BIG), s_text))
    probs = []
    for s_own, s_text in scores:
        top = jnp.maximum(
            jnp.max(s_own, -1, keepdims=True), jnp.max(s_text, -1, keepdims=True)
        )
        p_own = jnp.exp(s_own - top)
        p_text = jnp.exp(s_text - top)
        total = jnp.sum(p_own, -1, keepdims=True) + jnp.sum(p_text, -1, keepdims=True)
        probs.append((p_own.astype(BF16), p_text.astype(BF16), top, total))
    for head, (p_own, p_text, top, total) in enumerate(probs):
        cols = slice(head // 2 * lanes, (head // 2 + 1) * lanes)
        mixed = jnp.dot(p_own, own_ref[head, HEAD:, :], preferred_element_type=F32)
        from_text = jnp.dot(p_text, tv_ref[:, cols], preferred_element_type=F32)
        if head % 2 == 0:
            from_text = swap_halves(from_text)
        out_ref[head] = jnp.where(low, top + jnp.log(total), (mixed + from_text) / total)


def own_attend(live, own, text_rows):
    heads, packed, lanes = own.shape
    rows = packed - HEAD
    texts = text_rows.shape[0]
    group = 8
    steps = heads // group
    return pl.pallas_call(
        own_kernel,
        grid=(steps,),
        out_shape=jax.ShapeDtypeStruct((heads, rows, lanes), F32),
        in_specs=[
            pl.BlockSpec(memory_space=pltpu.SMEM),
            pl.BlockSpec((group, packed, lanes), lambda p: (p, 0, 0)),
            pl.BlockSpec((texts, group * HEAD), lambda p: (0, p)),
            pl.BlockSpec((texts, group * HEAD), lambda p: (0, p + steps)),
        ],
        out_specs=pl.BlockSpec((group, rows, lanes), lambda p: (p, 0, 0)),
        compiler_params=pltpu.CompilerParams(vmem_limit_bytes=24 << 20),
        cost_estimate=pl.CostEstimate(
            flops=2 * 4 * rows * (rows + texts) * 64 * heads,
            bytes_accessed=6 << 20,
            transcendentals=rows * (rows + texts) * heads,
        ),
        name="own_attend",
    )(live, own, text_rows, text_rows)


def head_kernel(len_ref, pack_ref, out_ref, v_ref, kt_ref, s_ref):
    step = pl.program_id(0)
    tiles, packed, lanes = pack_ref.shape
    rows = packed - HEAD
    total_rows = tiles * rows
    group = out_ref.shape[0]
    block = group * rows
    piece = 256
    chunk = 1920
    low = lane_iota((1, lanes)) < HEAD

    @pl.when(step == 0)
    def _():
        for pair in range(tiles // 2):
            both = jnp.concatenate(
                [pack_ref[2 * pair + t, HEAD:, :].astype(F32) for t in range(2)], axis=0
            )
            v_ref[pair * 2 * rows : (pair + 1) * 2 * rows, :] = both.astype(BF16)
        feature = row_iota((HEAD, piece))
        for c in range(total_rows // piece):
            part = slice(c * piece, (c + 1) * piece)
            kv = v_ref[part, :]
            index = lane_iota((HEAD, piece)) + c * piece
            own = jnp.logical_and(index >= feature * rows, index < feature * rows + rows)
            held = jnp.logical_or(own, jnp.logical_and(feature == tiles, index >= len_ref[0]))
            kt_ref[:HEAD, part] = jnp.transpose(kv.astype(F32))[:HEAD].astype(BF16)
            kt_ref[HEAD:, part] = jnp.where(held, 1.0, 0.0).astype(BF16)
            v_ref[part, :] = jnp.where(low, jnp.ones((), BF16), kv)

    feature = lane_iota((1, lanes)) - HEAD
    parts = []
    for t in range(group):
        tile = step * group + t
        mask = jnp.where(jnp.logical_or(feature == tile, feature == tiles), -BIG, 0.0)
        folded = pack_ref[tile, :HEAD, :].astype(F32)
        parts.append(jnp.where(low, folded, mask))
        parts.append(jnp.where(low, swap_halves(folded)[: rows - HEAD], mask))
    query = jnp.concatenate(parts, axis=0).astype(BF16)
    top = jnp.full((block, 128), -jnp.inf, F32)
    for c in range(total_rows // chunk):
        part = slice(c * chunk, (c + 1) * chunk)
        scores = jnp.dot(query, kt_ref[:, part], preferred_element_type=F32)
        s_ref[:, part] = scores
        for i in range(chunk // 128):
            top = jnp.maximum(top, scores[:, i * 128 : (i + 1) * 128])
    top = jnp.max(top, -1, keepdims=True)
    total = jnp.zeros((block, lanes), F32)
    for c in range(total_rows // chunk):
        part = slice(c * chunk, (c + 1) * chunk)
        probs = jnp.exp(s_ref[:, part] - top).astype(BF16)
        total = total + jnp.dot(probs, v_ref[part, :], preferred_element_type=F32)
    weight = total[:, 0:1]
    lse = jnp.broadcast_to(top + jnp.log(weight), (block, lanes))
    result = total / weight
    diagonal = row_iota((HEAD, lanes)) == lane_iota((HEAD, lanes))
    line = row_iota((8, lanes))
    pad = jnp.zeros((2 * HEAD - rows, lanes), F32)
    for t in range(group):
        first = slice(t * rows, t * rows + HEAD)
        rest = slice(t * rows + HEAD, (t + 1) * rows)
        lse_a = jnp.sum(jnp.where(diagonal, lse[first], 0.0), 0, keepdims=True)
        lse_b = jnp.concatenate([lse[rest], pad], axis=0)
        lse_b = jnp.sum(jnp.where(diagonal, lse_b, 0.0), 0, keepdims=True)
        high_a = lse_a.astype(BF16).astype(F32)
        high_b = lse_b.astype(BF16).astype(F32)
        stats = jnp.where(line == 2, lse_a - high_a, lse_b - high_b)
        stats = jnp.where(line == 0, high_a, jnp.where(line == 1, high_b, stats))
        folded = jnp.concatenate([swap_halves(result[rest]), stats], axis=0)
        out_ref[t] = jnp.where(low, folded, result[first]).astype(BF16)


def head_attend(length, pack):
    tiles, packed, lanes = pack.shape
    rows = packed - HEAD
    total_rows = tiles * rows
    group = 8
    block = group * rows
    return pl.pallas_call(
        head_kernel,
        grid=(tiles // group,),
        out_shape=pltpu.HBM((tiles, HEAD, lanes), BF16),
        in_specs=[
            pl.BlockSpec(memory_space=pltpu.SMEM),
            pl.BlockSpec((tiles, packed, lanes), lambda s: (0, 0, 0)),
        ],
        out_specs=pl.BlockSpec((group, HEAD, lanes), lambda s: (s, 0, 0)),
        scratch_shapes=[
            pltpu.VMEM((total_rows, lanes), BF16),
            pltpu.VMEM((lanes, total_rows), BF16),
            pltpu.VMEM((block, total_rows), F32),
        ],
        compiler_params=pltpu.CompilerParams(vmem_limit_bytes=44 << 20),
        cost_estimate=pl.CostEstimate(
            flops=4 * total_rows * total_rows * 128,
            bytes_accessed=4 << 20,
            transcendentals=total_rows * total_rows,
        ),
        name="head_attend",
    )(length, pack)


def join_kernel(far_ref, own_ref, w0, w1, w2, att_ref, w_ref, sems):
    heads, rows, lanes = own_ref.shape
    depth = att_ref.shape[2]
    copies = []
    first = 0
    for i, part in enumerate((w0, w1, w2)):
        last = first + part.shape[0]
        copies.append(pltpu.make_async_copy(part, w_ref.at[first:last], sems.at[i]))
        first = last
    for copy in copies:
        copy.start()
    per = depth // lanes
    low = lane_iota((1, lanes)) < HEAD
    diagonal = row_iota((HEAD, lanes)) == lane_iota((HEAD, lanes))

    def column(line):
        spread = jnp.where(diagonal, jnp.broadcast_to(line, (HEAD, lanes)), 0.0)
        return jnp.sum(spread, -1, keepdims=True)

    for pair in range(heads // 2):
        both = []
        for odd in range(2):
            head = 2 * pair + odd
            folded = far_ref[head + head // 3].astype(F32)
            stats = folded[rows - HEAD :]
            begin = column(stats[0:1] + stats[2:3])
            rest = column(stats[1:2] + stats[3:4])
            far_lse = jnp.concatenate([begin, rest[: rows - HEAD]], axis=0)
            far = jnp.concatenate([folded, swap_halves(folded)[: rows - HEAD]], axis=0)
            own = own_ref[head]
            gap = jnp.broadcast_to(far_lse, (rows, lanes)) - own[:, 0:1]
            share = 1.0 / (1.0 + jnp.exp(-gap))
            both.append(share * far + (1.0 - share) * own)
        joined = jnp.where(low, swap_halves(both[0]), both[1])
        at = (pair % per) * lanes
        att_ref[pair // per, :, at : at + lanes] = joined.astype(BF16)
    for copy in copies:
        copy.wait()


def join(far, own, w_parts):
    heads, rows, _ = own.shape
    depth, width = w_parts[0].shape
    fetched = sum(part.shape[0] for part in w_parts)
    local = pl.BlockSpec(memory_space=pltpu.VMEM)
    anywhere = pl.BlockSpec(memory_space=pltpu.HBM)
    return pl.pallas_call(
        join_kernel,
        out_shape=(
            jax.ShapeDtypeStruct((width // depth, rows, depth), BF16),
            pltpu.VMEM((fetched, width), BF16),
        ),
        in_specs=[local, local] + [anywhere] * 3,
        out_specs=(local, local),
        scratch_shapes=[pltpu.SemaphoreType.DMA((3,))],
        compiler_params=pltpu.CompilerParams(vmem_limit_bytes=24 << 20),
        cost_estimate=pl.CostEstimate(
            flops=64 * heads * rows * 128, bytes_accessed=8 << 20, transcendentals=heads * rows * 256
        ),
        name="join",
    )(far, own, *w_parts)


def mix_kernel(place_ref, att_ref, w_ref, last_ref, tokens_ref, mod_ref, mixed_ref, input_ref):
    place = place_ref[0]
    depth = att_ref.shape[2]
    owners = (place, place + 1 - 2 * (place % 2), (place + 2) % 4)
    projected = jnp.dot(att_ref[3 - place], last_ref[...], preferred_element_type=F32)
    for i, owner in enumerate(owners):
        part = w_ref[i * depth : (i + 1) * depth]
        projected += jnp.dot(att_ref[owner], part, preferred_element_type=F32)
    mod = mod_ref[...].astype(F32)
    mixed = tokens_ref[...].astype(F32) + mod[2:3] * projected
    mixed_ref[...] = mixed
    input_ref[...] = (layer_norm(mixed) * (1.0 + mod[4:5]) + mod[3:4]).astype(BF16)


def mix(place, attended, w_main, w_last, tokens, modulate):
    local = pl.BlockSpec(memory_space=pltpu.VMEM)
    return pl.pallas_call(
        mix_kernel,
        out_shape=(
            jax.ShapeDtypeStruct(tokens.shape, F32),
            jax.ShapeDtypeStruct(tokens.shape, BF16),
        ),
        in_specs=[pl.BlockSpec(memory_space=pltpu.SMEM)] + [local] * 5,
        out_specs=(local, local),
        compiler_params=pltpu.CompilerParams(vmem_limit_bytes=24 << 20),
        name="mix",
    )(place, attended, w_main, w_last, tokens, modulate)


def feed_blocks(first_ref, second_ref, keep_ref, pass_ref, up_ref, down_ref, ready):
    rows = first_ref.shape[0]
    hidden_width = up_ref.shape[1]
    wide = 512
    both = [first_ref[...].astype(F32), second_ref[...].astype(F32)]
    both = jnp.concatenate(both, axis=0).astype(BF16)
    total = None
    for c in range(hidden_width // wide):
        part = slice(c * wide, (c + 1) * wide)
        ready(2 * c)
        hidden = jnp.dot(both, up_ref[:, part], preferred_element_type=F32)
        hidden = jax.nn.gelu(hidden, approximate=True).astype(BF16)
        ready(2 * c + 1)
        product = jnp.dot(hidden, down_ref[part, :], preferred_element_type=F32)
        total = product if total is None else total + product
    keep_ref[...] = total[:rows]
    pass_ref[...] = total[rows:].astype(BF16)


def feed_near_kernel(first, second, up_hbm, down_hbm, keep, passed, up, down, sems):
    wide = 512
    copies = []
    for c in range(up.shape[1] // wide):
        part = slice(c * wide, (c + 1) * wide)
        copies.append(
            pltpu.make_async_copy(up_hbm.at[:, part], up.at[:, part], sems.at[2 * c])
        )
        copies.append(
            pltpu.make_async_copy(down_hbm.at[part], down.at[part], sems.at[2 * c + 1])
        )
    for copy in copies:
        copy.start()
    feed_blocks(first, second, keep, passed, up, down, lambda i: copies[i].wait())


def feed_far_kernel(first, second, up, down, keep, passed):
    feed_blocks(first, second, keep, passed, up, down, lambda i: None)


def feed_near(first, second, w_up, w_down):
    rows, width = first.shape
    local = pl.BlockSpec(memory_space=pltpu.VMEM)
    anywhere = pl.BlockSpec(memory_space=pltpu.HBM)
    return pl.pallas_call(
        feed_near_kernel,
        out_shape=(
            jax.ShapeDtypeStruct((rows, width), F32),
            jax.ShapeDtypeStruct((rows, width), BF16),
            pltpu.VMEM(w_up.shape, BF16),
            pltpu.VMEM(w_down.shape, BF16),
        ),
        in_specs=[local, local, anywhere, anywhere],
        out_specs=(local,) * 4,
        scratch_shapes=[pltpu.SemaphoreType.DMA((2 * (w_up.shape[1] // 512),))],
        compiler_params=pltpu.CompilerParams(vmem_limit_bytes=32 << 20),
        cost_estimate=pl.CostEstimate(
            flops=8 * rows * w_up.size, bytes_accessed=4 * w_up.size, transcendentals=0
        ),
        name="feed_near",
    )(first, second, w_up, w_down)


def feed_far(first, second, w_up, w_down):
    rows, width = first.shape
    local = pl.BlockSpec(memory_space=pltpu.VMEM)
    return pl.pallas_call(
        feed_far_kernel,
        out_shape=(
            jax.ShapeDtypeStruct((rows, width), F32),
            jax.ShapeDtypeStruct((rows, width), BF16),
        ),
        in_specs=[local] * 4,
        out_specs=(local,) * 2,
        compiler_params=pltpu.CompilerParams(vmem_limit_bytes=24 << 20),
        cost_estimate=pl.CostEstimate(
            flops=8 * rows * w_up.size, bytes_accessed=1 << 20, transcendentals=0
        ),
        name="feed_far",
    )(first, second, w_up, w_down)


def swap(values, axis):
    return lax.ppermute(values, axis, [(0, 1), (1, 0)])


def per_device(
    latents, modulation, kv_cache, text_kv, lengths, refresh, w_qkv, w_out, w_up, w_down
):
    tokens = latents[0]
    rows = tokens.shape[0]
    tile_index = lax.axis_index(TILE).astype(jnp.int32)
    length = lengths[0]
    place = lax.axis_index(REQ).astype(jnp.int32).reshape(1)
    send, own = project(
        tile_index.reshape(1), refresh, tokens, modulation[0], w_qkv, kv_cache[0]
    )
    pack = lax.all_to_all(send, TILE, split_axis=0, concat_axis=0, tiled=True)
    live = (length - tile_index * rows).reshape(1)
    own_part = own_attend(live, own, text_kv[0])
    own_part, w_here = lax.optimization_barrier((own_part, w_out))
    w2 = swap(w_here, "zh")
    pack, own_part = lax.optimization_barrier((pack, own_part))
    far = head_attend(lengths, pack)
    far, w2, w_here = lax.optimization_barrier((far, w2, w_here))
    w1 = swap(w_here, "co")
    w3 = swap(w2, "co")
    far = lax.all_to_all(far, TILE, split_axis=0, concat_axis=0, tiled=True)
    far, w1, w3 = lax.optimization_barrier((far, w1, w3))
    attended, w_main = join(far, own_part, (w_out, w1, w2))
    mixed, mlp_input = mix(place, attended, w_main, w3, tokens, modulation[0])

    far_z = swap(mlp_input, "zh")
    near = swap(mlp_input, "co")
    near_keep, near_pass, up, down = feed_near(mlp_input, near, w_up, w_down)
    far_z, near_keep, near_pass = lax.optimization_barrier((far_z, near_keep, near_pass))
    far_both = swap(far_z, "co")
    far_keep, far_pass = feed_far(far_z, far_both, up, down)
    sum_far = (far_keep + swap(far_pass, "co").astype(F32)).astype(BF16)
    near_sum = near_keep + swap(near_pass, "co").astype(F32)
    mlp_out = near_sum + swap(sum_far, "zh").astype(F32)
    positions = tile_index * rows + jnp.arange(rows, dtype=jnp.int32)
    live_rows = positions < length
    gate = modulation[0, 5].astype(F32)
    finished = jnp.where(live_rows[:, None], mixed + gate * mlp_out, 0.0)
    return finished.astype(BF16)[None]


def solution(mesh):
    fine = Mesh(mesh.devices.reshape(2, 2, 4, 2, 4), REQ + TILE)
    return jax.shard_map(
        per_device,
        mesh=fine,
        in_specs=(
            P(REQ, TILE, None),
            P(REQ, None, None),
            P(REQ, TILE, None),
            P(REQ, None, None),
            P(REQ),
            P(REQ, None),
            P(),
            P(REQ, None),
            P(None, REQ),
            P(REQ, None),
        ),
        out_specs=P(REQ, TILE, None),
        check_vma=False,
    )
```

```python
import jax
import jax.numpy as jnp
from jax import lax
from jax.experimental import pallas as pl
from jax.experimental.pallas import tpu as pltpu
from jax.sharding import Mesh
from jax.sharding import PartitionSpec as P

REQ = ("zh", "co")
TILE = ("y", "zl", "x")
HEAD = 64
BIG = 1e30
BLOCKS = ((0, 512), (512, 1024), (1024, 1536))
AHEAD = 2
F32 = jnp.float32
BF16 = jnp.bfloat16


def layer_norm(values):
    average = jnp.mean(values, -1, keepdims=True)
    centred = values - average
    spread = jnp.mean(centred * centred, -1, keepdims=True)
    return centred * lax.rsqrt(spread + 1e-06)


def lane_iota(shape):
    return lax.broadcasted_iota(jnp.int32, shape, len(shape) - 1)


def row_iota(shape):
    return lax.broadcasted_iota(jnp.int32, shape, len(shape) - 2)


def swap_halves(values):
    return pltpu.roll(values, HEAD, axis=1)


def project_kernel(
    tile_ref,
    refresh_ref,
    tokens_ref,
    mod_ref,
    w_ref,
    cache_ref,
    send_ref,
    own_ref,
    picks,
    tokens,
    mod,
    weights,
    cache,
    in_sems,
    w_sems,
):
    rows, width = tokens.shape
    half = HEAD
    inputs = (
        (tokens_ref, tokens),
        (mod_ref, mod),
        (refresh_ref, picks),
        (cache_ref, cache),
    )
    input_copies = [
        pltpu.make_async_copy(src, dst, in_sems.at[i]) for i, (src, dst) in enumerate(inputs)
    ]
    w_copies = [
        [
            pltpu.make_async_copy(
                w_ref.at[:, kind * width + low : kind * width + high],
                weights.at[:, kind * width + low : kind * width + high],
                w_sems.at[b, kind],
            )
            for kind in range(3)
        ]
        for b, (low, high) in enumerate(BLOCKS)
    ]
    for copy in input_copies:
        copy.start()
    for copies in w_copies[:AHEAD]:
        for copy in copies:
            copy.start()
    low = lane_iota((1, 2 * HEAD)) < HEAD
    pad = jnp.zeros((2 * half - rows, 2 * HEAD), F32)

    def joined(keys, values, odd):
        if odd:
            return jnp.where(low, swap_halves(keys), values).astype(BF16)
        return jnp.where(low, keys, swap_halves(values)).astype(BF16)

    def store(head, at, block):
        dest = head + head // 3
        for copy in range(2 if head % 3 == 2 else 1):
            send_ref[dest + copy, at] = block

    for copy in input_copies:
        copy.wait()
    normed = layer_norm(tokens[...].astype(F32)) * (1.0 + mod[1:2, :].astype(F32))
    normed = (normed + mod[0:1, :].astype(F32)).astype(BF16)
    flagged = picks[0, 0] == tile_ref[0]
    for slot in range(1, picks.shape[1]):
        flagged = jnp.logical_or(flagged, picks[0, slot] == tile_ref[0])
    above, below = slice(0, half), slice(half, half + rows)

    @pl.when(jnp.logical_not(flagged))
    def _():
        for head in range(width // HEAD):
            first = head // 2 * 2 * HEAD
            k_old = cache[:, first : first + 2 * HEAD].astype(F32)
            v_old = cache[:, width + first : width + first + 2 * HEAD].astype(F32)
            store(head, below, joined(k_old, v_old, head % 2))

    def multiply(b):
        start, end = BLOCKS[b]
        for copy in w_copies[b]:
            copy.wait()
        if b + AHEAD < len(BLOCKS):
            for copy in w_copies[b + AHEAD]:
                copy.start()
        return [
            jnp.dot(
                normed,
                weights[:, kind * width + start : kind * width + end],
                preferred_element_type=F32,
            )
            for kind in range(3)
        ]

    def pack(b, queries, keys, values):
        start, end = BLOCKS[b]
        queries = queries * 0.125
        for pair in range((end - start) // (2 * HEAD)):
            cols = slice(pair * 2 * HEAD, (pair + 1) * 2 * HEAD)
            q_top = queries[:half, cols]
            q_end = jnp.concatenate([queries[half:, cols], pad], axis=0)
            for odd in range(2):
                head = start // HEAD + pair * 2 + odd
                q_pack = joined(q_top, q_end, odd)
                own_ref[head, above] = q_pack
                own_ref[head, below] = joined(keys[:, cols], values[:, cols], odd)
                store(head, above, q_pack)

    made = multiply(0)
    for b in range(1, len(BLOCKS)):
        following = multiply(b)
        pack(b - 1, *made)
        made = following
    pack(len(BLOCKS) - 1, *made)

    @pl.when(flagged)
    def _():
        for head in range(width // HEAD):
            store(head, below, own_ref[head, below])


def project(tile_index, refresh, tokens, modulate, w_qkv, cached):
    rows, width = tokens.shape
    blocks = len(BLOCKS)
    heads = width // HEAD
    dests = heads + heads // 3
    packed = rows + HEAD
    anywhere = pl.BlockSpec(memory_space=pltpu.HBM)
    return pl.pallas_call(
        project_kernel,
        out_shape=(
            jax.ShapeDtypeStruct((dests, packed, 2 * HEAD), BF16),
            jax.ShapeDtypeStruct((heads, packed, 2 * HEAD), BF16),
        ),
        in_specs=[pl.BlockSpec(memory_space=pltpu.SMEM)] + [anywhere] * 5,
        out_specs=(pl.BlockSpec(memory_space=pltpu.VMEM),) * 2,
        scratch_shapes=[
            pltpu.SMEM(refresh.shape, jnp.int32),
            pltpu.VMEM(tokens.shape, BF16),
            pltpu.VMEM(modulate.shape, BF16),
            pltpu.VMEM(w_qkv.shape, BF16),
            pltpu.VMEM(cached.shape, BF16),
            pltpu.SemaphoreType.DMA((4,)),
            pltpu.SemaphoreType.DMA((blocks, 3)),
        ],
        compiler_params=pltpu.CompilerParams(vmem_limit_bytes=60 << 20),
        cost_estimate=pl.CostEstimate(
            flops=6 * rows * width * width,
            bytes_accessed=6 * width * width + (4 << 20),
            transcendentals=0,
        ),
        name="project",
    )(tile_index, refresh, tokens, modulate, w_qkv, cached)


def own_kernel(live_ref, own_ref, tk_ref, tv_ref, out_ref):
    heads, rows, lanes = out_ref.shape
    low = lane_iota((1, lanes)) < HEAD
    live = lane_iota((rows, rows)) < live_ref[0]
    nt = (((1,), (1,)), ((), ()))
    scores = []
    for head in range(heads):
        cols = slice(head // 2 * lanes, (head // 2 + 1) * lanes)
        folded = own_ref[head, :HEAD, :].astype(F32)
        query = jnp.concatenate([folded, swap_halves(folded)[: rows - HEAD]], axis=0)
        query = jnp.where(low, query, 0.0)
        text_query = swap_halves(query) if head % 2 else query
        s_own = lax.dot_general(
            query.astype(BF16), own_ref[head, HEAD:, :], nt, preferred_element_type=F32
        )
        s_text = lax.dot_general(
            text_query.astype(BF16), tk_ref[:, cols], nt, preferred_element_type=F32
        )
        scores.append((jnp.where(live, s_own, -BIG), s_text))
    probs = []
    for s_own, s_text in scores:
        top = jnp.maximum(
            jnp.max(s_own, -1, keepdims=True), jnp.max(s_text, -1, keepdims=True)
        )
        p_own = jnp.exp(s_own - top)
        p_text = jnp.exp(s_text - top)
        total = jnp.sum(p_own, -1, keepdims=True) + jnp.sum(p_text, -1, keepdims=True)
        probs.append((p_own.astype(BF16), p_text.astype(BF16), top, total))
    for head, (p_own, p_text, top, total) in enumerate(probs):
        cols = slice(head // 2 * lanes, (head // 2 + 1) * lanes)
        mixed = jnp.dot(p_own, own_ref[head, HEAD:, :], preferred_element_type=F32)
        from_text = jnp.dot(p_text, tv_ref[:, cols], preferred_element_type=F32)
        if head % 2 == 0:
            from_text = swap_halves(from_text)
        out_ref[head] = jnp.where(low, top + jnp.log(total), (mixed + from_text) / total)


def own_attend(live, own, text_rows):
    heads, packed, lanes = own.shape
    rows = packed - HEAD
    texts = text_rows.shape[0]
    group = 8
    steps = heads // group
    return pl.pallas_call(
        own_kernel,
        grid=(steps,),
        out_shape=jax.ShapeDtypeStruct((heads, rows, lanes), F32),
        in_specs=[
            pl.BlockSpec(memory_space=pltpu.SMEM),
            pl.BlockSpec((group, packed, lanes), lambda p: (p, 0, 0)),
            pl.BlockSpec((texts, group * HEAD), lambda p: (0, p)),
            pl.BlockSpec((texts, group * HEAD), lambda p: (0, p + steps)),
        ],
        out_specs=pl.BlockSpec((group, rows, lanes), lambda p: (p, 0, 0)),
        compiler_params=pltpu.CompilerParams(vmem_limit_bytes=14 << 20),
        cost_estimate=pl.CostEstimate(
            flops=2 * 4 * rows * (rows + texts) * 64 * heads,
            bytes_accessed=6 << 20,
            transcendentals=rows * (rows + texts) * heads,
        ),
        name="own_attend",
    )(live, own, text_rows, text_rows)


def head_kernel(len_ref, pack_ref, out_ref, v_ref, kt_ref, s_ref):
    step = pl.program_id(0)
    tiles, packed, lanes = pack_ref.shape
    rows = packed - HEAD
    total_rows = tiles * rows
    group = out_ref.shape[0]
    block = group * rows
    piece = 256
    chunk = 1920
    low = lane_iota((1, lanes)) < HEAD

    @pl.when(step == 0)
    def _():
        for pair in range(tiles // 2):
            both = jnp.concatenate(
                [pack_ref[2 * pair + t, HEAD:, :].astype(F32) for t in range(2)], axis=0
            )
            v_ref[pair * 2 * rows : (pair + 1) * 2 * rows, :] = both.astype(BF16)
        feature = row_iota((HEAD, piece))
        for c in range(total_rows // piece):
            part = slice(c * piece, (c + 1) * piece)
            kv = v_ref[part, :]
            index = lane_iota((HEAD, piece)) + c * piece
            own = jnp.logical_and(index >= feature * rows, index < feature * rows + rows)
            held = jnp.logical_or(own, jnp.logical_and(feature == tiles, index >= len_ref[0]))
            kt_ref[:HEAD, part] = jnp.transpose(kv.astype(F32))[:HEAD].astype(BF16)
            kt_ref[HEAD:, part] = jnp.where(held, 1.0, 0.0).astype(BF16)
            v_ref[part, :] = jnp.where(low, jnp.ones((), BF16), kv)

    feature = lane_iota((1, lanes)) - HEAD
    parts = []
    for t in range(group):
        tile = step * group + t
        mask = jnp.where(jnp.logical_or(feature == tile, feature == tiles), -BIG, 0.0)
        folded = pack_ref[tile, :HEAD, :].astype(F32)
        parts.append(jnp.where(low, folded, mask))
        parts.append(jnp.where(low, swap_halves(folded)[: rows - HEAD], mask))
    query = jnp.concatenate(parts, axis=0).astype(BF16)
    top = jnp.full((block, 128), -jnp.inf, F32)
    for c in range(total_rows // chunk):
        part = slice(c * chunk, (c + 1) * chunk)
        scores = jnp.dot(query, kt_ref[:, part], preferred_element_type=F32)
        s_ref[:, part] = scores
        for i in range(chunk // 128):
            top = jnp.maximum(top, scores[:, i * 128 : (i + 1) * 128])
    top = jnp.max(top, -1, keepdims=True)
    total = jnp.zeros((block, lanes), F32)
    for c in range(total_rows // chunk):
        part = slice(c * chunk, (c + 1) * chunk)
        probs = jnp.exp(s_ref[:, part] - top).astype(BF16)
        total = total + jnp.dot(probs, v_ref[part, :], preferred_element_type=F32)
    weight = total[:, 0:1]
    lse = jnp.broadcast_to(top + jnp.log(weight), (block, lanes))
    result = total / weight
    diagonal = row_iota((HEAD, lanes)) == lane_iota((HEAD, lanes))
    line = row_iota((8, lanes))
    pad = jnp.zeros((2 * HEAD - rows, lanes), F32)
    for t in range(group):
        first = slice(t * rows, t * rows + HEAD)
        rest = slice(t * rows + HEAD, (t + 1) * rows)
        lse_a = jnp.sum(jnp.where(diagonal, lse[first], 0.0), 0, keepdims=True)
        lse_b = jnp.concatenate([lse[rest], pad], axis=0)
        lse_b = jnp.sum(jnp.where(diagonal, lse_b, 0.0), 0, keepdims=True)
        high_a = lse_a.astype(BF16).astype(F32)
        high_b = lse_b.astype(BF16).astype(F32)
        stats = jnp.where(line == 2, lse_a - high_a, lse_b - high_b)
        stats = jnp.where(line == 0, high_a, jnp.where(line == 1, high_b, stats))
        folded = jnp.concatenate([swap_halves(result[rest]), stats], axis=0)
        out_ref[t] = jnp.where(low, folded, result[first]).astype(BF16)


def head_attend(length, pack):
    tiles, packed, lanes = pack.shape
    rows = packed - HEAD
    total_rows = tiles * rows
    group = 8
    block = group * rows
    return pl.pallas_call(
        head_kernel,
        grid=(tiles // group,),
        out_shape=pltpu.HBM((tiles, HEAD, lanes), BF16),
        in_specs=[
            pl.BlockSpec(memory_space=pltpu.SMEM),
            pl.BlockSpec((tiles, packed, lanes), lambda s: (0, 0, 0)),
        ],
        out_specs=pl.BlockSpec((group, HEAD, lanes), lambda s: (s, 0, 0)),
        scratch_shapes=[
            pltpu.VMEM((total_rows, lanes), BF16),
            pltpu.VMEM((lanes, total_rows), BF16),
            pltpu.VMEM((block, total_rows), F32),
        ],
        compiler_params=pltpu.CompilerParams(vmem_limit_bytes=44 << 20),
        cost_estimate=pl.CostEstimate(
            flops=4 * total_rows * total_rows * 128,
            bytes_accessed=4 << 20,
            transcendentals=total_rows * total_rows,
        ),
        name="head_attend",
    )(length, pack)


def join_kernel(far_ref, own_ref, w0, w1, w2, w3, att_ref, w_ref, sems):
    heads, rows, lanes = own_ref.shape
    depth = att_ref.shape[2]
    copies = []
    first = 0
    for i, part in enumerate((w0, w1, w2, w3)):
        last = first + part.shape[0]
        copies.append(pltpu.make_async_copy(part, w_ref.at[first:last], sems.at[i]))
        first = last
    for copy in copies:
        copy.start()
    per = depth // lanes
    low = lane_iota((1, lanes)) < HEAD
    diagonal = row_iota((HEAD, lanes)) == lane_iota((HEAD, lanes))

    def column(line):
        spread = jnp.where(diagonal, jnp.broadcast_to(line, (HEAD, lanes)), 0.0)
        return jnp.sum(spread, -1, keepdims=True)

    for pair in range(heads // 2):
        both = []
        for odd in range(2):
            head = 2 * pair + odd
            folded = far_ref[head + head // 3].astype(F32)
            stats = folded[rows - HEAD :]
            begin = column(stats[0:1] + stats[2:3])
            rest = column(stats[1:2] + stats[3:4])
            far_lse = jnp.concatenate([begin, rest[: rows - HEAD]], axis=0)
            far = jnp.concatenate([folded, swap_halves(folded)[: rows - HEAD]], axis=0)
            own = own_ref[head]
            gap = jnp.broadcast_to(far_lse, (rows, lanes)) - own[:, 0:1]
            share = 1.0 / (1.0 + jnp.exp(-gap))
            both.append(share * far + (1.0 - share) * own)
        joined = jnp.where(low, swap_halves(both[0]), both[1])
        at = (pair % per) * lanes
        att_ref[pair // per, :, at : at + lanes] = joined.astype(BF16)
    for copy in copies:
        copy.wait()


def join(far, own, w_parts):
    heads, rows, _ = own.shape
    depth, width = w_parts[0].shape
    fetched = sum(part.shape[0] for part in w_parts)
    local = pl.BlockSpec(memory_space=pltpu.VMEM)
    anywhere = pl.BlockSpec(memory_space=pltpu.HBM)
    return pl.pallas_call(
        join_kernel,
        out_shape=(
            jax.ShapeDtypeStruct((width // depth, rows, depth), BF16),
            pltpu.VMEM((fetched, width), BF16),
        ),
        in_specs=[local, local] + [anywhere] * 4,
        out_specs=(local, local),
        scratch_shapes=[pltpu.SemaphoreType.DMA((4,))],
        compiler_params=pltpu.CompilerParams(vmem_limit_bytes=24 << 20),
        cost_estimate=pl.CostEstimate(
            flops=64 * heads * rows * 128, bytes_accessed=8 << 20, transcendentals=heads * rows * 256
        ),
        name="join",
    )(far, own, *w_parts)


def mix_kernel(
    place_ref, att_ref, w_ref, w2_ref, w3_ref, tokens_ref, mod_ref, mixed_ref, input_ref
):
    place = place_ref[0]
    depth = att_ref.shape[2]
    late = w2_ref.shape[0]
    early = depth - late
    far = att_ref[(place + 2) % 4]
    far_near = att_ref[3 - place]
    dot = lambda a, b: jnp.dot(a, b, preferred_element_type=F32)
    projected = dot(att_ref[place], w_ref[:depth])
    projected += dot(att_ref[place + 1 - 2 * (place % 2)], w_ref[depth : 2 * depth])
    projected += dot(far[:, :early], w_ref[2 * depth : 2 * depth + early])
    projected += dot(far_near[:, :early], w_ref[2 * depth + early :])
    projected += dot(far[:, early:], w2_ref[...])
    projected += dot(far_near[:, early:], w3_ref[...])
    mod = mod_ref[...].astype(F32)
    mixed = tokens_ref[...].astype(F32) + mod[2:3] * projected
    mixed_ref[...] = mixed
    input_ref[...] = (layer_norm(mixed) * (1.0 + mod[4:5]) + mod[3:4]).astype(BF16)


def mix(place, attended, w_main, w2_late, w3_late, tokens, modulate):
    local = pl.BlockSpec(memory_space=pltpu.VMEM)
    return pl.pallas_call(
        mix_kernel,
        out_shape=(
            jax.ShapeDtypeStruct(tokens.shape, F32),
            jax.ShapeDtypeStruct(tokens.shape, BF16),
        ),
        in_specs=[pl.BlockSpec(memory_space=pltpu.SMEM)] + [local] * 6,
        out_specs=(local, local),
        compiler_params=pltpu.CompilerParams(vmem_limit_bytes=24 << 20),
        name="mix",
    )(place, attended, w_main, w2_late, w3_late, tokens, modulate)


def feed_blocks(first_ref, second_ref, keep_ref, pass_ref, up_ref, down_ref, ready):
    rows = first_ref.shape[0]
    hidden_width = up_ref.shape[1]
    wide = 512
    both = [first_ref[...].astype(F32), second_ref[...].astype(F32)]
    both = jnp.concatenate(both, axis=0).astype(BF16)
    total = None
    for c in range(hidden_width // wide):
        part = slice(c * wide, (c + 1) * wide)
        ready(2 * c)
        hidden = jnp.dot(both, up_ref[:, part], preferred_element_type=F32)
        hidden = jax.nn.gelu(hidden, approximate=True).astype(BF16)
        ready(2 * c + 1)
        product = jnp.dot(hidden, down_ref[part, :], preferred_element_type=F32)
        total = product if total is None else total + product
    keep_ref[...] = total[:rows]
    pass_ref[...] = total[rows:].astype(BF16)


def feed_near_kernel(first, second, up_hbm, down_hbm, keep, passed, up, down, sems):
    wide = 512
    copies = []
    for c in range(up.shape[1] // wide):
        part = slice(c * wide, (c + 1) * wide)
        copies.append(
            pltpu.make_async_copy(up_hbm.at[:, part], up.at[:, part], sems.at[2 * c])
        )
        copies.append(
            pltpu.make_async_copy(down_hbm.at[part], down.at[part], sems.at[2 * c + 1])
        )
    for copy in copies:
        copy.start()
    feed_blocks(first, second, keep, passed, up, down, lambda i: copies[i].wait())


def feed_far_kernel(first, second, up, down, keep, passed):
    feed_blocks(first, second, keep, passed, up, down, lambda i: None)


def feed_near(first, second, w_up, w_down):
    rows, width = first.shape
    local = pl.BlockSpec(memory_space=pltpu.VMEM)
    anywhere = pl.BlockSpec(memory_space=pltpu.HBM)
    return pl.pallas_call(
        feed_near_kernel,
        out_shape=(
            jax.ShapeDtypeStruct((rows, width), F32),
            jax.ShapeDtypeStruct((rows, width), BF16),
            pltpu.VMEM(w_up.shape, BF16),
            pltpu.VMEM(w_down.shape, BF16),
        ),
        in_specs=[local, local, anywhere, anywhere],
        out_specs=(local,) * 4,
        scratch_shapes=[pltpu.SemaphoreType.DMA((2 * (w_up.shape[1] // 512),))],
        compiler_params=pltpu.CompilerParams(vmem_limit_bytes=32 << 20),
        cost_estimate=pl.CostEstimate(
            flops=8 * rows * w_up.size, bytes_accessed=4 * w_up.size, transcendentals=0
        ),
        name="feed_near",
    )(first, second, w_up, w_down)


def feed_far(first, second, w_up, w_down):
    rows, width = first.shape
    local = pl.BlockSpec(memory_space=pltpu.VMEM)
    return pl.pallas_call(
        feed_far_kernel,
        out_shape=(
            jax.ShapeDtypeStruct((rows, width), F32),
            jax.ShapeDtypeStruct((rows, width), BF16),
        ),
        in_specs=[local] * 4,
        out_specs=(local,) * 2,
        compiler_params=pltpu.CompilerParams(vmem_limit_bytes=24 << 20),
        cost_estimate=pl.CostEstimate(
            flops=8 * rows * w_up.size, bytes_accessed=1 << 20, transcendentals=0
        ),
        name="feed_far",
    )(first, second, w_up, w_down)


def swap(values, axis):
    return lax.ppermute(values, axis, [(0, 1), (1, 0)])


def per_device(
    latents, modulation, kv_cache, text_kv, lengths, refresh, w_qkv, w_out, w_up, w_down
):
    tokens = latents[0]
    rows = tokens.shape[0]
    tile_index = lax.axis_index(TILE).astype(jnp.int32)
    length = lengths[0]
    place = lax.axis_index(REQ).astype(jnp.int32).reshape(1)
    send, own = project(
        tile_index.reshape(1), refresh, tokens, modulation[0], w_qkv, kv_cache[0]
    )
    pack = lax.all_to_all(send, TILE, split_axis=0, concat_axis=0, tiled=True)
    live = (length - tile_index * rows).reshape(1)
    own_part = own_attend(live, own, text_kv[0])
    own_part, w_here = lax.optimization_barrier((own_part, w_out))
    early = w_out.shape[0] * 5 // 6
    w2 = swap(w_here[:early], "zh")
    w2_late = swap(w_here[early:], "zh")
    pack, own_part = lax.optimization_barrier((pack, own_part))
    far = head_attend(lengths, pack)
    far, w2, w_here = lax.optimization_barrier((far, w2, w_here))
    w1 = swap(w_here, "co")
    w3 = swap(w2, "co")
    far = lax.all_to_all(far, TILE, split_axis=0, concat_axis=0, tiled=True)
    far, w1, w3, w2_late = lax.optimization_barrier((far, w1, w3, w2_late))
    w3_late = swap(w2_late, "co")
    attended, w_main = join(far, own_part, (w_out, w1, w2, w3))
    attended, w3_late = lax.optimization_barrier((attended, w3_late))
    mixed, mlp_input = mix(place, attended, w_main, w2_late, w3_late, tokens, modulation[0])

    far_z = swap(mlp_input, "zh")
    near = swap(mlp_input, "co")
    near_keep, near_pass, up, down = feed_near(mlp_input, near, w_up, w_down)
    far_z, near_keep, near_pass = lax.optimization_barrier((far_z, near_keep, near_pass))
    far_both = swap(far_z, "co")
    far_keep, far_pass = feed_far(far_z, far_both, up, down)
    sum_far = (far_keep + swap(far_pass, "co").astype(F32)).astype(BF16)
    near_sum = near_keep + swap(near_pass, "co").astype(F32)
    mlp_out = near_sum + swap(sum_far, "zh").astype(F32)
    positions = tile_index * rows + jnp.arange(rows, dtype=jnp.int32)
    live_rows = positions < length
    gate = modulation[0, 5].astype(F32)
    finished = jnp.where(live_rows[:, None], mixed + gate * mlp_out, 0.0)
    return finished.astype(BF16)[None]


def solution(mesh):
    fine = Mesh(mesh.devices.reshape(2, 2, 4, 2, 4), REQ + TILE)
    return jax.shard_map(
        per_device,
        mesh=fine,
        in_specs=(
            P(REQ, TILE, None),
            P(REQ, None, None),
            P(REQ, TILE, None),
            P(REQ, None, None),
            P(REQ),
            P(REQ, None),
            P(),
            P(REQ, None),
            P(None, REQ),
            P(REQ, None),
        ),
        out_specs=P(REQ, TILE, None),
        check_vma=False,
    )
```

```python
import jax
import jax.numpy as jnp
from jax import lax
from jax.experimental import pallas as pl
from jax.experimental.pallas import tpu as pltpu
from jax.sharding import Mesh
from jax.sharding import PartitionSpec as P

REQ = ("zh", "co")
TILE = ("y", "zl", "x")
HEAD = 64
BIG = 1e30
BLOCKS = ((0, 512), (512, 1024), (1024, 1536))
AHEAD = 2
F32 = jnp.float32
BF16 = jnp.bfloat16


def layer_norm(values):
    average = jnp.mean(values, -1, keepdims=True)
    centred = values - average
    spread = jnp.mean(centred * centred, -1, keepdims=True)
    return centred * lax.rsqrt(spread + 1e-06)


def lane_iota(shape):
    return lax.broadcasted_iota(jnp.int32, shape, len(shape) - 1)


def row_iota(shape):
    return lax.broadcasted_iota(jnp.int32, shape, len(shape) - 2)


def swap_halves(values):
    return pltpu.roll(values, HEAD, axis=1)


def project_kernel(
    tile_ref,
    refresh_ref,
    tokens_ref,
    mod_ref,
    w_ref,
    cache_ref,
    send_ref,
    own_ref,
    picks,
    tokens,
    mod,
    weights,
    cache,
    in_sems,
    w_sems,
):
    rows, width = tokens.shape
    half = HEAD
    inputs = (
        (tokens_ref, tokens),
        (mod_ref, mod),
        (refresh_ref, picks),
        (cache_ref, cache),
    )
    input_copies = [
        pltpu.make_async_copy(src, dst, in_sems.at[i]) for i, (src, dst) in enumerate(inputs)
    ]
    w_copies = [
        [
            pltpu.make_async_copy(
                w_ref.at[:, kind * width + low : kind * width + high],
                weights.at[:, kind * width + low : kind * width + high],
                w_sems.at[b, kind],
            )
            for kind in range(3)
        ]
        for b, (low, high) in enumerate(BLOCKS)
    ]
    for copy in input_copies:
        copy.start()
    for copies in w_copies[:AHEAD]:
        for copy in copies:
            copy.start()
    low = lane_iota((1, 2 * HEAD)) < HEAD
    pad = jnp.zeros((2 * half - rows, 2 * HEAD), F32)

    def joined(keys, values, odd):
        if odd:
            return jnp.where(low, swap_halves(keys), values).astype(BF16)
        return jnp.where(low, keys, swap_halves(values)).astype(BF16)

    def store(head, at, block):
        dest = head + head // 3
        for copy in range(2 if head % 3 == 2 else 1):
            send_ref[dest + copy, at] = block

    for copy in input_copies:
        copy.wait()
    normed = layer_norm(tokens[...].astype(F32)) * (1.0 + mod[1:2, :].astype(F32))
    normed = (normed + mod[0:1, :].astype(F32)).astype(BF16)
    flagged = picks[0, 0] == tile_ref[0]
    for slot in range(1, picks.shape[1]):
        flagged = jnp.logical_or(flagged, picks[0, slot] == tile_ref[0])
    above, below = slice(0, half), slice(half, half + rows)

    @pl.when(jnp.logical_not(flagged))
    def _():
        for head in range(width // HEAD):
            first = head // 2 * 2 * HEAD
            k_old = cache[:, first : first + 2 * HEAD].astype(F32)
            v_old = cache[:, width + first : width + first + 2 * HEAD].astype(F32)
            store(head, below, joined(k_old, v_old, head % 2))

    def multiply(b):
        start, end = BLOCKS[b]
        for copy in w_copies[b]:
            copy.wait()
        if b + AHEAD < len(BLOCKS):
            for copy in w_copies[b + AHEAD]:
                copy.start()
        return [
            jnp.dot(
                normed,
                weights[:, kind * width + start : kind * width + end],
                preferred_element_type=F32,
            )
            for kind in range(3)
        ]

    def pack(b, queries, keys, values):
        start, end = BLOCKS[b]
        queries = queries * 0.125
        for pair in range((end - start) // (2 * HEAD)):
            cols = slice(pair * 2 * HEAD, (pair + 1) * 2 * HEAD)
            q_top = queries[:half, cols]
            q_end = jnp.concatenate([queries[half:, cols], pad], axis=0)
            for odd in range(2):
                head = start // HEAD + pair * 2 + odd
                q_pack = joined(q_top, q_end, odd)
                own_ref[head, above] = q_pack
                own_ref[head, below] = joined(keys[:, cols], values[:, cols], odd)
                store(head, above, q_pack)

    made = multiply(0)
    for b in range(1, len(BLOCKS)):
        following = multiply(b)
        pack(b - 1, *made)
        made = following
    pack(len(BLOCKS) - 1, *made)

    @pl.when(flagged)
    def _():
        for head in range(width // HEAD):
            store(head, below, own_ref[head, below])


def project(tile_index, refresh, tokens, modulate, w_qkv, cached):
    rows, width = tokens.shape
    blocks = len(BLOCKS)
    heads = width // HEAD
    dests = heads + heads // 3
    packed = rows + HEAD
    anywhere = pl.BlockSpec(memory_space=pltpu.HBM)
    return pl.pallas_call(
        project_kernel,
        out_shape=(
            jax.ShapeDtypeStruct((dests, packed, 2 * HEAD), BF16),
            jax.ShapeDtypeStruct((heads, packed, 2 * HEAD), BF16),
        ),
        in_specs=[pl.BlockSpec(memory_space=pltpu.SMEM)] + [anywhere] * 5,
        out_specs=(pl.BlockSpec(memory_space=pltpu.VMEM),) * 2,
        scratch_shapes=[
            pltpu.SMEM(refresh.shape, jnp.int32),
            pltpu.VMEM(tokens.shape, BF16),
            pltpu.VMEM(modulate.shape, BF16),
            pltpu.VMEM(w_qkv.shape, BF16),
            pltpu.VMEM(cached.shape, BF16),
            pltpu.SemaphoreType.DMA((4,)),
            pltpu.SemaphoreType.DMA((blocks, 3)),
        ],
        compiler_params=pltpu.CompilerParams(vmem_limit_bytes=60 << 20),
        cost_estimate=pl.CostEstimate(
            flops=6 * rows * width * width,
            bytes_accessed=6 * width * width + (4 << 20),
            transcendentals=0,
        ),
        name="project",
    )(tile_index, refresh, tokens, modulate, w_qkv, cached)


def own_kernel(live_ref, own_ref, tk_ref, tv_ref, out_ref):
    heads, rows, lanes = out_ref.shape
    low = lane_iota((1, lanes)) < HEAD
    live = lane_iota((rows, rows)) < live_ref[0]
    nt = (((1,), (1,)), ((), ()))
    scores = []
    for head in range(heads):
        cols = slice(head // 2 * lanes, (head // 2 + 1) * lanes)
        folded = own_ref[head, :HEAD, :].astype(F32)
        query = jnp.concatenate([folded, swap_halves(folded)[: rows - HEAD]], axis=0)
        query = jnp.where(low, query, 0.0)
        text_query = swap_halves(query) if head % 2 else query
        s_own = lax.dot_general(
            query.astype(BF16), own_ref[head, HEAD:, :], nt, preferred_element_type=F32
        )
        s_text = lax.dot_general(
            text_query.astype(BF16), tk_ref[:, cols], nt, preferred_element_type=F32
        )
        scores.append((jnp.where(live, s_own, -BIG), s_text))
    probs = []
    for s_own, s_text in scores:
        top = jnp.maximum(
            jnp.max(s_own, -1, keepdims=True), jnp.max(s_text, -1, keepdims=True)
        )
        p_own = jnp.exp(s_own - top)
        p_text = jnp.exp(s_text - top)
        total = jnp.sum(p_own, -1, keepdims=True) + jnp.sum(p_text, -1, keepdims=True)
        probs.append((p_own.astype(BF16), p_text.astype(BF16), top, total))
    for head, (p_own, p_text, top, total) in enumerate(probs):
        cols = slice(head // 2 * lanes, (head // 2 + 1) * lanes)
        mixed = jnp.dot(p_own, own_ref[head, HEAD:, :], preferred_element_type=F32)
        from_text = jnp.dot(p_text, tv_ref[:, cols], preferred_element_type=F32)
        if head % 2 == 0:
            from_text = swap_halves(from_text)
        out_ref[head] = jnp.where(low, top + jnp.log(total), (mixed + from_text) / total)


def own_attend(live, own, text_rows):
    heads, packed, lanes = own.shape
    rows = packed - HEAD
    texts = text_rows.shape[0]
    group = 8
    steps = heads // group
    return pl.pallas_call(
        own_kernel,
        grid=(steps,),
        out_shape=jax.ShapeDtypeStruct((heads, rows, lanes), F32),
        in_specs=[
            pl.BlockSpec(memory_space=pltpu.SMEM),
            pl.BlockSpec((group, packed, lanes), lambda p: (p, 0, 0)),
            pl.BlockSpec((texts, group * HEAD), lambda p: (0, p)),
            pl.BlockSpec((texts, group * HEAD), lambda p: (0, p + steps)),
        ],
        out_specs=pl.BlockSpec((group, rows, lanes), lambda p: (p, 0, 0)),
        compiler_params=pltpu.CompilerParams(vmem_limit_bytes=14 << 20),
        cost_estimate=pl.CostEstimate(
            flops=2 * 4 * rows * (rows + texts) * 64 * heads,
            bytes_accessed=6 << 20,
            transcendentals=rows * (rows + texts) * heads,
        ),
        name="own_attend",
    )(live, own, text_rows, text_rows)


def head_kernel(len_ref, pack_ref, out_ref, v_ref, kt_ref, s_ref):
    step = pl.program_id(0)
    tiles, packed, lanes = pack_ref.shape
    rows = packed - HEAD
    total_rows = tiles * rows
    group = out_ref.shape[0]
    block = group * rows
    piece = 256
    chunk = 1920
    low = lane_iota((1, lanes)) < HEAD

    @pl.when(step == 0)
    def _():
        for pair in range(tiles // 2):
            both = jnp.concatenate(
                [pack_ref[2 * pair + t, HEAD:, :].astype(F32) for t in range(2)], axis=0
            )
            v_ref[pair * 2 * rows : (pair + 1) * 2 * rows, :] = both.astype(BF16)
        feature = row_iota((HEAD, piece))
        for c in range(total_rows // piece):
            part = slice(c * piece, (c + 1) * piece)
            kv = v_ref[part, :]
            index = lane_iota((HEAD, piece)) + c * piece
            own = jnp.logical_and(index >= feature * rows, index < feature * rows + rows)
            held = jnp.logical_or(own, jnp.logical_and(feature == tiles, index >= len_ref[0]))
            kt_ref[:HEAD, part] = jnp.transpose(kv.astype(F32))[:HEAD].astype(BF16)
            kt_ref[HEAD:, part] = jnp.where(held, 1.0, 0.0).astype(BF16)
            v_ref[part, :] = jnp.where(low, jnp.ones((), BF16), kv)

    feature = lane_iota((1, lanes)) - HEAD
    parts = []
    for t in range(group):
        tile = step * group + t
        mask = jnp.where(jnp.logical_or(feature == tile, feature == tiles), -BIG, 0.0)
        folded = pack_ref[tile, :HEAD, :].astype(F32)
        parts.append(jnp.where(low, folded, mask))
        parts.append(jnp.where(low, swap_halves(folded)[: rows - HEAD], mask))
    query = jnp.concatenate(parts, axis=0).astype(BF16)
    top = jnp.full((block, 128), -jnp.inf, F32)
    for c in range(total_rows // chunk):
        part = slice(c * chunk, (c + 1) * chunk)
        scores = jnp.dot(query, kt_ref[:, part], preferred_element_type=F32)
        s_ref[:, part] = scores
        for i in range(chunk // 128):
            top = jnp.maximum(top, scores[:, i * 128 : (i + 1) * 128])
    top = jnp.max(top, -1, keepdims=True)
    total = jnp.zeros((block, lanes), F32)
    for c in range(total_rows // chunk):
        part = slice(c * chunk, (c + 1) * chunk)
        probs = jnp.exp(s_ref[:, part] - top).astype(BF16)
        total = total + jnp.dot(probs, v_ref[part, :], preferred_element_type=F32)
    weight = total[:, 0:1]
    lse = jnp.broadcast_to(top + jnp.log(weight), (block, lanes))
    result = total / weight
    diagonal = row_iota((HEAD, lanes)) == lane_iota((HEAD, lanes))
    line = row_iota((8, lanes))
    pad = jnp.zeros((2 * HEAD - rows, lanes), F32)
    for t in range(group):
        first = slice(t * rows, t * rows + HEAD)
        rest = slice(t * rows + HEAD, (t + 1) * rows)
        lse_a = jnp.sum(jnp.where(diagonal, lse[first], 0.0), 0, keepdims=True)
        lse_b = jnp.concatenate([lse[rest], pad], axis=0)
        lse_b = jnp.sum(jnp.where(diagonal, lse_b, 0.0), 0, keepdims=True)
        high_a = lse_a.astype(BF16).astype(F32)
        high_b = lse_b.astype(BF16).astype(F32)
        stats = jnp.where(line == 2, lse_a - high_a, lse_b - high_b)
        stats = jnp.where(line == 0, high_a, jnp.where(line == 1, high_b, stats))
        folded = jnp.concatenate([swap_halves(result[rest]), stats], axis=0)
        out_ref[t] = jnp.where(low, folded, result[first]).astype(BF16)


def head_attend(length, pack):
    tiles, packed, lanes = pack.shape
    rows = packed - HEAD
    total_rows = tiles * rows
    group = 8
    block = group * rows
    return pl.pallas_call(
        head_kernel,
        grid=(tiles // group,),
        out_shape=pltpu.HBM((tiles, HEAD, lanes), BF16),
        in_specs=[
            pl.BlockSpec(memory_space=pltpu.SMEM),
            pl.BlockSpec((tiles, packed, lanes), lambda s: (0, 0, 0)),
        ],
        out_specs=pl.BlockSpec((group, HEAD, lanes), lambda s: (s, 0, 0)),
        scratch_shapes=[
            pltpu.VMEM((total_rows, lanes), BF16),
            pltpu.VMEM((lanes, total_rows), BF16),
            pltpu.VMEM((block, total_rows), F32),
        ],
        compiler_params=pltpu.CompilerParams(vmem_limit_bytes=44 << 20),
        cost_estimate=pl.CostEstimate(
            flops=4 * total_rows * total_rows * 128,
            bytes_accessed=4 << 20,
            transcendentals=total_rows * total_rows,
        ),
        name="head_attend",
    )(length, pack)


def join_kernel(far_ref, own_ref, w0, w1, w2a, w2b, w3a, w3b, att_ref, w_ref, sems):
    heads, rows, lanes = own_ref.shape
    depth = att_ref.shape[2]
    copies = []
    first = 0
    for i, part in enumerate((w0, w1, w2a, w2b, w3a, w3b)):
        last = first + part.shape[0]
        copies.append(pltpu.make_async_copy(part, w_ref.at[first:last], sems.at[i]))
        first = last
    for copy in copies:
        copy.start()
    per = depth // lanes
    low = lane_iota((1, lanes)) < HEAD
    diagonal = row_iota((HEAD, lanes)) == lane_iota((HEAD, lanes))

    def column(line):
        spread = jnp.where(diagonal, jnp.broadcast_to(line, (HEAD, lanes)), 0.0)
        return jnp.sum(spread, -1, keepdims=True)

    for pair in range(heads // 2):
        both = []
        for odd in range(2):
            head = 2 * pair + odd
            folded = far_ref[head + head // 3].astype(F32)
            stats = folded[rows - HEAD :]
            begin = column(stats[0:1] + stats[2:3])
            rest = column(stats[1:2] + stats[3:4])
            far_lse = jnp.concatenate([begin, rest[: rows - HEAD]], axis=0)
            far = jnp.concatenate([folded, swap_halves(folded)[: rows - HEAD]], axis=0)
            own = own_ref[head]
            gap = jnp.broadcast_to(far_lse, (rows, lanes)) - own[:, 0:1]
            share = 1.0 / (1.0 + jnp.exp(-gap))
            both.append(share * far + (1.0 - share) * own)
        joined = jnp.where(low, swap_halves(both[0]), both[1])
        at = (pair % per) * lanes
        att_ref[pair // per, :, at : at + lanes] = joined.astype(BF16)
    for copy in copies:
        copy.wait()


def join(far, own, w_parts):
    heads, rows, _ = own.shape
    depth, width = w_parts[0].shape
    fetched = sum(part.shape[0] for part in w_parts)
    local = pl.BlockSpec(memory_space=pltpu.VMEM)
    anywhere = pl.BlockSpec(memory_space=pltpu.HBM)
    return pl.pallas_call(
        join_kernel,
        out_shape=(
            jax.ShapeDtypeStruct((width // depth, rows, depth), BF16),
            pltpu.VMEM((fetched, width), BF16),
        ),
        in_specs=[local, local] + [anywhere] * 6,
        out_specs=(local, local),
        scratch_shapes=[pltpu.SemaphoreType.DMA((6,))],
        compiler_params=pltpu.CompilerParams(vmem_limit_bytes=24 << 20),
        cost_estimate=pl.CostEstimate(
            flops=64 * heads * rows * 128, bytes_accessed=8 << 20, transcendentals=heads * rows * 256
        ),
        name="join",
    )(far, own, *w_parts)


def mix_kernel(place_ref, att_ref, w_ref, tokens_ref, mod_ref, mixed_ref, input_ref):
    place = place_ref[0]
    depth = att_ref.shape[2]
    projected = jnp.zeros(mixed_ref.shape, F32)
    owners = (place, place + 1 - 2 * (place % 2), (place + 2) % 4, 3 - place)
    for i, owner in enumerate(owners):
        part = w_ref[i * depth : (i + 1) * depth]
        projected += jnp.dot(att_ref[owner], part, preferred_element_type=F32)
    mod = mod_ref[...].astype(F32)
    mixed = tokens_ref[...].astype(F32) + mod[2:3] * projected
    mixed_ref[...] = mixed
    input_ref[...] = (layer_norm(mixed) * (1.0 + mod[4:5]) + mod[3:4]).astype(BF16)


def mix(place, attended, w_main, tokens, modulate):
    local = pl.BlockSpec(memory_space=pltpu.VMEM)
    return pl.pallas_call(
        mix_kernel,
        out_shape=(
            jax.ShapeDtypeStruct(tokens.shape, F32),
            jax.ShapeDtypeStruct(tokens.shape, BF16),
        ),
        in_specs=[pl.BlockSpec(memory_space=pltpu.SMEM)] + [local] * 4,
        out_specs=(local, local),
        compiler_params=pltpu.CompilerParams(vmem_limit_bytes=24 << 20),
        name="mix",
    )(place, attended, w_main, tokens, modulate)


def feed_blocks(first_ref, second_ref, keep_ref, pass_ref, up_ref, down_ref, ready):
    rows = first_ref.shape[0]
    hidden_width = up_ref.shape[1]
    wide = 512
    both = [first_ref[...].astype(F32), second_ref[...].astype(F32)]
    both = jnp.concatenate(both, axis=0).astype(BF16)
    total = None
    for c in range(hidden_width // wide):
        part = slice(c * wide, (c + 1) * wide)
        ready(2 * c)
        hidden = jnp.dot(both, up_ref[:, part], preferred_element_type=F32)
        hidden = jax.nn.gelu(hidden, approximate=True).astype(BF16)
        ready(2 * c + 1)
        product = jnp.dot(hidden, down_ref[part, :], preferred_element_type=F32)
        total = product if total is None else total + product
    keep_ref[...] = total[:rows]
    pass_ref[...] = total[rows:].astype(BF16)


def feed_near_kernel(first, second, up_hbm, down_hbm, keep, passed, up, down, sems):
    wide = 512
    copies = []
    for c in range(up.shape[1] // wide):
        part = slice(c * wide, (c + 1) * wide)
        copies.append(
            pltpu.make_async_copy(up_hbm.at[:, part], up.at[:, part], sems.at[2 * c])
        )
        copies.append(
            pltpu.make_async_copy(down_hbm.at[part], down.at[part], sems.at[2 * c + 1])
        )
    for copy in copies:
        copy.start()
    feed_blocks(first, second, keep, passed, up, down, lambda i: copies[i].wait())


def feed_far_kernel(first, second, up, down, keep, passed):
    feed_blocks(first, second, keep, passed, up, down, lambda i: None)


def feed_near(first, second, w_up, w_down):
    rows, width = first.shape
    local = pl.BlockSpec(memory_space=pltpu.VMEM)
    anywhere = pl.BlockSpec(memory_space=pltpu.HBM)
    return pl.pallas_call(
        feed_near_kernel,
        out_shape=(
            jax.ShapeDtypeStruct((rows, width), F32),
            jax.ShapeDtypeStruct((rows, width), BF16),
            pltpu.VMEM(w_up.shape, BF16),
            pltpu.VMEM(w_down.shape, BF16),
        ),
        in_specs=[local, local, anywhere, anywhere],
        out_specs=(local,) * 4,
        scratch_shapes=[pltpu.SemaphoreType.DMA((2 * (w_up.shape[1] // 512),))],
        compiler_params=pltpu.CompilerParams(vmem_limit_bytes=32 << 20),
        cost_estimate=pl.CostEstimate(
            flops=8 * rows * w_up.size, bytes_accessed=4 * w_up.size, transcendentals=0
        ),
        name="feed_near",
    )(first, second, w_up, w_down)


def feed_far(first, second, w_up, w_down):
    rows, width = first.shape
    local = pl.BlockSpec(memory_space=pltpu.VMEM)
    return pl.pallas_call(
        feed_far_kernel,
        out_shape=(
            jax.ShapeDtypeStruct((rows, width), F32),
            jax.ShapeDtypeStruct((rows, width), BF16),
        ),
        in_specs=[local] * 4,
        out_specs=(local,) * 2,
        compiler_params=pltpu.CompilerParams(vmem_limit_bytes=24 << 20),
        cost_estimate=pl.CostEstimate(
            flops=8 * rows * w_up.size, bytes_accessed=1 << 20, transcendentals=0
        ),
        name="feed_far",
    )(first, second, w_up, w_down)


def swap(values, axis):
    return lax.ppermute(values, axis, [(0, 1), (1, 0)])


def per_device(
    latents, modulation, kv_cache, text_kv, lengths, refresh, w_qkv, w_out, w_up, w_down
):
    tokens = latents[0]
    rows = tokens.shape[0]
    tile_index = lax.axis_index(TILE).astype(jnp.int32)
    length = lengths[0]
    place = lax.axis_index(REQ).astype(jnp.int32).reshape(1)
    w2_first = swap(w_out[: w_out.shape[0] // 6], "zh")
    send, own = project(
        tile_index.reshape(1), refresh, tokens, modulation[0], w_qkv, kv_cache[0]
    )
    send, own, w2_first = lax.optimization_barrier((send, own, w2_first))
    pack = lax.all_to_all(send, TILE, split_axis=0, concat_axis=0, tiled=True)
    live = (length - tile_index * rows).reshape(1)
    own_part = own_attend(live, own, text_kv[0])
    own_part, w_here = lax.optimization_barrier((own_part, w_out))
    early = w_out.shape[0] // 6
    w1 = swap(w_here, "co")
    w2 = swap(w_here[early:], "zh")
    pack, own_part = lax.optimization_barrier((pack, own_part))
    far = head_attend(lengths, pack)
    far, w1, w2 = lax.optimization_barrier((far, w1, w2))
    w3 = swap(w2, "co")
    w3_first = swap(w2_first, "co")
    far = lax.all_to_all(far, TILE, split_axis=0, concat_axis=0, tiled=True)
    far, w3, w3_first = lax.optimization_barrier((far, w3, w3_first))
    attended, w_main = join(far, own_part, (w_out, w1, w2_first, w2, w3_first, w3))
    mixed, mlp_input = mix(place, attended, w_main, tokens, modulation[0])

    far_z = swap(mlp_input, "zh")
    near = swap(mlp_input, "co")
    near_keep, near_pass, up, down = feed_near(mlp_input, near, w_up, w_down)
    far_z, near_keep, near_pass = lax.optimization_barrier((far_z, near_keep, near_pass))
    far_both = swap(far_z, "co")
    far_keep, far_pass = feed_far(far_z, far_both, up, down)
    sum_far = (far_keep + swap(far_pass, "co").astype(F32)).astype(BF16)
    near_sum = near_keep + swap(near_pass, "co").astype(F32)
    mlp_out = near_sum + swap(sum_far, "zh").astype(F32)
    positions = tile_index * rows + jnp.arange(rows, dtype=jnp.int32)
    live_rows = positions < length
    gate = modulation[0, 5].astype(F32)
    finished = jnp.where(live_rows[:, None], mixed + gate * mlp_out, 0.0)
    return finished.astype(BF16)[None]


def solution(mesh):
    fine = Mesh(mesh.devices.reshape(2, 2, 4, 2, 4), REQ + TILE)
    return jax.shard_map(
        per_device,
        mesh=fine,
        in_specs=(
            P(REQ, TILE, None),
            P(REQ, None, None),
            P(REQ, TILE, None),
            P(REQ, None, None),
            P(REQ),
            P(REQ, None),
            P(),
            P(REQ, None),
            P(None, REQ),
            P(REQ, None),
        ),
        out_specs=P(REQ, TILE, None),
        check_vma=False,
    )
```

```python
import functools

import jax
import jax.numpy as jnp
from jax import lax
from jax.experimental import pallas as pl
from jax.experimental.pallas import tpu as pltpu
from jax.sharding import Mesh
from jax.sharding import PartitionSpec as P

REQ = ("zh", "co")
TILE = ("y", "zl", "x")
HEAD = 64
BIG = 1e30
BLOCKS = ((0, 512), (512, 1024), (1024, 1536))
AHEAD = 2
F32 = jnp.float32
BF16 = jnp.bfloat16


def layer_norm(values):
    average = jnp.mean(values, -1, keepdims=True)
    centred = values - average
    spread = jnp.mean(centred * centred, -1, keepdims=True)
    return centred * lax.rsqrt(spread + 1e-06)


def lane_iota(shape):
    return lax.broadcasted_iota(jnp.int32, shape, len(shape) - 1)


def row_iota(shape):
    return lax.broadcasted_iota(jnp.int32, shape, len(shape) - 2)


def swap_halves(values):
    return pltpu.roll(values, HEAD, axis=1)


def project_kernel(
    tile_ref,
    refresh_ref,
    tokens_ref,
    mod_ref,
    w_ref,
    cache_ref,
    send_ref,
    own_ref,
    picks,
    tokens,
    mod,
    weights,
    cache,
    in_sems,
    w_sems,
):
    rows, width = tokens.shape
    half = HEAD
    inputs = (
        (tokens_ref, tokens),
        (mod_ref, mod),
        (refresh_ref, picks),
        (cache_ref, cache),
    )
    input_copies = [
        pltpu.make_async_copy(src, dst, in_sems.at[i]) for i, (src, dst) in enumerate(inputs)
    ]
    w_copies = [
        [
            pltpu.make_async_copy(
                w_ref.at[:, kind * width + low : kind * width + high],
                weights.at[:, kind * width + low : kind * width + high],
                w_sems.at[b, kind],
            )
            for kind in range(3)
        ]
        for b, (low, high) in enumerate(BLOCKS)
    ]
    for copy in input_copies:
        copy.start()
    for copies in w_copies[:AHEAD]:
        for copy in copies:
            copy.start()
    low = lane_iota((1, 2 * HEAD)) < HEAD
    pad = jnp.zeros((2 * half - rows, 2 * HEAD), F32)

    def joined(keys, values, odd):
        if odd:
            return jnp.where(low, swap_halves(keys), values).astype(BF16)
        return jnp.where(low, keys, swap_halves(values)).astype(BF16)

    def store(head, at, block):
        dest = head + head // 3
        for copy in range(2 if head % 3 == 2 else 1):
            send_ref[dest + copy, at] = block

    for copy in input_copies:
        copy.wait()
    normed = layer_norm(tokens[...].astype(F32)) * (1.0 + mod[1:2, :].astype(F32))
    normed = (normed + mod[0:1, :].astype(F32)).astype(BF16)
    flagged = picks[0, 0] == tile_ref[0]
    for slot in range(1, picks.shape[1]):
        flagged = jnp.logical_or(flagged, picks[0, slot] == tile_ref[0])
    above, below = slice(0, half), slice(half, half + rows)

    @pl.when(jnp.logical_not(flagged))
    def _():
        for head in range(width // HEAD):
            first = head // 2 * 2 * HEAD
            k_old = cache[:, first : first + 2 * HEAD].astype(F32)
            v_old = cache[:, width + first : width + first + 2 * HEAD].astype(F32)
            store(head, below, joined(k_old, v_old, head % 2))

    def multiply(b):
        start, end = BLOCKS[b]
        for copy in w_copies[b]:
            copy.wait()
        if b + AHEAD < len(BLOCKS):
            for copy in w_copies[b + AHEAD]:
                copy.start()
        return [
            jnp.dot(
                normed,
                weights[:, kind * width + start : kind * width + end],
                preferred_element_type=F32,
            )
            for kind in range(3)
        ]

    def pack(b, queries, keys, values):
        start, end = BLOCKS[b]
        queries = queries * 0.125
        for pair in range((end - start) // (2 * HEAD)):
            cols = slice(pair * 2 * HEAD, (pair + 1) * 2 * HEAD)
            q_top = queries[:half, cols]
            q_end = jnp.concatenate([queries[half:, cols], pad], axis=0)
            for odd in range(2):
                head = start // HEAD + pair * 2 + odd
                q_pack = joined(q_top, q_end, odd)
                own_ref[head, above] = q_pack
                own_ref[head, below] = joined(keys[:, cols], values[:, cols], odd)
                store(head, above, q_pack)

    made = multiply(0)
    for b in range(1, len(BLOCKS)):
        following = multiply(b)
        pack(b - 1, *made)
        made = following
    pack(len(BLOCKS) - 1, *made)

    @pl.when(flagged)
    def _():
        for head in range(width // HEAD):
            store(head, below, own_ref[head, below])


def project(tile_index, refresh, tokens, modulate, w_qkv, cached):
    rows, width = tokens.shape
    blocks = len(BLOCKS)
    heads = width // HEAD
    dests = heads + heads // 3
    packed = rows + HEAD
    anywhere = pl.BlockSpec(memory_space=pltpu.HBM)
    return pl.pallas_call(
        project_kernel,
        out_shape=(
            jax.ShapeDtypeStruct((dests, packed, 2 * HEAD), BF16),
            jax.ShapeDtypeStruct((heads, packed, 2 * HEAD), BF16),
        ),
        in_specs=[pl.BlockSpec(memory_space=pltpu.SMEM)] + [anywhere] * 5,
        out_specs=(pl.BlockSpec(memory_space=pltpu.VMEM),) * 2,
        scratch_shapes=[
            pltpu.SMEM(refresh.shape, jnp.int32),
            pltpu.VMEM(tokens.shape, BF16),
            pltpu.VMEM(modulate.shape, BF16),
            pltpu.VMEM(w_qkv.shape, BF16),
            pltpu.VMEM(cached.shape, BF16),
            pltpu.SemaphoreType.DMA((4,)),
            pltpu.SemaphoreType.DMA((blocks, 3)),
        ],
        compiler_params=pltpu.CompilerParams(vmem_limit_bytes=60 << 20),
        cost_estimate=pl.CostEstimate(
            flops=6 * rows * width * width,
            bytes_accessed=6 * width * width + (4 << 20),
            transcendentals=0,
        ),
        name="project",
    )(tile_index, refresh, tokens, modulate, w_qkv, cached)


def own_kernel(live_ref, own_ref, tk_ref, tv_ref, out_ref):
    heads, rows, lanes = out_ref.shape
    low = lane_iota((1, lanes)) < HEAD
    live = lane_iota((rows, rows)) < live_ref[0]
    nt = (((1,), (1,)), ((), ()))
    scores = []
    for head in range(heads):
        cols = slice(head // 2 * lanes, (head // 2 + 1) * lanes)
        folded = own_ref[head, :HEAD, :].astype(F32)
        query = jnp.concatenate([folded, swap_halves(folded)[: rows - HEAD]], axis=0)
        query = jnp.where(low, query, 0.0)
        text_query = swap_halves(query) if head % 2 else query
        s_own = lax.dot_general(
            query.astype(BF16), own_ref[head, HEAD:, :], nt, preferred_element_type=F32
        )
        s_text = lax.dot_general(
            text_query.astype(BF16), tk_ref[:, cols], nt, preferred_element_type=F32
        )
        scores.append((jnp.where(live, s_own, -BIG), s_text))
    probs = []
    for s_own, s_text in scores:
        top = jnp.maximum(
            jnp.max(s_own, -1, keepdims=True), jnp.max(s_text, -1, keepdims=True)
        )
        p_own = jnp.exp(s_own - top)
        p_text = jnp.exp(s_text - top)
        total = jnp.sum(p_own, -1, keepdims=True) + jnp.sum(p_text, -1, keepdims=True)
        probs.append((p_own.astype(BF16), p_text.astype(BF16), top, total))
    for head, (p_own, p_text, top, total) in enumerate(probs):
        cols = slice(head // 2 * lanes, (head // 2 + 1) * lanes)
        mixed = jnp.dot(p_own, own_ref[head, HEAD:, :], preferred_element_type=F32)
        from_text = jnp.dot(p_text, tv_ref[:, cols], preferred_element_type=F32)
        if head % 2 == 0:
            from_text = swap_halves(from_text)
        out_ref[head] = jnp.where(low, top + jnp.log(total), (mixed + from_text) / total)


def own_attend(live, own, text_rows):
    heads, packed, lanes = own.shape
    rows = packed - HEAD
    texts = text_rows.shape[0]
    group = 8
    steps = heads // group
    return pl.pallas_call(
        own_kernel,
        grid=(steps,),
        out_shape=jax.ShapeDtypeStruct((heads, rows, lanes), F32),
        in_specs=[
            pl.BlockSpec(memory_space=pltpu.SMEM),
            pl.BlockSpec((group, packed, lanes), lambda p: (p, 0, 0)),
            pl.BlockSpec((texts, group * HEAD), lambda p: (0, p)),
            pl.BlockSpec((texts, group * HEAD), lambda p: (0, p + steps)),
        ],
        out_specs=pl.BlockSpec((group, rows, lanes), lambda p: (p, 0, 0)),
        compiler_params=pltpu.CompilerParams(vmem_limit_bytes=14 << 20),
        cost_estimate=pl.CostEstimate(
            flops=2 * 4 * rows * (rows + texts) * 64 * heads,
            bytes_accessed=6 << 20,
            transcendentals=rows * (rows + texts) * heads,
        ),
        name="own_attend",
    )(live, own, text_rows, text_rows)


def head_kernel(len_ref, pack_ref, out_ref, v_ref, kt_ref, s_ref):
    step = pl.program_id(0)
    tiles, packed, lanes = pack_ref.shape
    rows = packed - HEAD
    total_rows = tiles * rows
    group = out_ref.shape[0]
    block = group * rows
    piece = 256
    chunk = 1920
    low = lane_iota((1, lanes)) < HEAD

    @pl.when(step == 0)
    def _():
        for pair in range(tiles // 2):
            both = jnp.concatenate(
                [pack_ref[2 * pair + t, HEAD:, :].astype(F32) for t in range(2)], axis=0
            )
            v_ref[pair * 2 * rows : (pair + 1) * 2 * rows, :] = both.astype(BF16)
        feature = row_iota((HEAD, piece))
        for c in range(total_rows // piece):
            part = slice(c * piece, (c + 1) * piece)
            kv = v_ref[part, :]
            index = lane_iota((HEAD, piece)) + c * piece
            own = jnp.logical_and(index >= feature * rows, index < feature * rows + rows)
            held = jnp.logical_or(own, jnp.logical_and(feature == tiles, index >= len_ref[0]))
            kt_ref[:HEAD, part] = jnp.transpose(kv.astype(F32))[:HEAD].astype(BF16)
            kt_ref[HEAD:, part] = jnp.where(held, 1.0, 0.0).astype(BF16)
            v_ref[part, :] = jnp.where(low, jnp.ones((), BF16), kv)

    feature = lane_iota((1, lanes)) - HEAD
    parts = []
    for t in range(group):
        tile = step * group + t
        mask = jnp.where(jnp.logical_or(feature == tile, feature == tiles), -BIG, 0.0)
        folded = pack_ref[tile, :HEAD, :].astype(F32)
        parts.append(jnp.where(low, folded, mask))
        parts.append(jnp.where(low, swap_halves(folded)[: rows - HEAD], mask))
    query = jnp.concatenate(parts, axis=0).astype(BF16)
    top = jnp.full((block, 128), -jnp.inf, F32)
    for c in range(total_rows // chunk):
        part = slice(c * chunk, (c + 1) * chunk)
        scores = jnp.dot(query, kt_ref[:, part], preferred_element_type=F32)
        s_ref[:, part] = scores
        for i in range(chunk // 128):
            top = jnp.maximum(top, scores[:, i * 128 : (i + 1) * 128])
    top = jnp.max(top, -1, keepdims=True)
    total = jnp.zeros((block, lanes), F32)
    for c in range(total_rows // chunk):
        part = slice(c * chunk, (c + 1) * chunk)
        probs = jnp.exp(s_ref[:, part] - top).astype(BF16)
        total = total + jnp.dot(probs, v_ref[part, :], preferred_element_type=F32)
    weight = total[:, 0:1]
    lse = jnp.broadcast_to(top + jnp.log(weight), (block, lanes))
    result = total / weight
    diagonal = row_iota((HEAD, lanes)) == lane_iota((HEAD, lanes))
    line = row_iota((8, lanes))
    pad = jnp.zeros((2 * HEAD - rows, lanes), F32)
    for t in range(group):
        first = slice(t * rows, t * rows + HEAD)
        rest = slice(t * rows + HEAD, (t + 1) * rows)
        lse_a = jnp.sum(jnp.where(diagonal, lse[first], 0.0), 0, keepdims=True)
        lse_b = jnp.concatenate([lse[rest], pad], axis=0)
        lse_b = jnp.sum(jnp.where(diagonal, lse_b, 0.0), 0, keepdims=True)
        high_a = lse_a.astype(BF16).astype(F32)
        high_b = lse_b.astype(BF16).astype(F32)
        stats = jnp.where(line == 2, lse_a - high_a, lse_b - high_b)
        stats = jnp.where(line == 0, high_a, jnp.where(line == 1, high_b, stats))
        folded = jnp.concatenate([swap_halves(result[rest]), stats], axis=0)
        out_ref[t] = jnp.where(low, folded, result[first]).astype(BF16)


def head_attend(length, pack):
    tiles, packed, lanes = pack.shape
    rows = packed - HEAD
    total_rows = tiles * rows
    group = 8
    block = group * rows
    return pl.pallas_call(
        head_kernel,
        grid=(tiles // group,),
        out_shape=pltpu.HBM((tiles, HEAD, lanes), BF16),
        in_specs=[
            pl.BlockSpec(memory_space=pltpu.SMEM),
            pl.BlockSpec((tiles, packed, lanes), lambda s: (0, 0, 0)),
        ],
        out_specs=pl.BlockSpec((group, HEAD, lanes), lambda s: (s, 0, 0)),
        scratch_shapes=[
            pltpu.VMEM((total_rows, lanes), BF16),
            pltpu.VMEM((lanes, total_rows), BF16),
            pltpu.VMEM((block, total_rows), F32),
        ],
        compiler_params=pltpu.CompilerParams(vmem_limit_bytes=44 << 20),
        cost_estimate=pl.CostEstimate(
            flops=4 * total_rows * total_rows * 128,
            bytes_accessed=4 << 20,
            transcendentals=total_rows * total_rows,
        ),
        name="head_attend",
    )(length, pack)


def mix_rows(
    second, place_ref, far_ref, own_ref, w_ref, tokens_ref, mod_ref, mixed_ref, input_ref, att_ref, ready
):
    heads, rows, lanes = own_ref.shape
    count, width = mixed_ref.shape
    depth = att_ref.shape[2]
    per = depth // lanes
    here = slice(HEAD, rows) if second else slice(0, HEAD)
    low = lane_iota((1, lanes)) < HEAD
    diagonal = row_iota((count, lanes)) == lane_iota((count, lanes))

    for pair in range(heads // 2):
        both = []
        for odd in range(2):
            head = 2 * pair + odd
            folded = far_ref[head + head // 3].astype(F32)
            stats = folded[rows - HEAD :]
            line = stats[1:2] + stats[3:4] if second else stats[0:1] + stats[2:3]
            spread = jnp.where(diagonal, jnp.broadcast_to(line, (count, lanes)), 0.0)
            far_lse = jnp.sum(spread, -1, keepdims=True)
            far = swap_halves(folded)[:count] if second else folded
            own = own_ref[head, here]
            gap = jnp.broadcast_to(far_lse, (count, lanes)) - own[:, 0:1]
            share = 1.0 / (1.0 + jnp.exp(-gap))
            both.append(share * far + (1.0 - share) * own)
        joined = jnp.where(low, swap_halves(both[0]), both[1])
        at = (pair % per) * lanes
        att_ref[pair // per, :, at : at + lanes] = joined.astype(BF16)
    ready()
    place = place_ref[0]
    projected = jnp.zeros((count, width), F32)
    owners = (place, place + 1 - 2 * (place % 2), (place + 2) % 4, 3 - place)
    for i, owner in enumerate(owners):
        part = w_ref[i * depth : (i + 1) * depth]
        projected += jnp.dot(att_ref[owner], part, preferred_element_type=F32)
    mod = mod_ref[...].astype(F32)
    mixed = tokens_ref[here].astype(F32) + mod[2:3] * projected
    mixed_ref[...] = mixed
    input_ref[...] = (layer_norm(mixed) * (1.0 + mod[4:5]) + mod[3:4]).astype(BF16)


def mix_a_kernel(
    place, far, own, w0, w1, w2, w3, tokens, mod, mixed, out, w_ref, att, sems
):
    copies = []
    first = 0
    for i, part in enumerate((w0, w1, w2, w3)):
        last = first + part.shape[0]
        copies.append(pltpu.make_async_copy(part, w_ref.at[first:last], sems.at[i]))
        first = last
    for copy in copies:
        copy.start()

    def ready():
        for copy in copies:
            copy.wait()

    mix_rows(False, place, far, own, w_ref, tokens, mod, mixed, out, att, ready)


def mix_b_kernel(place, far, own, w_ref, tokens, mod, mixed, out, att):
    mix_rows(True, place, far, own, w_ref, tokens, mod, mixed, out, att, lambda: None)


def mix(second, place, far, own, weights, tokens, modulate):
    rows, width = tokens.shape
    count = rows - HEAD if second else HEAD
    owners = 4
    local = pl.BlockSpec(memory_space=pltpu.VMEM)
    outs = [
        jax.ShapeDtypeStruct((count, width), F32),
        jax.ShapeDtypeStruct((count, width), BF16),
    ]
    scratch = [pltpu.VMEM((owners, count, width // owners), BF16)]
    if not second:
        outs.append(pltpu.VMEM((width, width), BF16))
        scratch.append(pltpu.SemaphoreType.DMA((owners,)))
    weight_spec = local if second else pl.BlockSpec(memory_space=pl.ANY)
    return pl.pallas_call(
        mix_b_kernel if second else mix_a_kernel,
        out_shape=tuple(outs),
        in_specs=[pl.BlockSpec(memory_space=pltpu.SMEM), local, local]
        + [weight_spec] * len(weights)
        + [local, local],
        out_specs=(local,) * len(outs),
        scratch_shapes=scratch,
        compiler_params=pltpu.CompilerParams(vmem_limit_bytes=20 << 20),
        name="mix_b" if second else "mix_a",
    )(place, far, own, *weights, tokens, modulate)


def feed_kernel(count, *refs):
    pieces, (up_ref, down_ref), outs = refs[:count], refs[count : count + 2], refs[count + 2 :]
    both = jnp.concatenate([piece[...].astype(F32) for piece in pieces], axis=0).astype(BF16)
    wide = 512
    total = None
    for c in range(up_ref.shape[1] // wide):
        part = slice(c * wide, (c + 1) * wide)
        hidden = jnp.dot(both, up_ref[:, part], preferred_element_type=F32)
        hidden = jax.nn.gelu(hidden, approximate=True).astype(BF16)
        product = jnp.dot(hidden, down_ref[part, :], preferred_element_type=F32)
        total = product if total is None else total + product
    first = 0
    for out in outs:
        last = first + out.shape[0]
        out[...] = total[first:last].astype(out.dtype)
        first = last


def feed(name, pieces, w_up, w_down):
    count = len(pieces)
    kinds = [F32] * (count // 2) + [BF16] * (count // 2)
    local = pl.BlockSpec(memory_space=pltpu.VMEM)
    return pl.pallas_call(
        functools.partial(feed_kernel, count),
        out_shape=tuple(jax.ShapeDtypeStruct(p.shape, k) for p, k in zip(pieces, kinds)),
        in_specs=[local] * (count + 2),
        out_specs=(local,) * count,
        compiler_params=pltpu.CompilerParams(vmem_limit_bytes=20 << 20),
        name=name,
    )(*pieces, w_up, w_down)


def final_kernel(
    live_ref, mod_ref, mix_a, mix_b, near_a, near_b, core_a, core_b, far_a, far_b, out_ref
):
    gate = mod_ref[...].astype(F32)[5:6]
    first = 0
    for mixed, near, core, far in (
        (mix_a, near_a, core_a, far_a),
        (mix_b, near_b, core_b, far_b),
    ):
        total = near[...] + core[...].astype(F32) + far[...].astype(F32)
        result = mixed[...] + gate * total
        position = row_iota(result.shape) + first
        last = first + mixed.shape[0]
        out_ref[first:last] = jnp.where(position < live_ref[0], result, 0.0).astype(BF16)
        first = last


def final(live, modulate, *pieces):
    rows = sum(piece.shape[0] for piece in pieces[:2])
    local = pl.BlockSpec(memory_space=pltpu.VMEM)
    return pl.pallas_call(
        final_kernel,
        out_shape=jax.ShapeDtypeStruct((rows, modulate.shape[1]), BF16),
        in_specs=[pl.BlockSpec(memory_space=pltpu.SMEM)] + [local] * 9,
        out_specs=local,
        compiler_params=pltpu.CompilerParams(vmem_limit_bytes=16 << 20),
        name="final",
    )(live, modulate, *pieces)


def swap(values, axis):
    return lax.ppermute(values, axis, [(0, 1), (1, 0)])


def per_device(
    latents, modulation, kv_cache, text_kv, lengths, refresh, w_qkv, w_out, w_up, w_down
):
    tokens = latents[0]
    rows = tokens.shape[0]
    tile_index = lax.axis_index(TILE).astype(jnp.int32)
    length = lengths[0]
    place = lax.axis_index(REQ).astype(jnp.int32).reshape(1)
    send, own = project(
        tile_index.reshape(1), refresh, tokens, modulation[0], w_qkv, kv_cache[0]
    )
    send, own, w_here = lax.optimization_barrier((send, own, w_out))
    pack = lax.all_to_all(send, TILE, split_axis=0, concat_axis=0, tiled=True)
    w2 = swap(w_here, "zh")
    w1 = swap(w_here, "co")
    live = (length - tile_index * rows).reshape(1)
    own_part = own_attend(live, own, text_kv[0])
    pack, own_part = lax.optimization_barrier((pack, own_part))
    far = head_attend(lengths, pack)
    far, w1, w2 = lax.optimization_barrier((far, w1, w2))
    w3 = swap(w2, "co")
    far = lax.all_to_all(far, TILE, split_axis=0, concat_axis=0, tiled=True)
    far, w3 = lax.optimization_barrier((far, w3))

    w_parts = (w_out, w1, w2, w3)
    mixed_a, input_a, w_main = mix(False, place, far, own_part, w_parts, tokens, modulation[0])
    z_a, core_a = swap(input_a, "zh"), swap(input_a, "co")
    mixed_b, input_b = mix(True, place, far, own_part, (w_main,), tokens, modulation[0])
    z_b, core_b = swap(input_b, "zh"), swap(input_b, "co")
    near = feed("feed_near", (input_a, input_b, core_a, core_b), w_up, w_down)
    z_a, z_b, near = lax.optimization_barrier((z_a, z_b, near))
    far_a = feed("feed_a", (z_a, swap(z_a, "co")), w_up, w_down)
    sum_a = (far_a[0] + swap(far_a[1], "co").astype(F32)).astype(BF16)
    z_b, sum_a = lax.optimization_barrier((z_b, sum_a))
    back_a = swap(sum_a, "zh")
    far_b = feed("feed_b", (z_b, swap(z_b, "co")), w_up, w_down)
    sum_b = (far_b[0] + swap(far_b[1], "co").astype(F32)).astype(BF16)
    back_b = swap(sum_b, "zh")
    near_a, near_b = swap(near[2], "co"), swap(near[3], "co")
    pieces = (mixed_a, mixed_b, near[0], near[1], near_a, near_b, back_a, back_b)
    return final(live, modulation[0], *pieces)[None]


def solution(mesh):
    fine = Mesh(mesh.devices.reshape(2, 2, 4, 2, 4), REQ + TILE)
    return jax.shard_map(
        per_device,
        mesh=fine,
        in_specs=(
            P(REQ, TILE, None),
            P(REQ, None, None),
            P(REQ, TILE, None),
            P(REQ, None, None),
            P(REQ),
            P(REQ, None),
            P(),
            P(REQ, None),
            P(None, REQ),
            P(REQ, None),
        ),
        out_specs=P(REQ, TILE, None),
        check_vma=False,
    )
```

```python
import jax
import jax.numpy as jnp
from jax import lax
from jax.experimental import pallas as pl
from jax.experimental.pallas import tpu as pltpu
from jax.sharding import Mesh
from jax.sharding import PartitionSpec as P

REQ = ("zh", "co")
TILE = ("y", "zl", "x")
HEAD = 64
BIG = 1e30
BLOCKS = ((0, 512), (512, 1024), (1024, 1536))
AHEAD = 2
F32 = jnp.float32
BF16 = jnp.bfloat16


def layer_norm(values):
    average = jnp.mean(values, -1, keepdims=True)
    centred = values - average
    spread = jnp.mean(centred * centred, -1, keepdims=True)
    return centred * lax.rsqrt(spread + 1e-06)


def lane_iota(shape):
    return lax.broadcasted_iota(jnp.int32, shape, len(shape) - 1)


def row_iota(shape):
    return lax.broadcasted_iota(jnp.int32, shape, len(shape) - 2)


def swap_halves(values):
    return pltpu.roll(values, HEAD, axis=1)


def project_kernel(
    tile_ref,
    refresh_ref,
    tokens_ref,
    mod_ref,
    w_ref,
    cache_ref,
    send_ref,
    own_ref,
    picks,
    tokens,
    mod,
    weights,
    cache,
    sent,
    kept,
    in_sems,
    w_sems,
    out_sems,
):
    rows, width = tokens.shape
    half = HEAD
    inputs = (
        (tokens_ref, tokens),
        (mod_ref, mod),
        (refresh_ref, picks),
        (cache_ref, cache),
    )
    input_copies = [
        pltpu.make_async_copy(src, dst, in_sems.at[i]) for i, (src, dst) in enumerate(inputs)
    ]
    w_copies = [
        [
            pltpu.make_async_copy(
                w_ref.at[:, kind * width + low : kind * width + high],
                weights.at[:, kind * width + low : kind * width + high],
                w_sems.at[b, kind],
            )
            for kind in range(3)
        ]
        for b, (low, high) in enumerate(BLOCKS)
    ]
    for copy in input_copies:
        copy.start()
    for copies in w_copies[:AHEAD]:
        for copy in copies:
            copy.start()
    low = lane_iota((1, 2 * HEAD)) < HEAD
    pad = jnp.zeros((2 * half - rows, 2 * HEAD), F32)

    def joined(keys, values, odd):
        if odd:
            return jnp.where(low, swap_halves(keys), values).astype(BF16)
        return jnp.where(low, keys, swap_halves(values)).astype(BF16)

    def store(head, at, block):
        dest = head + head // 3
        for copy in range(2 if head % 3 == 2 else 1):
            sent[dest + copy, at] = block

    for copy in input_copies:
        copy.wait()
    normed = layer_norm(tokens[...].astype(F32)) * (1.0 + mod[1:2, :].astype(F32))
    normed = (normed + mod[0:1, :].astype(F32)).astype(BF16)
    flagged = picks[0, 0] == tile_ref[0]
    for slot in range(1, picks.shape[1]):
        flagged = jnp.logical_or(flagged, picks[0, slot] == tile_ref[0])
    above, below = slice(0, half), slice(half, half + rows)

    @pl.when(jnp.logical_not(flagged))
    def _():
        for head in range(width // HEAD):
            first = head // 2 * 2 * HEAD
            k_old = cache[:, first : first + 2 * HEAD].astype(F32)
            v_old = cache[:, width + first : width + first + 2 * HEAD].astype(F32)
            store(head, below, joined(k_old, v_old, head % 2))

    def multiply(b):
        start, end = BLOCKS[b]
        for copy in w_copies[b]:
            copy.wait()
        if b + AHEAD < len(BLOCKS):
            for copy in w_copies[b + AHEAD]:
                copy.start()
        return [
            jnp.dot(
                normed,
                weights[:, kind * width + start : kind * width + end],
                preferred_element_type=F32,
            )
            for kind in range(3)
        ]

    def pack(b, queries, keys, values):
        start, end = BLOCKS[b]
        queries = queries * 0.125
        for pair in range((end - start) // (2 * HEAD)):
            cols = slice(pair * 2 * HEAD, (pair + 1) * 2 * HEAD)
            q_top = queries[:half, cols]
            q_end = jnp.concatenate([queries[half:, cols], pad], axis=0)
            for odd in range(2):
                head = start // HEAD + pair * 2 + odd
                q_pack = joined(q_top, q_end, odd)
                kept[head, above] = q_pack
                kept[head, below] = joined(keys[:, cols], values[:, cols], odd)
                store(head, above, q_pack)

    out_copies = []

    def hand_out(b):
        head, last = (edge // HEAD for edge in BLOCKS[b])

        @pl.when(flagged)
        def _():
            for h in range(head, last):
                store(h, below, kept[h, below])

        dest, dest_last = head + head // 3, last + last // 3
        for i, (src, dst, part) in enumerate(
            ((sent, send_ref, slice(dest, dest_last)), (kept, own_ref, slice(head, last)))
        ):
            out_copies.append(
                pltpu.make_async_copy(src.at[part], dst.at[part], out_sems.at[b, i])
            )
            out_copies[-1].start()

    made = multiply(0)
    for b in range(1, len(BLOCKS)):
        following = multiply(b)
        pack(b - 1, *made)
        hand_out(b - 1)
        made = following
    pack(len(BLOCKS) - 1, *made)
    hand_out(len(BLOCKS) - 1)
    for copy in out_copies:
        copy.wait()


def project(tile_index, refresh, tokens, modulate, w_qkv, cached):
    rows, width = tokens.shape
    blocks = len(BLOCKS)
    heads = width // HEAD
    dests = heads + heads // 3
    packed = rows + HEAD
    anywhere = pl.BlockSpec(memory_space=pltpu.HBM)
    return pl.pallas_call(
        project_kernel,
        out_shape=(
            pltpu.HBM((dests, packed, 2 * HEAD), BF16),
            pltpu.HBM((heads, packed, 2 * HEAD), BF16),
        ),
        in_specs=[pl.BlockSpec(memory_space=pltpu.SMEM)] + [anywhere] * 5,
        out_specs=(anywhere, anywhere),
        scratch_shapes=[
            pltpu.SMEM(refresh.shape, jnp.int32),
            pltpu.VMEM(tokens.shape, BF16),
            pltpu.VMEM(modulate.shape, BF16),
            pltpu.VMEM(w_qkv.shape, BF16),
            pltpu.VMEM(cached.shape, BF16),
            pltpu.VMEM((dests, packed, 2 * HEAD), BF16),
            pltpu.VMEM((heads, packed, 2 * HEAD), BF16),
            pltpu.SemaphoreType.DMA((4,)),
            pltpu.SemaphoreType.DMA((blocks, 3)),
            pltpu.SemaphoreType.DMA((blocks, 2)),
        ],
        compiler_params=pltpu.CompilerParams(vmem_limit_bytes=60 << 20),
        cost_estimate=pl.CostEstimate(
            flops=6 * rows * width * width,
            bytes_accessed=6 * width * width + (4 << 20),
            transcendentals=0,
        ),
        name="project",
    )(tile_index, refresh, tokens, modulate, w_qkv, cached)


def own_kernel(live_ref, own_ref, tk_ref, tv_ref, out_ref):
    heads, rows, lanes = out_ref.shape
    low = lane_iota((1, lanes)) < HEAD
    live = lane_iota((rows, rows)) < live_ref[0]
    nt = (((1,), (1,)), ((), ()))
    scores = []
    for head in range(heads):
        cols = slice(head // 2 * lanes, (head // 2 + 1) * lanes)
        folded = own_ref[head, :HEAD, :].astype(F32)
        query = jnp.concatenate([folded, swap_halves(folded)[: rows - HEAD]], axis=0)
        query = jnp.where(low, query, 0.0)
        text_query = swap_halves(query) if head % 2 else query
        s_own = lax.dot_general(
            query.astype(BF16), own_ref[head, HEAD:, :], nt, preferred_element_type=F32
        )
        s_text = lax.dot_general(
            text_query.astype(BF16), tk_ref[:, cols], nt, preferred_element_type=F32
        )
        scores.append((jnp.where(live, s_own, -BIG), s_text))
    probs = []
    for s_own, s_text in scores:
        top = jnp.maximum(
            jnp.max(s_own, -1, keepdims=True), jnp.max(s_text, -1, keepdims=True)
        )
        p_own = jnp.exp(s_own - top)
        p_text = jnp.exp(s_text - top)
        total = jnp.sum(p_own, -1, keepdims=True) + jnp.sum(p_text, -1, keepdims=True)
        probs.append((p_own.astype(BF16), p_text.astype(BF16), top, total))
    for head, (p_own, p_text, top, total) in enumerate(probs):
        cols = slice(head // 2 * lanes, (head // 2 + 1) * lanes)
        mixed = jnp.dot(p_own, own_ref[head, HEAD:, :], preferred_element_type=F32)
        from_text = jnp.dot(p_text, tv_ref[:, cols], preferred_element_type=F32)
        if head % 2 == 0:
            from_text = swap_halves(from_text)
        out_ref[head] = jnp.where(low, top + jnp.log(total), (mixed + from_text) / total)


def own_attend(live, own, text_rows):
    heads, packed, lanes = own.shape
    rows = packed - HEAD
    texts = text_rows.shape[0]
    group = 8
    steps = heads // group
    return pl.pallas_call(
        own_kernel,
        grid=(steps,),
        out_shape=jax.ShapeDtypeStruct((heads, rows, lanes), F32),
        in_specs=[
            pl.BlockSpec(memory_space=pltpu.SMEM),
            pl.BlockSpec((group, packed, lanes), lambda p: (p, 0, 0)),
            pl.BlockSpec((texts, group * HEAD), lambda p: (0, p)),
            pl.BlockSpec((texts, group * HEAD), lambda p: (0, p + steps)),
        ],
        out_specs=pl.BlockSpec((group, rows, lanes), lambda p: (p, 0, 0)),
        compiler_params=pltpu.CompilerParams(vmem_limit_bytes=14 << 20),
        cost_estimate=pl.CostEstimate(
            flops=2 * 4 * rows * (rows + texts) * 64 * heads,
            bytes_accessed=6 << 20,
            transcendentals=rows * (rows + texts) * heads,
        ),
        name="own_attend",
    )(live, own, text_rows, text_rows)


def head_kernel(len_ref, pack_ref, out_ref, v_ref, kt_ref, s_ref):
    step = pl.program_id(0)
    tiles, packed, lanes = pack_ref.shape
    rows = packed - HEAD
    total_rows = tiles * rows
    group = out_ref.shape[0]
    block = group * rows
    piece = 256
    chunk = 1920
    low = lane_iota((1, lanes)) < HEAD

    @pl.when(step == 0)
    def _():
        for pair in range(tiles // 2):
            both = jnp.concatenate(
                [pack_ref[2 * pair + t, HEAD:, :].astype(F32) for t in range(2)], axis=0
            )
            v_ref[pair * 2 * rows : (pair + 1) * 2 * rows, :] = both.astype(BF16)
        feature = row_iota((HEAD, piece))
        for c in range(total_rows // piece):
            part = slice(c * piece, (c + 1) * piece)
            kv = v_ref[part, :]
            index = lane_iota((HEAD, piece)) + c * piece
            own = jnp.logical_and(index >= feature * rows, index < feature * rows + rows)
            held = jnp.logical_or(own, jnp.logical_and(feature == tiles, index >= len_ref[0]))
            kt_ref[:HEAD, part] = jnp.transpose(kv.astype(F32))[:HEAD].astype(BF16)
            kt_ref[HEAD:, part] = jnp.where(held, 1.0, 0.0).astype(BF16)
            v_ref[part, :] = jnp.where(low, jnp.ones((), BF16), kv)

    feature = lane_iota((1, lanes)) - HEAD
    parts = []
    for t in range(group):
        tile = step * group + t
        mask = jnp.where(jnp.logical_or(feature == tile, feature == tiles), -BIG, 0.0)
        folded = pack_ref[tile, :HEAD, :].astype(F32)
        parts.append(jnp.where(low, folded, mask))
        parts.append(jnp.where(low, swap_halves(folded)[: rows - HEAD], mask))
    query = jnp.concatenate(parts, axis=0).astype(BF16)
    top = jnp.full((block, 128), -jnp.inf, F32)
    for c in range(total_rows // chunk):
        part = slice(c * chunk, (c + 1) * chunk)
        scores = jnp.dot(query, kt_ref[:, part], preferred_element_type=F32)
        s_ref[:, part] = scores
        for i in range(chunk // 128):
            top = jnp.maximum(top, scores[:, i * 128 : (i + 1) * 128])
    top = jnp.max(top, -1, keepdims=True)
    total = jnp.zeros((block, lanes), F32)
    for c in range(total_rows // chunk):
        part = slice(c * chunk, (c + 1) * chunk)
        probs = jnp.exp(s_ref[:, part] - top).astype(BF16)
        total = total + jnp.dot(probs, v_ref[part, :], preferred_element_type=F32)
    weight = total[:, 0:1]
    lse = jnp.broadcast_to(top + jnp.log(weight), (block, lanes))
    result = total / weight
    diagonal = row_iota((HEAD, lanes)) == lane_iota((HEAD, lanes))
    line = row_iota((8, lanes))
    pad = jnp.zeros((2 * HEAD - rows, lanes), F32)
    for t in range(group):
        first = slice(t * rows, t * rows + HEAD)
        rest = slice(t * rows + HEAD, (t + 1) * rows)
        lse_a = jnp.sum(jnp.where(diagonal, lse[first], 0.0), 0, keepdims=True)
        lse_b = jnp.concatenate([lse[rest], pad], axis=0)
        lse_b = jnp.sum(jnp.where(diagonal, lse_b, 0.0), 0, keepdims=True)
        high_a = lse_a.astype(BF16).astype(F32)
        high_b = lse_b.astype(BF16).astype(F32)
        stats = jnp.where(line == 2, lse_a - high_a, lse_b - high_b)
        stats = jnp.where(line == 0, high_a, jnp.where(line == 1, high_b, stats))
        folded = jnp.concatenate([swap_halves(result[rest]), stats], axis=0)
        out_ref[t] = jnp.where(low, folded, result[first]).astype(BF16)


def head_attend(length, pack):
    tiles, packed, lanes = pack.shape
    rows = packed - HEAD
    total_rows = tiles * rows
    group = 8
    block = group * rows
    return pl.pallas_call(
        head_kernel,
        grid=(tiles // group,),
        out_shape=pltpu.HBM((tiles, HEAD, lanes), BF16),
        in_specs=[
            pl.BlockSpec(memory_space=pltpu.SMEM),
            pl.BlockSpec((tiles, packed, lanes), lambda s: (0, 0, 0)),
        ],
        out_specs=pl.BlockSpec((group, HEAD, lanes), lambda s: (s, 0, 0)),
        scratch_shapes=[
            pltpu.VMEM((total_rows, lanes), BF16),
            pltpu.VMEM((lanes, total_rows), BF16),
            pltpu.VMEM((block, total_rows), F32),
        ],
        compiler_params=pltpu.CompilerParams(vmem_limit_bytes=44 << 20),
        cost_estimate=pl.CostEstimate(
            flops=4 * total_rows * total_rows * 128,
            bytes_accessed=4 << 20,
            transcendentals=total_rows * total_rows,
        ),
        name="head_attend",
    )(length, pack)


def join_kernel(far_ref, own_ref, w0, w1, w2a, w2b, w3a, w3b, att_ref, w_ref, sems):
    heads, rows, lanes = own_ref.shape
    depth = att_ref.shape[2]
    copies = []
    first = 0
    for i, part in enumerate((w0, w1, w2a, w2b, w3a, w3b)):
        last = first + part.shape[0]
        copies.append(pltpu.make_async_copy(part, w_ref.at[first:last], sems.at[i]))
        first = last
    for copy in copies:
        copy.start()
    per = depth // lanes
    low = lane_iota((1, lanes)) < HEAD
    diagonal = row_iota((HEAD, lanes)) == lane_iota((HEAD, lanes))

    def column(line):
        spread = jnp.where(diagonal, jnp.broadcast_to(line, (HEAD, lanes)), 0.0)
        return jnp.sum(spread, -1, keepdims=True)

    for pair in range(heads // 2):
        both = []
        for odd in range(2):
            head = 2 * pair + odd
            folded = far_ref[head + head // 3].astype(F32)
            stats = folded[rows - HEAD :]
            begin = column(stats[0:1] + stats[2:3])
            rest = column(stats[1:2] + stats[3:4])
            far_lse = jnp.concatenate([begin, rest[: rows - HEAD]], axis=0)
            far = jnp.concatenate([folded, swap_halves(folded)[: rows - HEAD]], axis=0)
            own = own_ref[head]
            gap = jnp.broadcast_to(far_lse, (rows, lanes)) - own[:, 0:1]
            share = 1.0 / (1.0 + jnp.exp(-gap))
            both.append(share * far + (1.0 - share) * own)
        joined = jnp.where(low, swap_halves(both[0]), both[1])
        at = (pair % per) * lanes
        att_ref[pair // per, :, at : at + lanes] = joined.astype(BF16)
    for copy in copies:
        copy.wait()


def join(far, own, w_parts):
    heads, rows, _ = own.shape
    depth, width = w_parts[0].shape
    fetched = sum(part.shape[0] for part in w_parts)
    local = pl.BlockSpec(memory_space=pltpu.VMEM)
    anywhere = pl.BlockSpec(memory_space=pl.ANY)
    fixed = pl.BlockSpec(memory_space=pltpu.HBM)
    return pl.pallas_call(
        join_kernel,
        out_shape=(
            jax.ShapeDtypeStruct((width // depth, rows, depth), BF16),
            pltpu.VMEM((fetched, width), BF16),
        ),
        in_specs=[local, local, fixed, anywhere, fixed] + [anywhere] * 3,
        out_specs=(local, local),
        scratch_shapes=[pltpu.SemaphoreType.DMA((6,))],
        compiler_params=pltpu.CompilerParams(vmem_limit_bytes=24 << 20),
        cost_estimate=pl.CostEstimate(
            flops=64 * heads * rows * 128, bytes_accessed=8 << 20, transcendentals=heads * rows * 256
        ),
        name="join",
    )(far, own, *w_parts)


def mix_kernel(place_ref, att_ref, w_ref, tokens_ref, mod_ref, mixed_ref, input_ref):
    place = place_ref[0]
    depth = att_ref.shape[2]
    projected = jnp.zeros(mixed_ref.shape, F32)
    owners = (place, place + 1 - 2 * (place % 2), (place + 2) % 4, 3 - place)
    for i, owner in enumerate(owners):
        part = w_ref[i * depth : (i + 1) * depth]
        projected += jnp.dot(att_ref[owner], part, preferred_element_type=F32)
    mod = mod_ref[...].astype(F32)
    mixed = tokens_ref[...].astype(F32) + mod[2:3] * projected
    mixed_ref[...] = mixed
    input_ref[...] = (layer_norm(mixed) * (1.0 + mod[4:5]) + mod[3:4]).astype(BF16)


def mix(place, attended, w_main, tokens, modulate):
    local = pl.BlockSpec(memory_space=pltpu.VMEM)
    return pl.pallas_call(
        mix_kernel,
        out_shape=(
            jax.ShapeDtypeStruct(tokens.shape, F32),
            jax.ShapeDtypeStruct(tokens.shape, BF16),
        ),
        in_specs=[pl.BlockSpec(memory_space=pltpu.SMEM)] + [local] * 4,
        out_specs=(local, local),
        compiler_params=pltpu.CompilerParams(vmem_limit_bytes=24 << 20),
        name="mix",
    )(place, attended, w_main, tokens, modulate)


def feed_blocks(first_ref, second_ref, keep_ref, pass_ref, up_ref, down_ref, ready):
    rows = first_ref.shape[0]
    hidden_width = up_ref.shape[1]
    wide = 512
    both = [first_ref[...].astype(F32), second_ref[...].astype(F32)]
    both = jnp.concatenate(both, axis=0).astype(BF16)
    total = None
    for c in range(hidden_width // wide):
        part = slice(c * wide, (c + 1) * wide)
        ready(2 * c)
        hidden = jnp.dot(both, up_ref[:, part], preferred_element_type=F32)
        hidden = jax.nn.gelu(hidden, approximate=True).astype(BF16)
        ready(2 * c + 1)
        product = jnp.dot(hidden, down_ref[part, :], preferred_element_type=F32)
        total = product if total is None else total + product
    keep_ref[...] = total[:rows]
    pass_ref[...] = total[rows:].astype(BF16)


def feed_near_kernel(first, second, up_hbm, down_hbm, keep, passed, up, down, sems):
    wide = 512
    copies = []
    for c in range(up.shape[1] // wide):
        part = slice(c * wide, (c + 1) * wide)
        copies.append(
            pltpu.make_async_copy(up_hbm.at[:, part], up.at[:, part], sems.at[2 * c])
        )
        copies.append(
            pltpu.make_async_copy(down_hbm.at[part], down.at[part], sems.at[2 * c + 1])
        )
    for copy in copies:
        copy.start()
    feed_blocks(first, second, keep, passed, up, down, lambda i: copies[i].wait())


def feed_far_kernel(first, second, up, down, keep, passed):
    feed_blocks(first, second, keep, passed, up, down, lambda i: None)


def feed_near(first, second, w_up, w_down):
    rows, width = first.shape
    local = pl.BlockSpec(memory_space=pltpu.VMEM)
    anywhere = pl.BlockSpec(memory_space=pltpu.HBM)
    return pl.pallas_call(
        feed_near_kernel,
        out_shape=(
            jax.ShapeDtypeStruct((rows, width), F32),
            jax.ShapeDtypeStruct((rows, width), BF16),
            pltpu.VMEM(w_up.shape, BF16),
            pltpu.VMEM(w_down.shape, BF16),
        ),
        in_specs=[local, local, anywhere, anywhere],
        out_specs=(local,) * 4,
        scratch_shapes=[pltpu.SemaphoreType.DMA((2 * (w_up.shape[1] // 512),))],
        compiler_params=pltpu.CompilerParams(vmem_limit_bytes=32 << 20),
        cost_estimate=pl.CostEstimate(
            flops=8 * rows * w_up.size, bytes_accessed=4 * w_up.size, transcendentals=0
        ),
        name="feed_near",
    )(first, second, w_up, w_down)


def feed_far(first, second, w_up, w_down):
    rows, width = first.shape
    local = pl.BlockSpec(memory_space=pltpu.VMEM)
    return pl.pallas_call(
        feed_far_kernel,
        out_shape=(
            jax.ShapeDtypeStruct((rows, width), F32),
            jax.ShapeDtypeStruct((rows, width), BF16),
        ),
        in_specs=[local] * 4,
        out_specs=(local,) * 2,
        compiler_params=pltpu.CompilerParams(vmem_limit_bytes=24 << 20),
        cost_estimate=pl.CostEstimate(
            flops=8 * rows * w_up.size, bytes_accessed=1 << 20, transcendentals=0
        ),
        name="feed_far",
    )(first, second, w_up, w_down)


def swap(values, axis):
    return lax.ppermute(values, axis, [(0, 1), (1, 0)])


def per_device(
    latents, modulation, kv_cache, text_kv, lengths, refresh, w_qkv, w_out, w_up, w_down
):
    tokens = latents[0]
    rows = tokens.shape[0]
    tile_index = lax.axis_index(TILE).astype(jnp.int32)
    length = lengths[0]
    place = lax.axis_index(REQ).astype(jnp.int32).reshape(1)
    w2_first = swap(w_out[: w_out.shape[0] // 4], "zh")
    send, own = project(
        tile_index.reshape(1), refresh, tokens, modulation[0], w_qkv, kv_cache[0]
    )
    send, own, w2_first = lax.optimization_barrier((send, own, w2_first))
    pack = lax.all_to_all(send, TILE, split_axis=0, concat_axis=0, tiled=True)
    live = (length - tile_index * rows).reshape(1)
    own_part = own_attend(live, own, text_kv[0])
    own_part, w_here = lax.optimization_barrier((own_part, w_out))
    early = w_out.shape[0] // 4
    w1 = swap(w_here, "co")
    w2 = swap(w_here[early:], "zh")
    pack, own_part = lax.optimization_barrier((pack, own_part))
    far = head_attend(lengths, pack)
    far, w1, w2 = lax.optimization_barrier((far, w1, w2))
    w3 = swap(w2, "co")
    w3_first = swap(w2_first, "co")
    far = lax.all_to_all(far, TILE, split_axis=0, concat_axis=0, tiled=True)
    far, w3, w3_first = lax.optimization_barrier((far, w3, w3_first))
    attended, w_main = join(far, own_part, (w_out, w1, w2_first, w2, w3_first, w3))
    mixed, mlp_input = mix(place, attended, w_main, tokens, modulation[0])

    far_z = swap(mlp_input, "zh")
    near = swap(mlp_input, "co")
    near_keep, near_pass, up, down = feed_near(mlp_input, near, w_up, w_down)
    far_z, near_keep, near_pass = lax.optimization_barrier((far_z, near_keep, near_pass))
    far_both = swap(far_z, "co")
    far_keep, far_pass = feed_far(far_z, far_both, up, down)
    sum_far = (far_keep + swap(far_pass, "co").astype(F32)).astype(BF16)
    near_sum = near_keep + swap(near_pass, "co").astype(F32)
    mlp_out = near_sum + swap(sum_far, "zh").astype(F32)
    positions = tile_index * rows + jnp.arange(rows, dtype=jnp.int32)
    live_rows = positions < length
    gate = modulation[0, 5].astype(F32)
    finished = jnp.where(live_rows[:, None], mixed + gate * mlp_out, 0.0)
    return finished.astype(BF16)[None]


def solution(mesh):
    fine = Mesh(mesh.devices.reshape(2, 2, 4, 2, 4), REQ + TILE)
    return jax.shard_map(
        per_device,
        mesh=fine,
        in_specs=(
            P(REQ, TILE, None),
            P(REQ, None, None),
            P(REQ, TILE, None),
            P(REQ, None, None),
            P(REQ),
            P(REQ, None),
            P(),
            P(REQ, None),
            P(None, REQ),
            P(REQ, None),
        ),
        out_specs=P(REQ, TILE, None),
        check_vma=False,
    )
```
